32 devices in a mesh: row: 8 (over z, x), col: 4 (over y, core).
Axes of the slice: x: 2, y: 2, z: 4, core: 2. Of those that a mesh axis runs over, the one named last changes fastest.
Arguments:
- geneo_vectors: bfloat16 [32, 32, 512, 512], P(None, None, 'row', 'col'), as said below
- phase_labels: int32 [32, 512, 512], P(None, 'row', 'col'), may hold values from 0 to 3, as said below
- phase_mobility: float32 [4], replicated, may hold values from 0.5 to 5
Outputs:
- coarse_factor: float32 [32, 4, 4, 2, 2, 8, 2, 32], P(None, None, 'col', None, None, 'row')
The draws below stay inside these ranges and needn't reach their ends.
Inputs may be any that keep to these rules, and one draw needn't show every extreme that they name: `geneo_vectors`: the 32 vectors of each subdomain are linearly independent on its cells. `phase_labels`: within one subdomain the labels take one or two values, some q and (q + 1) modulo 4.
All inputs are finite; a program needn't handle non-finite values.
Results may differ from the reference program's by a relative error of at most 0.00055.
Values may be sent and summed in bfloat16 or wider, within the bound.
A program may use at most 512 MiB of HBM per device.

```python
import math
import jax
import jax.numpy as jnp
from jax import lax

K = 32
NB = 2
PHASES = 4
CX = 64
CY = 128
CZ = 32
NX = 512
NY = 512
NSUB = 32
ORDER = 1024
KTR = 2
KTC = 4
WIDTH = 64
N_ROW = 8
N_COL = 4


def smooth_line(key, count, length):
    key_amp, key_wave, key_shift = jax.random.split(key, 3)
    amplitude = jnp.clip(jax.random.normal(key_amp, (count, 4, 1), jnp.float32), -3.0, 3.0) * 0.7071
    wavenumber = jax.random.uniform(key_wave, (count, 4, 1), jnp.float32, 0.0, 0.6)
    offset = jax.random.uniform(key_shift, (count, 4, 1), jnp.float32, -3.1416, 3.1416)
    coords = jnp.arange(length, dtype=jnp.float32)[None, None, :]
    values = amplitude * jnp.cos(wavenumber * coords + offset)
    return values[:, 0] + values[:, 1] + values[:, 2] + values[:, 3]


def draw_geneo_vectors(key, part):
    key_line, key_own, key_mix, key_noise = jax.random.split(key, 4)
    terms = 3
    line_x = smooth_line(jax.random.fold_in(key_line, 0), K * terms, NX).reshape(K, terms, NX)
    line_y = smooth_line(jax.random.fold_in(key_line, 1), K * terms, NY).reshape(K, terms, NY)
    line_z = smooth_line(jax.random.fold_in(key_line, 2), K * terms, CZ).reshape(K, terms, CZ)
    blocks_x = NX // CX
    blocks_y = NY // CY
    own_low, own_high, mix_bound = (0.6, 1.4, 0.5)
    own_scale = jax.random.uniform(key_own, (K, blocks_x, blocks_y), jnp.float32, own_low, own_high)
    mixing = jax.random.uniform(key_mix, (3, K, blocks_x, blocks_y), jnp.float32, -mix_bound, mix_bound)
    steps_list = (1, 5, 11)

    def expand(grid):
        return jnp.repeat(jnp.repeat(grid, CX, axis=0), CY, axis=1)

    def base_of(vector):
        total = jnp.zeros((CZ, NX, NY), jnp.float32)
        for term in range(terms):
            total = total + line_z[vector, term][:, None, None] * line_x[vector, term][None, :, None] * line_y[vector, term][None, None, :]
        return total * 0.57735
    coords_x = jnp.arange(NX) % CX
    coords_y = jnp.arange(NY) % CY
    dist_x = jnp.minimum(coords_x, CX - 1 - coords_x)
    dist_y = jnp.minimum(coords_y, CY - 1 - coords_y)
    dist = jnp.minimum(dist_x[:, None], dist_y[None, :]).astype(jnp.float32)
    envelope = 1.0 + 4.0 * jnp.exp(-dist)

    def one_vector(vector):
        mixed = expand(own_scale[vector])[None, :, :] * base_of(vector)
        for index, step in enumerate(steps_list):
            mixed = mixed + expand(mixing[index, vector])[None, :, :] * base_of((vector + step) % K)
        noise_key = jax.random.fold_in(key_noise, vector)
        noise = jnp.clip(jax.random.normal(noise_key, (CZ, NX, NY), jnp.float32), -4.0, 4.0)
        return mixed * envelope[None, :, :] + 0.12 * noise
    factor = 0.5 * float(CX * CY * CZ) ** (-0.5)
    fields = lax.map(one_vector, jnp.arange(K, dtype=jnp.int32))
    return (fields * factor).astype(jnp.bfloat16)


def draw_phase_labels(key, part):
    key_cell, key_zone = jax.random.split(key)
    cells = jax.random.randint(key_cell, (CZ, NX, NY), 0, 2)
    zones = jax.random.randint(key_zone, (1, NX // CX, NY // CY), 0, PHASES)
    zones = jnp.repeat(jnp.repeat(zones, CX, axis=1), CY, axis=2)
    return ((cells + zones) % PHASES).astype(jnp.int32)


def setup_inputs(seed: int = 0) -> dict:
    key_of = jax.random.split(jax.random.key(seed), 4)
    return {
        "geneo_vectors": draw_geneo_vectors(jax.random.fold_in(key_of[3], 71), 0),
        "phase_labels": draw_phase_labels(jax.random.fold_in(key_of[3], 71), 0),
        "phase_mobility": jnp.clip(jnp.exp(jax.random.uniform(key_of[2], (PHASES,), jnp.float32, math.log(0.5), math.log(5.0))), 0.5, 5.0),
    }


FACES = ((-1, 0), (1, 0), (0, -1), (0, 1))

def slot_offsets():
    offsets = [((0, 0), (0, 0))]
    for face in FACES:
        offsets += [((0, 0), face), (face, (0, 0)), (face, face)]
    for face_x in FACES[:2]:
        for face_y in FACES[2:]:
            offsets += [(face_x, face_y), (face_y, face_x)]
    return offsets

def band_index(from_off, to_off):
    return (to_off[0] - from_off[0] + 1) * 3 + (to_off[1] - from_off[1] + 1)

def laplace_own(own):
    field = own.astype(jnp.float32)
    padded = jnp.pad(field, ((0, 0), (1, 1), (1, 1), (1, 1)))
    near = padded[:, 2:, 1:-1, 1:-1] + padded[:, :-2, 1:-1, 1:-1]
    near = near + padded[:, 1:-1, 2:, 1:-1] + padded[:, 1:-1, :-2, 1:-1]
    near = near + padded[:, 1:-1, 1:-1, 2:] + padded[:, 1:-1, 1:-1, :-2]
    return near - 6.0 * field

def contract_cells(left, right):
    flat_left = left.reshape(left.shape[0], -1)
    flat_right = right.reshape(right.shape[0], -1)
    return lax.dot_general(flat_left.astype(jnp.float32), flat_right.astype(jnp.float32), (((1,), (1,)), ((), ())), preferred_element_type=jnp.float32)

def local_tiles(window, labels, mobility_table):
    own = window[:, :, 1:-1, 1:-1]
    root_table = jnp.sqrt(mobility_table)
    cell_root = jnp.zeros(labels.shape, jnp.float32)
    for phase in range(mobility_table.shape[0]):
        cell_root = cell_root + jnp.where(labels == phase, root_table[phase], jnp.float32(0.0))
    flux = (laplace_own(own) * cell_root).astype(jnp.bfloat16)
    tiles = [contract_cells(own, own) + contract_cells(flux, flux)]
    face_data = [(flux[:, :, 0, :], window[:, :, 0, 1:-1], cell_root[:, 0, :]), (flux[:, :, -1, :], window[:, :, -1, 1:-1], cell_root[:, -1, :]), (flux[:, :, :, 0], window[:, :, 1:-1, 0], cell_root[:, :, 0]), (flux[:, :, :, -1], window[:, :, 1:-1, -1], cell_root[:, :, -1])]
    for layer_f, layer_z, layer_r in face_data:
        across = (layer_z.astype(jnp.float32) * layer_r).astype(jnp.bfloat16)
        cross = contract_cells(layer_f, across)
        tiles += [cross, cross.T, contract_cells(across, across)]
    for x_first in (True, False):
        for y_first in (True, False):
            inner_x = 1 if x_first else -2
            outer_x = 0 if x_first else -1
            inner_y = 1 if y_first else -2
            outer_y = 0 if y_first else -1
            cell_x = 0 if x_first else -1
            cell_y = 0 if y_first else -1
            corner_r = cell_root[:, cell_x, cell_y]
            along_x = (window[:, :, outer_x, inner_y].astype(jnp.float32) * corner_r).astype(jnp.bfloat16)
            along_y = (window[:, :, inner_x, outer_y].astype(jnp.float32) * corner_r).astype(jnp.bfloat16)
            pair = contract_cells(along_x, along_y)
            tiles += [pair, pair.T]
    return jnp.stack(tiles)

def shift_grid(values, offset):
    widths = [(1, 1), (1, 1)] + [(0, 0)] * (values.ndim - 2)
    padded = jnp.pad(values, widths)
    start_x = 1 - offset[0]
    start_y = 1 - offset[1]
    return padded[start_x:start_x + values.shape[0], start_y:start_y + values.shape[1]]

def reference(geneo_vectors, phase_labels, phase_mobility):
    padded = jnp.pad(geneo_vectors, ((0, 0), (0, 0), (1, 1), (1, 1)))
    zero = jnp.zeros((), jnp.int32)

    def one_device(index):
        grid_x = (index // N_COL).astype(jnp.int32)
        grid_y = (index % N_COL).astype(jnp.int32)
        start_x = (grid_x * CX).astype(jnp.int32)
        start_y = (grid_y * CY).astype(jnp.int32)
        window = lax.dynamic_slice(padded, (zero, zero, start_x, start_y), (K, CZ, CX + 2, CY + 2))
        labels = lax.dynamic_slice(phase_labels, (zero, start_x, start_y), (CZ, CX, CY))
        return local_tiles(window, labels, phase_mobility)
    offsets = slot_offsets()
    tiles = lax.map(one_device, jnp.arange(NSUB, dtype=jnp.int32))
    grid = tiles.reshape(N_ROW, N_COL, len(offsets), K, K)
    bands = [jnp.zeros((N_ROW, N_COL, K, K), jnp.float32) for count in range(9)]
    for slot, pair_off in enumerate(offsets):
        place = band_index(pair_off[0], pair_off[1])
        bands[place] = bands[place] + shift_grid(grid[:, :, slot], pair_off[0])
    sub_x = (jnp.arange(NSUB, dtype=jnp.int32) // N_COL).astype(jnp.int32)
    sub_y = (jnp.arange(NSUB, dtype=jnp.int32) % N_COL).astype(jnp.int32)
    dense = jnp.zeros((NSUB, K, NSUB, K), jnp.float32)
    for index in range(9):
        step_x = index // 3 - 1
        step_y = index % 3 - 1
        match = ((sub_x[None, :] == sub_x[:, None] + step_x) & (sub_y[None, :] == sub_y[:, None] + step_y)).astype(jnp.float32)
        dense = dense + match[:, None, :, None] * bands[index].reshape(NSUB, K, 1, K)
    matrix = dense.reshape(ORDER, ORDER)
    for panel in range(2):
        first = panel * WIDTH
        last = first + WIDTH
        low = jnp.linalg.cholesky(matrix[first:last, first:last])
        block = matrix[first:, first:last].T
        solved = lax.linalg.triangular_solve(low, block, left_side=True, lower=True)
        matrix = matrix.at[:first, first:last].set(0.0)
        matrix = matrix.at[first:, first:last].set(solved.T)
        tail = solved[:, WIDTH:]
        product = lax.dot_general(tail.astype(jnp.float32), tail.astype(jnp.float32), (((0,), (0,)), ((), ())), precision=lax.Precision.HIGHEST, preferred_element_type=jnp.float32)
        matrix = matrix.at[last:, last:].add(-product)
        matrix = matrix.at[first:last, last:].set(0.0)
    shaped = matrix.reshape(NSUB, KTR, N_ROW, NB, NSUB, KTC, N_COL, NB)
    return shaped.transpose(4, 5, 6, 7, 1, 2, 3, 0)
```

```python
import jax
import jax.numpy as jnp
from jax import lax
from jax.experimental import pallas as pl
from jax.experimental.pallas import tpu as pltpu
from jax.sharding import PartitionSpec as P

NB = 2
PSUB = 2


FACES = ((-1, 0), (1, 0), (0, -1), (0, 1))


def slot_offsets():
    offsets = [((0, 0), (0, 0))]
    for face in FACES:
        offsets += [((0, 0), face), (face, (0, 0)), (face, face)]
    for face_x in FACES[:2]:
        for face_y in FACES[2:]:
            offsets += [(face_x, face_y), (face_y, face_x)]
    return offsets


def band_index(from_off, to_off):
    return (to_off[0] - from_off[0] + 1) * 3 + (to_off[1] - from_off[1] + 1)


ROWS = 8
GROUP = 8


def gram_kernel(mob_ref, own_ref, lab_ref, acc_ref, rim_ref, frim_ref, edge_ref, rootx_ref, rooty_ref,
                plain_ref, part_ref, rows_ref, root_ref, lines_ref, side_ref):
    g = pl.program_id(0)
    n_z = pl.num_programs(0) - 1
    vectors, n_x, n_y = edge_ref.shape
    blocks = n_x // ROWS
    groups = vectors // GROUP
    per = blocks // groups
    lanes = lax.broadcasted_iota(jnp.int32, (n_x, n_y), 1)
    now = lax.rem(g, 2)
    old = 1 - now

    @pl.when(g == 0)
    def _():
        acc_ref[...] = jnp.zeros_like(acc_ref)
        side_ref[...] = jnp.zeros_like(side_ref)
        rooty_ref[...] = jnp.zeros_like(rooty_ref)
        plain_ref[...] = jnp.zeros_like(plain_ref)
        part_ref[...] = jnp.zeros_like(part_ref)
        rows_ref[...] = jnp.zeros_like(rows_ref)
        root_ref[...] = jnp.zeros_like(root_ref)

    def gram(slot, j):
        both = rows_ref[slot, j]
        acc_ref[...] += lax.dot_general(both, both, (((1,), (1,)), ((), ())), preferred_element_type=jnp.float32)

    def trip(j, fresh):
        root = root_ref[old]
        spot = pl.multiple_of(j * GROUP * ROWS, GROUP * ROWS)
        line = pl.multiple_of(j * GROUP, GROUP)
        ok = (lanes < 4 * g + 4) & (lanes >= 4 * g)
        fluxes, olds = [], []
        for i in range(GROUP):
            v = j * GROUP + i
            before = plain_ref[old, v, ROWS : ROWS + n_x]
            total = part_ref[v]
            if fresh:
                own = own_ref[v, 0].astype(jnp.float32)
                plain_ref[now, v, ROWS : ROWS + n_x] = own
                total = total + own
                near = plain_ref[now, v, ROWS + 1 : ROWS + 1 + n_x] + plain_ref[now, v, ROWS - 1 : ROWS - 1 + n_x]
                near = near + jnp.where(lanes == n_y - 1, 0.0, pltpu.roll(own, n_y - 1, 1))
                near = near + jnp.where(lanes == 0, 0.0, pltpu.roll(own, 1, 1))
                near = near + before
                part_ref[v] = near - 6.0 * own
                turned = pltpu.roll(own, 4 * g + 2, 1)
                side_ref[v] = jnp.where(ok, turned, side_ref[v])
                lines_ref[0, pl.ds(line + i, 1)] = own[:1]
                lines_ref[1, pl.ds(line + i, 1)] = own[n_x - 1 :]
            flux = total * root
            lines_ref[2, pl.ds(line + i, 1)] = flux[:1]
            lines_ref[3, pl.ds(line + i, 1)] = flux[n_x - 1 :]
            fluxes.append(flux)
            olds.append(before)
            if i % 2:
                for b in range(blocks):
                    part = slice(b * ROWS, b * ROWS + ROWS)
                    where = pl.ds(spot + (i - 1) * ROWS, 2 * ROWS)
                    at = (b % per) * 2 * n_y
                    rows_ref[now, b // per, where, at : at + n_y] = jnp.concatenate(
                        [olds[i - 1][part], olds[i][part]], axis=0).astype(jnp.bfloat16)
                    rows_ref[now, b // per, where, at + n_y : at + 2 * n_y] = jnp.concatenate(
                        [fluxes[i - 1][part], fluxes[i][part]], axis=0).astype(jnp.bfloat16)
        gram(old, j)

    @pl.when(g < n_z)
    def _():
        def step(j, carry):
            trip(j, True)
            return carry
        lax.fori_loop(0, groups, step, 0)
        value = jnp.zeros((n_x, n_y), jnp.float32)
        for phase in range(mob_ref.shape[0]):
            value = value + jnp.where(lab_ref[0] == phase, mob_ref[phase], jnp.float32(0.0))
        root = jnp.sqrt(value)
        root_ref[now] = root
        rootx_ref[0, 0:1] = root[:1]
        rootx_ref[0, 1:2] = root[n_x - 1 :]
        ok = (lanes < 4 * g + 4) & (lanes >= 4 * g)
        rooty_ref[...] = jnp.where(ok, pltpu.roll(root, 4 * g + 2, 1), rooty_ref[...])
        for side in range(2):
            rim_ref[0, side] = lines_ref[side].astype(jnp.bfloat16)

    @pl.when(g == n_z)
    def _():
        def step(j, carry):
            trip(j, False)
            return carry
        lax.fori_loop(0, groups, step, 0)
        for j in range(groups):
            gram(now, j)
        edge_ref[...] = side_ref[...].astype(jnp.bfloat16)

    for side in range(2):
        frim_ref[0, side] = lines_ref[2 + side].astype(jnp.bfloat16)


def gram_call(own, labels, mobility):
    vectors, n_z, n_x, n_y = own.shape
    order = vectors * ROWS
    blocks = n_x // ROWS
    groups = vectors // GROUP
    f32, bf16 = jnp.float32, jnp.bfloat16
    last = n_z - 1
    return pl.pallas_call(
        gram_kernel,
        grid=(n_z + 1,),
        in_specs=[
            pl.BlockSpec(memory_space=pltpu.SMEM),
            pl.BlockSpec((vectors, 1, n_x, n_y), lambda g: (0, jnp.minimum(g, last), 0, 0)),
            pl.BlockSpec((1, n_x, n_y), lambda g: (jnp.minimum(g, last), 0, 0)),
        ],
        out_specs=[
            pl.BlockSpec((order, order), lambda g: (0, 0)),
            pl.BlockSpec((1, 2, vectors, n_y), lambda g: (jnp.minimum(g, last), 0, 0, 0)),
            pl.BlockSpec((1, 2, vectors, n_y), lambda g: (jnp.maximum(g - 1, 0), 0, 0, 0)),
            pl.BlockSpec((vectors, n_x, n_y), lambda g: (0, 0, 0)),
            pl.BlockSpec((1, 2, n_y), lambda g: (jnp.minimum(g, last), 0, 0)),
            pl.BlockSpec((n_x, n_y), lambda g: (0, 0)),
        ],
        out_shape=[
            jax.ShapeDtypeStruct((order, order), f32),
            jax.ShapeDtypeStruct((n_z, 2, vectors, n_y), bf16),
            jax.ShapeDtypeStruct((n_z, 2, vectors, n_y), bf16),
            jax.ShapeDtypeStruct((vectors, n_x, n_y), bf16),
            jax.ShapeDtypeStruct((n_z, 2, n_y), f32),
            jax.ShapeDtypeStruct((n_x, n_y), f32),
        ],
        scratch_shapes=[
            pltpu.VMEM((2, vectors, n_x + 2 * ROWS, n_y), f32),
            pltpu.VMEM((vectors, n_x, n_y), f32),
            pltpu.VMEM((2, groups, order, blocks // groups * 2 * n_y), bf16),
            pltpu.VMEM((2, n_x, n_y), f32),
            pltpu.VMEM((4, vectors, n_y), f32),
            pltpu.VMEM((vectors, n_x, n_y), f32),
        ],
        compiler_params=pltpu.CompilerParams(vmem_limit_bytes=40 * 1024 * 1024),
    )(mobility, own, labels)


SLOTS = 21
MINOR = (((1,), (1,)), ((), ()))


def tile_kernel(acc_ref, frim_ref, edge_ref, rootx_ref, rooty_ref, xlow_ref, xupp_ref, ylow_ref, yupp_ref, out_ref,
                left_ref, right_ref, faces_ref, cut_ref):
    vectors, n_x, n_y = edge_ref.shape
    n_z = frim_ref.shape[0]
    order = acc_ref.shape[0]
    blocks = n_x // ROWS
    f32, bf16 = jnp.float32, jnp.bfloat16
    rows = lax.broadcasted_iota(jnp.int32, (n_x, n_y), 0)
    lanes = lax.broadcasted_iota(jnp.int32, (n_x, n_y), 1)
    spot = lanes % 4
    root = jnp.where((spot == 1) | (spot == 2), rooty_ref[...], 0.0)

    def pair_of(m, carry):
        kept = []
        for i in range(2):
            v = 2 * m + i
            own = edge_ref[v].astype(f32)
            near = jnp.where(lanes < 4, 0.0, pltpu.roll(own, 4, 1))
            near = near + jnp.where(lanes >= n_y - 4, 0.0, pltpu.roll(own, n_y - 4, 1))
            near = near + jnp.where(rows == 0, 0.0, pltpu.roll(own, 1, 0))
            near = near + jnp.where(rows == n_x - 1, 0.0, pltpu.roll(own, n_x - 1, 0))
            near = near + jnp.where(spot == 2, pltpu.roll(own, n_y - 1, 1), pltpu.roll(own, 1, 1))
            flux = (near - 6.0 * own) * root
            low = pltpu.roll(ylow_ref[v].astype(f32), 1, 1)
            upp = pltpu.roll(yupp_ref[v].astype(f32), n_y - 1, 1)
            over = jnp.where(spot == 2, low, upp) * root
            cut_ref[0, pl.ds(v, 1)] = over[:1]
            cut_ref[1, pl.ds(v, 1)] = over[n_x - 1 :]
            kept.append((flux, over, jnp.where(spot == 2, over, 0.0), jnp.where(spot == 1, over, 0.0)))
        for b in range(blocks):
            part = slice(b * ROWS, b * ROWS + ROWS)
            both = [jnp.concatenate([x[part], y[part]], axis=0).astype(bf16) for x, y in zip(*kept)]
            at = slice(b * n_y, b * n_y + n_y)
            first = pl.ds(pl.multiple_of(m * 2 * ROWS, 2 * ROWS), 2 * ROWS)
            second = pl.ds(pl.multiple_of(order + m * 2 * ROWS, 2 * ROWS), 2 * ROWS)
            left_ref[first, at] = both[0]
            left_ref[second, at] = both[1]
            right_ref[first, at] = both[2]
            right_ref[second, at] = both[3]
        return carry

    lax.fori_loop(0, vectors // 2, pair_of, 0)
    crossed = lax.dot_general(left_ref[...], right_ref[...], MINOR, preferred_element_type=f32)

    thin = lax.broadcasted_iota(jnp.int32, (vectors, n_y), 1)
    ends = []
    for side, halo_ref in enumerate((xlow_ref, xupp_ref)):
        total = jnp.zeros((vectors, n_y), f32)
        for z in range(n_z):
            over = halo_ref[z].astype(f32) * rootx_ref[z, side : side + 1]
            at = slice(z * n_y, z * n_y + n_y)
            faces_ref[side, :vectors, at] = frim_ref[z, side]
            faces_ref[side, vectors:, at] = over.astype(bf16)
            ok = (thin >= 4 * z) & (thin < 4 * z + 4)
            total = jnp.where(ok, pltpu.roll(over, (4 * z + 2) % n_y, 1), total)
        ends.append(total.astype(bf16))

    def put(slot, value):
        out_ref[:, slot * vectors : (slot + 1) * vectors] = value

    line = lax.broadcasted_iota(jnp.int32, (order, order), 0)
    column = lax.broadcasted_iota(jnp.int32, (order, order), 1)
    same = line % ROWS == column % ROWS
    pick = (lax.broadcasted_iota(jnp.int32, (order, vectors), 0) // ROWS
            == lax.broadcasted_iota(jnp.int32, (order, vectors), 1)).astype(f32)

    def fold(square):
        thick = jnp.where(same, square, 0.0).reshape(vectors, ROWS, order).sum(1)
        return lax.dot_general(thick, pick, (((1,), (0,)), ((), ())), precision=lax.Precision.HIGHEST,
                               preferred_element_type=f32)

    put(0, fold(acc_ref[...]))
    for side in range(2):
        gram = lax.dot_general(faces_ref[side], faces_ref[side], MINOR, preferred_element_type=f32)
        put(1 + 3 * side, gram[vectors:, :vectors])
        put(2 + 3 * side, gram[:vectors, vectors:])
        put(3 + 3 * side, gram[vectors:, vectors:])
        here = slice(side * order, side * order + order)
        cross = fold(crossed[:order, here])
        put(7 + 3 * side, cross.T)
        put(8 + 3 * side, cross)
        put(9 + 3 * side, fold(crossed[order:, here]))
    slot = 13
    for x in range(2):
        for y in range(2):
            along = jnp.where(thin % 4 == 2 - y, cut_ref[x], 0.0).astype(bf16)
            put(slot, lax.dot_general(along, ends[x], MINOR, preferred_element_type=f32))
            put(slot + 1, lax.dot_general(ends[x], along, MINOR, preferred_element_type=f32))
            slot += 2
    out_ref[:, SLOTS * vectors :] = jnp.zeros((vectors, out_ref.shape[1] - SLOTS * vectors), f32)


def tile_call(acc, frim, edge, rootx, rooty, xlow, xupp, ylow, yupp):
    vectors, n_x, n_y = edge.shape
    n_z = frim.shape[0]
    order = acc.shape[0]
    whole = pl.BlockSpec(memory_space=pltpu.VMEM)
    return pl.pallas_call(
        tile_kernel,
        in_specs=[whole] * 9,
        out_specs=whole,
        out_shape=jax.ShapeDtypeStruct((vectors, -(-SLOTS * vectors // n_y) * n_y), jnp.float32),
        scratch_shapes=[
            pltpu.VMEM((2 * order, n_x // ROWS * n_y), jnp.bfloat16),
            pltpu.VMEM((2 * order, n_x // ROWS * n_y), jnp.bfloat16),
            pltpu.VMEM((2, 2 * vectors, n_z * n_y), jnp.bfloat16),
            pltpu.VMEM((2, vectors, n_y), jnp.float32),
        ],
        compiler_params=pltpu.CompilerParams(vmem_limit_bytes=40 * 1024 * 1024),
    )(acc, frim, edge, rootx, rooty, xlow, xupp, ylow, yupp)


def local_tiles(own, labels, mobility_table):
    acc, rim, frim, edge, rootx, rooty = gram_call(own, labels, mobility_table)
    n_row = lax.axis_size("row")
    n_col = lax.axis_size("col")

    def up(values, axis, count):
        return lax.ppermute(values, axis, [(i, i + 1) for i in range(count - 1)])

    def down(values, axis, count):
        return lax.ppermute(values, axis, [(i + 1, i) for i in range(count - 1)])

    tiles = tile_call(
        acc, frim, edge, rootx, rooty,
        up(rim[:, 1], "row", n_row), down(rim[:, 0], "row", n_row),
        up(edge, "col", n_col), down(edge, "col", n_col),
    )
    vectors = own.shape[0]
    return tiles[:, : SLOTS * vectors].reshape(vectors, SLOTS, vectors).transpose(1, 2, 0)


def shift_grid(values, offset):
    widths = [(1, 1), (1, 1)] + [(0, 0)] * (values.ndim - 2)
    padded = jnp.pad(values, widths)
    start_x = 1 - offset[0]
    start_y = 1 - offset[1]
    return padded[start_x : start_x + values.shape[0], start_y : start_y + values.shape[1]]


def to_owner(stack, n_row, n_col):
    slots = stack.shape[0]
    vectors = stack.shape[1]
    row_blocks = vectors // (NB * n_row)
    col_blocks = vectors // (NB * n_col)
    split = stack.reshape(slots, row_blocks, n_row, NB, col_blocks, n_col, NB)
    moved = split.transpose(2, 5, 0, 4, 6, 1, 3)
    return moved.reshape(n_row, n_col, slots * col_blocks * NB * row_blocks * NB)


def place_bands(bands, n_row, n_col):
    n_sub = n_row * n_col
    sub_x = jnp.arange(n_sub, dtype=jnp.int32) // n_col
    sub_y = jnp.arange(n_sub, dtype=jnp.int32) % n_col
    total = None
    for index in range(9):
        step_x = index // 3 - 1
        step_y = index % 3 - 1
        match = (
            (sub_x[:, None] == sub_x[None, :] + step_x)
            & (sub_y[:, None] == sub_y[None, :] + step_y)
        ).astype(jnp.float32)
        flat = bands[index].reshape(n_sub, -1).T
        term = match[:, None, :] * flat[None, :, :]
        total = term if total is None else total + term
    return total


def body(geneo_vectors, phase_labels, phase_mobility):
    vectors = geneo_vectors.shape[0]
    n_row = lax.axis_size("row")
    n_col = lax.axis_size("col")
    n_sub = n_row * n_col
    row_blocks = vectors // (NB * n_row)
    col_blocks = vectors // (NB * n_col)
    rows_here = row_blocks * NB * n_sub
    piece_len = col_blocks * NB * row_blocks * NB
    width = PSUB * vectors
    tiles = local_tiles(geneo_vectors, phase_labels, phase_mobility)
    offsets = slot_offsets()
    routed = lax.all_to_all(
        lax.all_to_all(
            to_owner(tiles, n_row, n_col), "row", split_axis=0, concat_axis=0, tiled=True
        ),
        "col",
        split_axis=1,
        concat_axis=1,
        tiled=True,
    )
    routed = routed.reshape(n_row, n_col, len(offsets), piece_len)
    bands = [jnp.zeros((n_row, n_col, piece_len), jnp.float32) for count in range(9)]
    for slot, pair_off in enumerate(offsets):
        place = band_index(pair_off[0], pair_off[1])
        bands[place] = bands[place] + shift_grid(routed[:, :, slot], pair_off[0])
    local = place_bands(bands, n_row, n_col).reshape(n_sub, col_blocks * NB, rows_here)
    row_index = lax.axis_index("row")
    col_index = lax.axis_index("col")
    row_sub = jnp.arange(rows_here, dtype=jnp.int32) % n_sub
    ends = 2 * PSUB
    mine = local[:ends].reshape(ends, col_blocks, NB, rows_here)
    parts = lax.all_gather(mine, ("row", "col"), axis=0, tiled=False)
    parts = parts.reshape(n_row, n_col, ends, col_blocks, NB, rows_here)
    panels = parts.transpose(2, 3, 1, 4, 0, 5).reshape(2, width, n_row, rows_here)

    def rows_of(block, first, last):
        grid = block.reshape(width, n_row, row_blocks, NB, n_sub)[..., first:last]
        return grid.transpose(0, 4, 2, 1, 3).reshape(width, (last - first) * vectors)

    done = []
    for panel in range(2):
        first = panel * PSUB
        last = first + PSUB
        block = panels[panel]
        for solved in done:
            change = lax.dot_general(
                rows_of(solved, first, last),
                solved.reshape(width, n_row * rows_here),
                (((0,), (0,)), ((), ())),
                precision=lax.Precision.HIGHEST,
                preferred_element_type=jnp.float32,
            )
            block = block - change.reshape(width, n_row, rows_here)
        block = jnp.where(row_sub >= first, block, jnp.float32(0.0))
        low = jnp.linalg.cholesky(rows_of(block, first, last).T)
        solved = lax.linalg.triangular_solve(
            low, block.reshape(width, n_row * rows_here), left_side=True, lower=True
        ).reshape(width, n_row, rows_here)
        done.append(solved)
    both = jnp.concatenate(done, axis=0)
    rows_mine = lax.dynamic_index_in_dim(both, row_index, 1, keepdims=False)
    by_block = both.reshape(2 * width, n_row, row_blocks, NB, n_sub).transpose(0, 2, 1, 3, 4)
    picked = lax.dynamic_index_in_dim(
        by_block.reshape(2 * width, row_blocks, n_row // n_col, n_col, NB, n_sub),
        col_index,
        3,
        keepdims=False,
    )
    columns = (
        picked.reshape(2 * width, col_blocks * NB, n_sub)
        .transpose(0, 2, 1)
        .reshape(2 * width, n_sub * col_blocks * NB)
    )
    update = lax.dot_general(
        columns,
        rows_mine,
        (((0,), (0,)), ((), ())),
        precision=lax.Precision.HIGHEST,
        preferred_element_type=jnp.float32,
    ).reshape(n_sub, col_blocks * NB, rows_here)
    panel_mine = lax.dynamic_index_in_dim(
        rows_mine.reshape(ends, col_blocks, n_col, NB, rows_here), col_index, 2, keepdims=False
    ).reshape(ends, col_blocks * NB, rows_here)
    rest = jnp.where(row_sub < ends, jnp.float32(0.0), local[ends:] - update[ends:])
    local = jnp.concatenate([panel_mine, rest], axis=0)
    return local.reshape(n_sub, col_blocks, 1, NB, row_blocks, 1, NB, n_sub)


def solution(mesh):
    return jax.shard_map(
        body,
        mesh=mesh,
        in_specs=(P(None, None, "row", "col"), P(None, "row", "col"), P()),
        out_specs=P(None, None, "col", None, None, "row", None, None),
        check_vma=False,
    )
```

```python
import functools

import jax
import jax.numpy as jnp
from jax import lax
from jax.experimental import pallas as pl
from jax.experimental.pallas import tpu as pltpu
from jax.sharding import PartitionSpec as P

NB = 2
PSUB = 2
SLOTS = 21
MESH = pl.DeviceIdType.MESH
PLAIN = (((1,), (0,)), ((), ()))

ROWS = 8
GROUP = 8


def gram_kernel(mob_ref, own_ref, lab_ref, acc_ref, rim_ref, frim_ref, edge_ref, rootx_ref, rooty_ref,
                plain_ref, part_ref, rows_ref, root_ref, lines_ref, side_ref):
    g = pl.program_id(0)
    n_z = pl.num_programs(0) - 1
    vectors, n_x, n_y = edge_ref.shape
    blocks = n_x // ROWS
    groups = vectors // GROUP
    per = blocks // groups
    lanes = lax.broadcasted_iota(jnp.int32, (n_x, n_y), 1)
    now = lax.rem(g, 2)
    old = 1 - now

    @pl.when(g == 0)
    def _():
        acc_ref[...] = jnp.zeros_like(acc_ref)
        side_ref[...] = jnp.zeros_like(side_ref)
        rooty_ref[...] = jnp.zeros_like(rooty_ref)
        plain_ref[...] = jnp.zeros_like(plain_ref)
        part_ref[...] = jnp.zeros_like(part_ref)
        rows_ref[...] = jnp.zeros_like(rows_ref)
        root_ref[...] = jnp.zeros_like(root_ref)

    def gram(slot, j):
        both = rows_ref[slot, j]
        acc_ref[...] += lax.dot_general(both, both, (((1,), (1,)), ((), ())), preferred_element_type=jnp.float32)

    def trip(j, fresh):
        root = root_ref[old]
        spot = pl.multiple_of(j * GROUP * ROWS, GROUP * ROWS)
        line = pl.multiple_of(j * GROUP, GROUP)
        ok = (lanes < 4 * g + 4) & (lanes >= 4 * g)
        fluxes, olds = [], []
        for i in range(GROUP):
            v = j * GROUP + i
            before = plain_ref[old, v, ROWS : ROWS + n_x]
            total = part_ref[v]
            if fresh:
                own = own_ref[v, 0].astype(jnp.float32)
                plain_ref[now, v, ROWS : ROWS + n_x] = own
                total = total + own
                near = plain_ref[now, v, ROWS + 1 : ROWS + 1 + n_x] + plain_ref[now, v, ROWS - 1 : ROWS - 1 + n_x]
                near = near + jnp.where(lanes == n_y - 1, 0.0, pltpu.roll(own, n_y - 1, 1))
                near = near + jnp.where(lanes == 0, 0.0, pltpu.roll(own, 1, 1))
                near = near + before
                part_ref[v] = near - 6.0 * own
                turned = pltpu.roll(own, 4 * g + 2, 1)
                side_ref[v] = jnp.where(ok, turned, side_ref[v])
                lines_ref[0, pl.ds(line + i, 1)] = own[:1]
                lines_ref[1, pl.ds(line + i, 1)] = own[n_x - 1 :]
            flux = total * root
            lines_ref[2, pl.ds(line + i, 1)] = flux[:1]
            lines_ref[3, pl.ds(line + i, 1)] = flux[n_x - 1 :]
            fluxes.append(flux)
            olds.append(before)
            if i % 2:
                for b in range(blocks):
                    part = slice(b * ROWS, b * ROWS + ROWS)
                    where = pl.ds(spot + (i - 1) * ROWS, 2 * ROWS)
                    at = (b % per) * 2 * n_y
                    rows_ref[now, b // per, where, at : at + n_y] = jnp.concatenate(
                        [olds[i - 1][part], olds[i][part]], axis=0).astype(jnp.bfloat16)
                    rows_ref[now, b // per, where, at + n_y : at + 2 * n_y] = jnp.concatenate(
                        [fluxes[i - 1][part], fluxes[i][part]], axis=0).astype(jnp.bfloat16)
        gram(old, j)

    @pl.when(g < n_z)
    def _():
        def step(j, carry):
            trip(j, True)
            return carry
        lax.fori_loop(0, groups, step, 0)
        value = jnp.zeros((n_x, n_y), jnp.float32)
        for phase in range(mob_ref.shape[0]):
            value = value + jnp.where(lab_ref[0] == phase, mob_ref[phase], jnp.float32(0.0))
        root = jnp.sqrt(value)
        root_ref[now] = root
        rootx_ref[0, 0:1] = root[:1]
        rootx_ref[0, 1:2] = root[n_x - 1 :]
        ok = (lanes < 4 * g + 4) & (lanes >= 4 * g)
        rooty_ref[...] = jnp.where(ok, pltpu.roll(root, 4 * g + 2, 1), rooty_ref[...])
        for side in range(2):
            rim_ref[0, side] = lines_ref[side].astype(jnp.bfloat16)

    @pl.when(g == n_z)
    def _():
        def step(j, carry):
            trip(j, False)
            return carry
        lax.fori_loop(0, groups, step, 0)
        for j in range(groups):
            gram(now, j)
        edge_ref[...] = side_ref[...].astype(jnp.bfloat16)

    for side in range(2):
        frim_ref[0, side] = lines_ref[2 + side].astype(jnp.bfloat16)


def gram_call(own, labels, mobility):
    vectors, n_z, n_x, n_y = own.shape
    order = vectors * ROWS
    blocks = n_x // ROWS
    groups = vectors // GROUP
    f32, bf16 = jnp.float32, jnp.bfloat16
    last = n_z - 1
    return pl.pallas_call(
        gram_kernel,
        grid=(n_z + 1,),
        in_specs=[
            pl.BlockSpec(memory_space=pltpu.SMEM),
            pl.BlockSpec((vectors, 1, n_x, n_y), lambda g: (0, jnp.minimum(g, last), 0, 0)),
            pl.BlockSpec((1, n_x, n_y), lambda g: (jnp.minimum(g, last), 0, 0)),
        ],
        out_specs=[
            pl.BlockSpec((order, order), lambda g: (0, 0)),
            pl.BlockSpec((1, 2, vectors, n_y), lambda g: (jnp.minimum(g, last), 0, 0, 0)),
            pl.BlockSpec((1, 2, vectors, n_y), lambda g: (jnp.maximum(g - 1, 0), 0, 0, 0)),
            pl.BlockSpec((vectors, n_x, n_y), lambda g: (0, 0, 0)),
            pl.BlockSpec((1, 2, n_y), lambda g: (jnp.minimum(g, last), 0, 0)),
            pl.BlockSpec((n_x, n_y), lambda g: (0, 0)),
        ],
        out_shape=[
            jax.ShapeDtypeStruct((order, order), f32),
            jax.ShapeDtypeStruct((n_z, 2, vectors, n_y), bf16),
            jax.ShapeDtypeStruct((n_z, 2, vectors, n_y), bf16),
            jax.ShapeDtypeStruct((vectors, n_x, n_y), bf16),
            jax.ShapeDtypeStruct((n_z, 2, n_y), f32),
            jax.ShapeDtypeStruct((n_x, n_y), f32),
        ],
        scratch_shapes=[
            pltpu.VMEM((2, vectors, n_x + 2 * ROWS, n_y), f32),
            pltpu.VMEM((vectors, n_x, n_y), f32),
            pltpu.VMEM((2, groups, order, blocks // groups * 2 * n_y), bf16),
            pltpu.VMEM((2, n_x, n_y), f32),
            pltpu.VMEM((4, vectors, n_y), f32),
            pltpu.VMEM((vectors, n_x, n_y), f32),
        ],
        compiler_params=pltpu.CompilerParams(vmem_limit_bytes=40 * 1024 * 1024),
    )(mobility, own, labels)


MINOR = (((1,), (1,)), ((), ()))


def tile_kernel(acc_ref, frim_ref, edge_ref, rootx_ref, rooty_ref, xlow_ref, xupp_ref, ylow_ref, yupp_ref, out_ref,
                left_ref, right_ref, faces_ref, cut_ref):
    vectors, n_x, n_y = edge_ref.shape
    n_z = frim_ref.shape[0]
    order = acc_ref.shape[0]
    blocks = n_x // ROWS
    f32, bf16 = jnp.float32, jnp.bfloat16
    rows = lax.broadcasted_iota(jnp.int32, (n_x, n_y), 0)
    lanes = lax.broadcasted_iota(jnp.int32, (n_x, n_y), 1)
    spot = lanes % 4
    root = jnp.where((spot == 1) | (spot == 2), rooty_ref[...], 0.0)

    def pair_of(m, carry):
        kept = []
        for i in range(2):
            v = 2 * m + i
            own = edge_ref[v].astype(f32)
            near = jnp.where(lanes < 4, 0.0, pltpu.roll(own, 4, 1))
            near = near + jnp.where(lanes >= n_y - 4, 0.0, pltpu.roll(own, n_y - 4, 1))
            near = near + jnp.where(rows == 0, 0.0, pltpu.roll(own, 1, 0))
            near = near + jnp.where(rows == n_x - 1, 0.0, pltpu.roll(own, n_x - 1, 0))
            near = near + jnp.where(spot == 2, pltpu.roll(own, n_y - 1, 1), pltpu.roll(own, 1, 1))
            flux = (near - 6.0 * own) * root
            low = pltpu.roll(ylow_ref[v].astype(f32), 1, 1)
            upp = pltpu.roll(yupp_ref[v].astype(f32), n_y - 1, 1)
            over = jnp.where(spot == 2, low, upp) * root
            cut_ref[0, pl.ds(v, 1)] = over[:1]
            cut_ref[1, pl.ds(v, 1)] = over[n_x - 1 :]
            kept.append((flux, over, jnp.where(spot == 2, over, 0.0), jnp.where(spot == 1, over, 0.0)))
        for b in range(blocks):
            part = slice(b * ROWS, b * ROWS + ROWS)
            both = [jnp.concatenate([x[part], y[part]], axis=0).astype(bf16) for x, y in zip(*kept)]
            at = slice(b * n_y, b * n_y + n_y)
            first = pl.ds(pl.multiple_of(m * 2 * ROWS, 2 * ROWS), 2 * ROWS)
            second = pl.ds(pl.multiple_of(order + m * 2 * ROWS, 2 * ROWS), 2 * ROWS)
            left_ref[first, at] = both[0]
            left_ref[second, at] = both[1]
            right_ref[first, at] = both[2]
            right_ref[second, at] = both[3]
        return carry

    lax.fori_loop(0, vectors // 2, pair_of, 0)
    crossed = lax.dot_general(left_ref[...], right_ref[...], MINOR, preferred_element_type=f32)

    thin = lax.broadcasted_iota(jnp.int32, (vectors, n_y), 1)
    ends = []
    for side, halo_ref in enumerate((xlow_ref, xupp_ref)):
        total = jnp.zeros((vectors, n_y), f32)
        for z in range(n_z):
            over = halo_ref[z].astype(f32) * rootx_ref[z, side : side + 1]
            at = slice(z * n_y, z * n_y + n_y)
            faces_ref[side, :vectors, at] = frim_ref[z, side]
            faces_ref[side, vectors:, at] = over.astype(bf16)
            ok = (thin >= 4 * z) & (thin < 4 * z + 4)
            total = jnp.where(ok, pltpu.roll(over, (4 * z + 2) % n_y, 1), total)
        ends.append(total.astype(bf16))

    def put(slot, value):
        out_ref[:, slot * vectors : (slot + 1) * vectors] = value

    line = lax.broadcasted_iota(jnp.int32, (order, order), 0)
    column = lax.broadcasted_iota(jnp.int32, (order, order), 1)
    same = line % ROWS == column % ROWS
    pick = (lax.broadcasted_iota(jnp.int32, (order, vectors), 0) // ROWS
            == lax.broadcasted_iota(jnp.int32, (order, vectors), 1)).astype(f32)

    def fold(square):
        thick = jnp.where(same, square, 0.0).reshape(vectors, ROWS, order).sum(1)
        return lax.dot_general(thick, pick, (((1,), (0,)), ((), ())), precision=lax.Precision.HIGHEST,
                               preferred_element_type=f32)

    put(0, fold(acc_ref[...]))
    for side in range(2):
        gram = lax.dot_general(faces_ref[side], faces_ref[side], MINOR, preferred_element_type=f32)
        put(1 + 3 * side, gram[vectors:, :vectors])
        put(2 + 3 * side, gram[:vectors, vectors:])
        put(3 + 3 * side, gram[vectors:, vectors:])
        here = slice(side * order, side * order + order)
        cross = fold(crossed[:order, here])
        put(7 + 3 * side, cross.T)
        put(8 + 3 * side, cross)
        put(9 + 3 * side, fold(crossed[order:, here]))
    slot = 13
    for x in range(2):
        for y in range(2):
            along = jnp.where(thin % 4 == 2 - y, cut_ref[x], 0.0).astype(bf16)
            put(slot, lax.dot_general(along, ends[x], MINOR, preferred_element_type=f32))
            put(slot + 1, lax.dot_general(ends[x], along, MINOR, preferred_element_type=f32))
            slot += 2
    out_ref[:, SLOTS * vectors :] = jnp.zeros((vectors, out_ref.shape[1] - SLOTS * vectors), f32)


def tile_call(acc, frim, edge, rootx, rooty, xlow, xupp, ylow, yupp, n_col):
    vectors, n_x, n_y = edge.shape
    n_z = frim.shape[0]
    order = acc.shape[0]
    whole = pl.BlockSpec(memory_space=pltpu.VMEM)
    return pl.pallas_call(
        tile_kernel,
        in_specs=[whole] * 9,
        out_specs=whole,
        out_shape=jax.ShapeDtypeStruct((vectors, -(-SLOTS // n_col) * n_col * vectors), jnp.float32),
        scratch_shapes=[
            pltpu.VMEM((2 * order, n_x // ROWS * n_y), jnp.bfloat16),
            pltpu.VMEM((2 * order, n_x // ROWS * n_y), jnp.bfloat16),
            pltpu.VMEM((2, 2 * vectors, n_z * n_y), jnp.bfloat16),
            pltpu.VMEM((2, vectors, n_y), jnp.float32),
        ],
        compiler_params=pltpu.CompilerParams(vmem_limit_bytes=40 * 1024 * 1024),
    )(acc, frim, edge, rootx, rooty, xlow, xupp, ylow, yupp)


FACES = ((-1, 0), (1, 0), (0, -1), (0, 1))


def slot_offsets():
    offsets = [((0, 0), (0, 0))]
    for face in FACES:
        offsets += [((0, 0), face), (face, (0, 0)), (face, face)]
    for face_x in FACES[:2]:
        for face_y in FACES[2:]:
            offsets += [(face_x, face_y), (face_y, face_x)]
    return offsets


def exact_dot(left, right, dims=PLAIN):
    return lax.dot_general(left, right, dims, precision=lax.Precision.HIGHEST, preferred_element_type=jnp.float32)


def swap_bits(tiles, bits):
    lanes = lax.broadcasted_iota(jnp.int32, tiles[0].shape, 1)
    width = tiles[0].shape[1]
    for index, lane in bits:
        low = lanes // lane % 2 == 0
        out = list(tiles)
        for i in range(len(tiles)):
            if i // index % 2 == 0:
                a, b = tiles[i], tiles[i + index]
                out[i] = jnp.where(low, a, pltpu.roll(b, lane, 1))
                out[i + index] = jnp.where(low, pltpu.roll(a, width - lane, 1), b)
        tiles = out
    return tiles


def powers(count):
    return [1 << i for i in range(count.bit_length() - 1)]


def trade_kernel(n_row, n_col, tile_ref, out_ref, all_ref, send_ref, mine_ref, here_ref,
                 send_sem, recv_sem, send_sem2, recv_sem2):
    vectors = tile_ref.shape[0]
    n_sub = n_row * n_col
    col_blocks = vectors // (NB * n_col)
    width = n_col * vectors
    depth = col_blocks * NB
    r = lax.axis_index("row")
    c = lax.axis_index("col")
    me = r * n_col + c

    def peer(k):
        other = lax.rem(me + k, n_sub)
        return other, (other // n_col, lax.rem(other, n_col))

    barrier = pltpu.get_barrier_semaphore()

    def greet(k, carry):
        pl.semaphore_signal(barrier, inc=1, device_id=peer(k)[1], device_id_type=MESH)
        return carry

    lax.fori_loop(1, n_sub, greet, 0)

    at = lax.broadcasted_iota(jnp.int32, (vectors, vectors), 0)
    source = (at // NB % col_blocks * n_col + at // (NB * col_blocks)) * NB + at % NB
    turn = (source == lax.broadcasted_iota(jnp.int32, (vectors, vectors), 1)).astype(jnp.float32)
    ordered = exact_dot(turn, tile_ref[...])
    packs = tile_ref.shape[1] // width
    blank = jnp.zeros((depth, width), jnp.float32)
    for column in range(n_col):
        some = slice(column * depth, column * depth + depth)
        tiles = [ordered[some, k * width : k * width + width] if k < packs else blank for k in range(n_row)]
        tiles = swap_bits(tiles, [(bit, NB * bit) for bit in powers(n_row)])
        for row in range(n_row):
            send_ref[row * n_col + column] = tiles[row]
    pl.semaphore_wait(barrier, n_sub - 1)

    def exchange(kind, source_of, target_ref, sends, recvs):
        def copy(k):
            other, where = peer(k)
            return pltpu.make_async_remote_copy(
                src_ref=source_of(other), dst_ref=target_ref.at[me], send_sem=sends.at[other], recv_sem=recvs.at[me],
                device_id=where, device_id_type=MESH)

        def begin(k, carry):
            copy(k).start()
            return carry

        lax.fori_loop(1, n_sub, begin, 0)

        def finish(k, carry):
            other, where = peer(k)
            pltpu.make_async_remote_copy(
                src_ref=source_of(other), dst_ref=target_ref.at[other], send_sem=sends.at[other],
                recv_sem=recvs.at[other], device_id=where, device_id_type=MESH).wait_recv()
            return carry

        lax.fori_loop(1, n_sub, finish, 0)

        def drain(k, carry):
            copy(k).wait_send()
            return carry

        lax.fori_loop(1, n_sub, drain, 0)

    here_ref[me] = send_ref[me]
    exchange("tiles", lambda other: send_ref.at[other], here_ref, send_sem, recv_sem)

    tiles = [here_ref[s] for s in range(n_sub)]
    quads = n_sub // n_row
    bits = [(bit, NB * bit) for bit in powers(n_row)]
    bits += [(n_row * bit, vectors * bit) for bit in powers(quads)]
    tiles = swap_bits(tiles, bits)
    offsets = slot_offsets()
    stack = jnp.concatenate([tiles[slot % quads * n_row + slot // quads] for slot in range(SLOTS)], axis=0)
    into = lax.broadcasted_iota(jnp.int32, (width, width), 1)
    sub, tru = into % n_sub, into // n_sub
    origin = sub // n_row * vectors + (tru // NB * n_row + sub % n_row) * NB + tru % NB
    order = (origin == lax.broadcasted_iota(jnp.int32, (width, width), 0)).astype(jnp.float32)
    stack = exact_dot(stack, order)
    bands = {}
    for slot, (start, stop) in enumerate(offsets):
        value = stack[slot * depth : slot * depth + depth]
        shift = start[0] * n_col + start[1]
        if shift:
            value = pltpu.roll(value, shift % width, 1)
        step = (stop[0] - start[0]) * n_col + stop[1] - start[1]
        bands[step] = bands[step] + value if step in bands else value
    lanes = lax.broadcasted_iota(jnp.int32, (depth, width), 1) % n_sub
    ends = 2 * PSUB
    reach = 2 * n_col
    packed = jnp.zeros((depth, width), jnp.float32)
    for b in range(n_sub):
        value = jnp.zeros((depth, width), jnp.float32)
        for step, band in bands.items():
            if 0 <= b - step < n_sub:
                value = jnp.where(lanes == b - step, band, value)
        out_ref[b] = value
        if b < ends:
            value = jnp.where(lanes < reach, value, 0.0)
            packed = packed + (pltpu.roll(value, reach * b, 1) if b else value)
    mine_ref[...] = packed
    all_ref[me] = packed
    exchange("panel", lambda other: mine_ref, all_ref, send_sem2, recv_sem2)


def trade_call(tiles, n_row, n_col):
    vectors = tiles.shape[0]
    n_sub = n_row * n_col
    depth = vectors // n_col
    width = vectors // n_row * n_sub
    f32 = jnp.float32
    whole = pl.BlockSpec(memory_space=pltpu.VMEM)
    return pl.pallas_call(
        functools.partial(trade_kernel, n_row, n_col),
        in_specs=[whole],
        out_specs=[whole, whole],
        out_shape=[jax.ShapeDtypeStruct((n_sub, depth, width), f32), jax.ShapeDtypeStruct((n_sub, depth, width), f32)],
        scratch_shapes=[
            pltpu.VMEM((n_sub, depth, width), f32),
            pltpu.VMEM((depth, width), f32),
            pltpu.VMEM((n_sub, depth, width), f32),
            pltpu.SemaphoreType.DMA((n_sub,)),
            pltpu.SemaphoreType.DMA((n_sub,)),
            pltpu.SemaphoreType.DMA((n_sub,)),
            pltpu.SemaphoreType.DMA((n_sub,)),
        ],
        compiler_params=pltpu.CompilerParams(collective_id=0, has_side_effects=True,
                                             vmem_limit_bytes=24 * 1024 * 1024),
    )(tiles)


def panel_kernel(n_row, n_col, local_ref, all_ref, out_ref, low_ref):
    n_sub, depth, width = local_ref.shape
    vectors = depth * n_col
    ends, reach = 2 * PSUB, 2 * n_col
    f32 = jnp.float32
    r = lax.axis_index("row")
    c = lax.axis_index("col")
    order = ends * vectors
    at = lax.broadcasted_iota(jnp.int32, (vectors, vectors), 1)
    col_blocks = depth // NB
    source = (at // NB % col_blocks * n_col + at // (NB * col_blocks)) * NB + at % NB
    turn = (source == lax.broadcasted_iota(jnp.int32, (vectors, vectors), 0)).astype(f32)
    high = reach // ends
    by_column = []
    for column in range(n_col):
        tiles = [all_ref[row * n_col + column] for row in range(n_row)]
        bits = [(bit, ends * bit) for bit in powers(n_row)]
        by_column.append(swap_bits(tiles, bits))
    halves = []
    for h in range(high):
        parts = []
        for b in range(ends):
            parts.append(exact_dot(turn, jnp.concatenate([by_column[column][b * high + h] for column in range(n_col)], axis=0)))
        halves.append(jnp.concatenate(parts, axis=0))
    tall = 8
    count = order // tall
    work = [[halves[h][t * tall : t * tall + tall] for t in range(count)] for h in range(high)]
    for k in range(order):
        t, s = divmod(k, tall)
        b, q = divmod(k, vectors)
        tr, row, u = q // (NB * n_row), q // NB % n_row, q % NB
        lane = (tr * NB + u) * n_sub + row * ends + b
        rows = [work[h][t][s : s + 1] for h in range(high)]
        pivot = rows[0][:, lane : lane + 1]
        scale = lax.rsqrt(pivot)
        scaled = [x * scale for x in rows]
        for h in range(high):
            low_ref[k : k + 1, h * width : h * width + width] = scaled[h]
        for i in range(t, count):
            weight = work[0][i][:, lane : lane + 1] * scale
            for h in range(high):
                work[h][i] = work[h][i] - weight * scaled[h]
    shape = (order, high * width)
    lane = lax.broadcasted_iota(jnp.int32, shape, 1)
    inner = lane % width
    a = lane // width * ends + inner % ends
    p = (inner // (NB * n_sub) * n_row + inner % n_sub // ends) * NB + inner // n_sub % NB
    keep = a * vectors + p >= lax.broadcasted_iota(jnp.int32, shape, 0)
    low = jnp.where(keep, low_ref[...], 0.0)

    shape = (high * width, width)
    lane = lax.broadcasted_iota(jnp.int32, shape, 0)
    goal = lax.broadcasted_iota(jnp.int32, shape, 1)
    inner = lane % width
    a = lane // width * ends + inner % ends
    mine = (inner % n_sub // ends == r) & (inner // n_sub == goal // n_sub) & (a == goal % n_sub)
    rows_mine = exact_dot(low, mine.astype(f32))
    shape = (ends * depth, order)
    goal = lax.broadcasted_iota(jnp.int32, shape, 0)
    lane = lax.broadcasted_iota(jnp.int32, shape, 1)
    b, inner = goal // depth, goal % depth
    q = (inner // NB * n_col + c) * NB + inner % NB
    pick = (lane == b * vectors + q).astype(f32)
    panel = exact_dot(pick, rows_mine)
    for b in range(ends):
        out_ref[b] = panel[b * depth : b * depth + depth]
    lanes = lax.broadcasted_iota(jnp.int32, (depth, width), 1) % n_sub
    for h in range(1, high):
        shape = (ends * depth, width)
        goal = lax.broadcasted_iota(jnp.int32, shape, 0)
        lane = lax.broadcasted_iota(jnp.int32, shape, 1)
        b, inner = goal // depth, goal % depth
        q = (inner // NB * n_col + c) * NB + inner % NB
        place = (q // (NB * n_row) * NB + q % NB) * n_sub + q // NB % n_row * ends + b
        pick = (lane == place).astype(f32)
        chosen = exact_dot(pick, low[:, h * width : h * width + width], (((1,), (1,)), ((), ())))
        change = exact_dot(chosen, rows_mine)
        for b in range(ends):
            value = local_ref[h * ends + b] - change[b * depth : b * depth + depth]
            out_ref[h * ends + b] = jnp.where(lanes < ends, 0.0, value)
    for b in range(reach, n_sub):
        out_ref[b] = jnp.where(lanes < ends, 0.0, local_ref[b])


def panel_call(local, gathered, n_row, n_col):
    n_sub, depth, width = local.shape
    vectors = depth * n_col
    whole = pl.BlockSpec(memory_space=pltpu.VMEM)
    return pl.pallas_call(
        functools.partial(panel_kernel, n_row, n_col),
        in_specs=[whole, whole],
        out_specs=whole,
        out_shape=jax.ShapeDtypeStruct(local.shape, jnp.float32),
        scratch_shapes=[pltpu.VMEM((2 * PSUB * vectors, 2 * n_col // (2 * PSUB) * width), jnp.float32)],
        compiler_params=pltpu.CompilerParams(vmem_limit_bytes=24 * 1024 * 1024),
    )(local, gathered)


def body(own, labels, mobility):
    n_row = lax.axis_size("row")
    n_col = lax.axis_size("col")
    n_sub = n_row * n_col
    vectors = own.shape[0]
    acc, rim, frim, edge, rootx, rooty = gram_call(own, labels, mobility)

    def up(values, axis, count):
        return lax.ppermute(values, axis, [(i, i + 1) for i in range(count - 1)])

    def down(values, axis, count):
        return lax.ppermute(values, axis, [(i + 1, i) for i in range(count - 1)])

    tiles = tile_call(
        acc, frim, edge, rootx, rooty,
        up(rim[:, 1], "row", n_row), down(rim[:, 0], "row", n_row),
        up(edge, "col", n_col), down(edge, "col", n_col), n_col,
    )
    local, gathered = trade_call(tiles, n_row, n_col)
    local = panel_call(local, gathered, n_row, n_col)
    return local.reshape(
        n_sub, vectors // (NB * n_col), 1, NB, vectors // (NB * n_row), 1, NB, n_sub
    )


def solution(mesh):
    return jax.shard_map(
        body,
        mesh=mesh,
        in_specs=(P(None, None, "row", "col"), P(None, "row", "col"), P()),
        out_specs=P(None, None, "col", None, None, "row", None, None),
        check_vma=False,
    )
```

```python
import functools

import jax
import jax.numpy as jnp
from jax import lax
from jax.experimental import pallas as pl
from jax.experimental.pallas import tpu as pltpu
from jax.sharding import PartitionSpec as P

NB = 2
PSUB = 2
SLOTS = 21
MESH = pl.DeviceIdType.MESH
PLAIN = (((1,), (0,)), ((), ()))


FACES = ((-1, 0), (1, 0), (0, -1), (0, 1))


def slot_offsets():
    offsets = [((0, 0), (0, 0))]
    for face in FACES:
        offsets += [((0, 0), face), (face, (0, 0)), (face, face)]
    for face_x in FACES[:2]:
        for face_y in FACES[2:]:
            offsets += [(face_x, face_y), (face_y, face_x)]
    return offsets


def exact_dot(left, right, dims=PLAIN):
    return lax.dot_general(left, right, dims, precision=lax.Precision.HIGHEST, preferred_element_type=jnp.float32)


def swap_bits(tiles, bits):
    lanes = lax.broadcasted_iota(jnp.int32, tiles[0].shape, 1)
    width = tiles[0].shape[1]
    for index, lane in bits:
        low = lanes // lane % 2 == 0
        out = list(tiles)
        for i in range(len(tiles)):
            if i // index % 2 == 0:
                a, b = tiles[i], tiles[i + index]
                out[i] = jnp.where(low, a, pltpu.roll(b, lane, 1))
                out[i + index] = jnp.where(low, pltpu.roll(a, width - lane, 1), b)
        tiles = out
    return tiles


def powers(count):
    return [1 << i for i in range(count.bit_length() - 1)]


def trade(n_row, n_col, tile_ref, out_ref, all_ref, send_ref, mine_ref, here_ref,
          send_sem, recv_sem, send_sem2, recv_sem2):
    vectors = tile_ref.shape[0]
    n_sub = n_row * n_col
    col_blocks = vectors // (NB * n_col)
    width = n_col * vectors
    depth = col_blocks * NB
    r = lax.axis_index("row")
    c = lax.axis_index("col")
    me = r * n_col + c

    def peer(k):
        other = lax.rem(me + k, n_sub)
        return other, (other // n_col, lax.rem(other, n_col))

    at = lax.broadcasted_iota(jnp.int32, (vectors, vectors), 0)
    source = (at // NB % col_blocks * n_col + at // (NB * col_blocks)) * NB + at % NB
    turn = (source == lax.broadcasted_iota(jnp.int32, (vectors, vectors), 1)).astype(jnp.float32)
    ordered = exact_dot(turn, tile_ref[...])
    packs = tile_ref.shape[1] // width
    blank = jnp.zeros((depth, width), jnp.float32)
    for column in range(n_col):
        some = slice(column * depth, column * depth + depth)
        tiles = [ordered[some, k * width : k * width + width] if k < packs else blank for k in range(n_row)]
        tiles = swap_bits(tiles, [(bit, NB * bit) for bit in powers(n_row)])
        for row in range(n_row):
            send_ref[row * n_col + column] = tiles[row]

    def exchange(kind, source_of, target_ref, sends, recvs):
        def copy(k):
            other, where = peer(k)
            return pltpu.make_async_remote_copy(
                src_ref=source_of(other), dst_ref=target_ref.at[me], send_sem=sends.at[other], recv_sem=recvs.at[me],
                device_id=where, device_id_type=MESH)

        def begin(k, carry):
            copy(k).start()
            return carry

        lax.fori_loop(1, n_sub, begin, 0)

        def finish(k, carry):
            other, where = peer(k)
            pltpu.make_async_remote_copy(
                src_ref=source_of(other), dst_ref=target_ref.at[other], send_sem=sends.at[other],
                recv_sem=recvs.at[other], device_id=where, device_id_type=MESH).wait_recv()
            return carry

        lax.fori_loop(1, n_sub, finish, 0)

        def drain(k, carry):
            copy(k).wait_send()
            return carry

        lax.fori_loop(1, n_sub, drain, 0)

    here_ref[me] = send_ref[me]
    exchange("tiles", lambda other: send_ref.at[other], here_ref, send_sem, recv_sem)

    tiles = [here_ref[s] for s in range(n_sub)]
    quads = n_sub // n_row
    bits = [(bit, NB * bit) for bit in powers(n_row)]
    bits += [(n_row * bit, vectors * bit) for bit in powers(quads)]
    tiles = swap_bits(tiles, bits)
    offsets = slot_offsets()
    stack = jnp.concatenate([tiles[slot % quads * n_row + slot // quads] for slot in range(SLOTS)], axis=0)
    into = lax.broadcasted_iota(jnp.int32, (width, width), 1)
    sub, tru = into % n_sub, into // n_sub
    origin = sub // n_row * vectors + (tru // NB * n_row + sub % n_row) * NB + tru % NB
    order = (origin == lax.broadcasted_iota(jnp.int32, (width, width), 0)).astype(jnp.float32)
    stack = exact_dot(stack, order)
    bands = {}
    for slot, (start, stop) in enumerate(offsets):
        value = stack[slot * depth : slot * depth + depth]
        shift = start[0] * n_col + start[1]
        if shift:
            value = pltpu.roll(value, shift % width, 1)
        step = (stop[0] - start[0]) * n_col + stop[1] - start[1]
        bands[step] = bands[step] + value if step in bands else value
    lanes = lax.broadcasted_iota(jnp.int32, (depth, width), 1) % n_sub
    ends = 2 * PSUB
    reach = 2 * n_col
    packed = jnp.zeros((depth, width), jnp.float32)
    for b in range(n_sub):
        value = jnp.zeros((depth, width), jnp.float32)
        for step, band in bands.items():
            if 0 <= b - step < n_sub:
                value = jnp.where(lanes == b - step, band, value)
        out_ref[b] = value
        if b < ends:
            value = jnp.where(lanes < reach, value, 0.0)
            packed = packed + (pltpu.roll(value, reach * b, 1) if b else value)
    mine_ref[...] = packed
    all_ref[me] = packed
    exchange("panel", lambda other: mine_ref, all_ref, send_sem2, recv_sem2)


def panel_kernel(n_row, n_col, local_ref, all_ref, out_ref, low_ref):
    n_sub, depth, width = local_ref.shape
    vectors = depth * n_col
    ends, reach = 2 * PSUB, 2 * n_col
    f32 = jnp.float32
    r = lax.axis_index("row")
    c = lax.axis_index("col")
    order = ends * vectors
    at = lax.broadcasted_iota(jnp.int32, (vectors, vectors), 1)
    col_blocks = depth // NB
    source = (at // NB % col_blocks * n_col + at // (NB * col_blocks)) * NB + at % NB
    turn = (source == lax.broadcasted_iota(jnp.int32, (vectors, vectors), 0)).astype(f32)
    high = reach // ends
    by_column = []
    for column in range(n_col):
        tiles = [all_ref[row * n_col + column] for row in range(n_row)]
        bits = [(bit, ends * bit) for bit in powers(n_row)]
        by_column.append(swap_bits(tiles, bits))
    halves = []
    for h in range(high):
        parts = []
        for b in range(ends):
            parts.append(exact_dot(turn, jnp.concatenate([by_column[column][b * high + h] for column in range(n_col)], axis=0)))
        halves.append(jnp.concatenate(parts, axis=0))
    tall = 8
    count = order // tall
    work = [[halves[h][t * tall : t * tall + tall] for t in range(count)] for h in range(high)]
    for k in range(order):
        t, s = divmod(k, tall)
        b, q = divmod(k, vectors)
        tr, row, u = q // (NB * n_row), q // NB % n_row, q % NB
        lane = (tr * NB + u) * n_sub + row * ends + b
        rows = [work[h][t][s : s + 1] for h in range(high)]
        pivot = rows[0][:, lane : lane + 1]
        scale = lax.rsqrt(pivot)
        scaled = [x * scale for x in rows]
        for h in range(high):
            low_ref[k : k + 1, h * width : h * width + width] = scaled[h]
        for i in range(t, count):
            weight = work[0][i][:, lane : lane + 1] * scale
            for h in range(high):
                work[h][i] = work[h][i] - weight * scaled[h]
    shape = (order, high * width)
    lane = lax.broadcasted_iota(jnp.int32, shape, 1)
    inner = lane % width
    a = lane // width * ends + inner % ends
    p = (inner // (NB * n_sub) * n_row + inner % n_sub // ends) * NB + inner // n_sub % NB
    keep = a * vectors + p >= lax.broadcasted_iota(jnp.int32, shape, 0)
    low = jnp.where(keep, low_ref[...], 0.0)

    shape = (high * width, width)
    lane = lax.broadcasted_iota(jnp.int32, shape, 0)
    goal = lax.broadcasted_iota(jnp.int32, shape, 1)
    inner = lane % width
    a = lane // width * ends + inner % ends
    mine = (inner % n_sub // ends == r) & (inner // n_sub == goal // n_sub) & (a == goal % n_sub)
    rows_mine = exact_dot(low, mine.astype(f32))
    shape = (ends * depth, order)
    goal = lax.broadcasted_iota(jnp.int32, shape, 0)
    lane = lax.broadcasted_iota(jnp.int32, shape, 1)
    b, inner = goal // depth, goal % depth
    q = (inner // NB * n_col + c) * NB + inner % NB
    pick = (lane == b * vectors + q).astype(f32)
    panel = exact_dot(pick, rows_mine)
    for b in range(ends):
        out_ref[b] = panel[b * depth : b * depth + depth]
    lanes = lax.broadcasted_iota(jnp.int32, (depth, width), 1) % n_sub
    for h in range(1, high):
        shape = (ends * depth, width)
        goal = lax.broadcasted_iota(jnp.int32, shape, 0)
        lane = lax.broadcasted_iota(jnp.int32, shape, 1)
        b, inner = goal // depth, goal % depth
        q = (inner // NB * n_col + c) * NB + inner % NB
        place = (q // (NB * n_row) * NB + q % NB) * n_sub + q // NB % n_row * ends + b
        pick = (lane == place).astype(f32)
        chosen = exact_dot(pick, low[:, h * width : h * width + width], (((1,), (1,)), ((), ())))
        change = exact_dot(chosen, rows_mine)
        for b in range(ends):
            value = local_ref[h * ends + b] - change[b * depth : b * depth + depth]
            out_ref[h * ends + b] = jnp.where(lanes < ends, 0.0, value)
    for b in range(reach, n_sub):
        out_ref[b] = jnp.where(lanes < ends, 0.0, local_ref[b])


def panel_call(local, gathered, n_row, n_col):
    n_sub, depth, width = local.shape
    vectors = depth * n_col
    whole = pl.BlockSpec(memory_space=pltpu.VMEM)
    return pl.pallas_call(
        functools.partial(panel_kernel, n_row, n_col),
        in_specs=[whole, whole],
        out_specs=whole,
        out_shape=jax.ShapeDtypeStruct(local.shape, jnp.float32),
        scratch_shapes=[pltpu.VMEM((2 * PSUB * vectors, 2 * n_col // (2 * PSUB) * width), jnp.float32)],
        compiler_params=pltpu.CompilerParams(vmem_limit_bytes=24 * 1024 * 1024),
    )(local, gathered)


ROWS = 8
GROUP = 8
SPOTS = 4
CHUNK = 4
MINOR = (((1,), (1,)), ((), ()))


def slice_step(g, n_z, fresh, mob_ref, own_ref, lab_ref, acc_ref, rims_ref, frims_ref, side_ref, rootx_ref, rooty_ref,
               plain_ref, part_ref, rows_ref, root_ref, lines_ref):
    vectors, n_x, n_y = part_ref.shape
    blocks = n_x // ROWS
    groups = vectors // GROUP
    per = blocks // groups
    lanes = lax.broadcasted_iota(jnp.int32, (n_x, n_y), 1)
    now = lax.rem(g, 2)
    old = 1 - now

    def gram(slot, j):
        both = rows_ref[slot, j]
        acc_ref[...] += lax.dot_general(both, both, MINOR, preferred_element_type=jnp.float32)

    def trip(j, carry):
        root = root_ref[old]
        spot = pl.multiple_of(j * GROUP * ROWS, GROUP * ROWS)
        line = pl.multiple_of(j * GROUP, GROUP)
        ok = (lanes < SPOTS * g + SPOTS) & (lanes >= SPOTS * g)
        fluxes, olds = [], []
        for i in range(GROUP):
            v = j * GROUP + i
            before = plain_ref[old, v, ROWS : ROWS + n_x]
            total = part_ref[v]
            if fresh:
                own = own_ref[v, 0].astype(jnp.float32)
                plain_ref[now, v, ROWS : ROWS + n_x] = own
                total = total + own
                near = plain_ref[now, v, ROWS + 1 : ROWS + 1 + n_x] + plain_ref[now, v, ROWS - 1 : ROWS - 1 + n_x]
                near = near + jnp.where(lanes == n_y - 1, 0.0, pltpu.roll(own, n_y - 1, 1))
                near = near + jnp.where(lanes == 0, 0.0, pltpu.roll(own, 1, 1))
                near = near + before
                part_ref[v] = near - 6.0 * own
                turned = pltpu.roll(own, SPOTS * g + 2, 1)
                side_ref[v] = jnp.where(ok, turned, side_ref[v])
                lines_ref[0, pl.ds(line + i, 1)] = own[:1]
                lines_ref[1, pl.ds(line + i, 1)] = own[n_x - 1 :]
            flux = total * root
            lines_ref[2, pl.ds(line + i, 1)] = flux[:1]
            lines_ref[3, pl.ds(line + i, 1)] = flux[n_x - 1 :]
            fluxes.append(flux)
            olds.append(before)
            if i % 2:
                for b in range(blocks):
                    part = slice(b * ROWS, b * ROWS + ROWS)
                    where = pl.ds(spot + (i - 1) * ROWS, 2 * ROWS)
                    at = (b % per) * 2 * n_y
                    rows_ref[now, b // per, where, at : at + n_y] = jnp.concatenate(
                        [olds[i - 1][part], olds[i][part]], axis=0).astype(jnp.bfloat16)
                    rows_ref[now, b // per, where, at + n_y : at + 2 * n_y] = jnp.concatenate(
                        [fluxes[i - 1][part], fluxes[i][part]], axis=0).astype(jnp.bfloat16)
        gram(old, j)
        return carry

    lax.fori_loop(0, groups, trip, 0)
    if fresh:
        value = jnp.zeros((n_x, n_y), jnp.float32)
        for phase in range(mob_ref.shape[0]):
            value = value + jnp.where(lab_ref[0] == phase, mob_ref[phase], jnp.float32(0.0))
        root = jnp.sqrt(value)
        root_ref[now] = root
        rootx_ref[g, 0:1] = root[:1]
        rootx_ref[g, 1:2] = root[n_x - 1 :]
        ok = (lanes < SPOTS * g + SPOTS) & (lanes >= SPOTS * g)
        rooty_ref[...] = jnp.where(ok, pltpu.roll(root, SPOTS * g + 2, 1), rooty_ref[...])
        for side in range(2):
            rims_ref[side, g] = lines_ref[side].astype(jnp.bfloat16)
    else:
        for j in range(groups):
            gram(now, j)
    for side in range(2):
        frims_ref[side, jnp.maximum(g - 1, 0)] = lines_ref[2 + side].astype(jnp.bfloat16)


def pack_columns(side_ref, pack_ref):
    vectors, n_x, n_y = side_ref.shape
    quarter = n_x // SPOTS
    spot = lax.broadcasted_iota(jnp.int32, (quarter, n_y), 1) % SPOTS

    def one(v, carry):
        for to, column in enumerate((1, 2)):
            total = jnp.zeros((quarter, n_y), jnp.float32)
            for k in range(SPOTS):
                part = side_ref[v, k * quarter : k * quarter + quarter]
                part = pltpu.roll(part, (k - column) % n_y, 1) if k != column else part
                total = jnp.where(spot == k, part, total)
            pack_ref[to, v] = total.astype(jnp.bfloat16)
        return carry

    lax.fori_loop(0, vectors, one, 0)


def x_tiles(tiles_ref, frims_ref, xhalo_ref, rootx_ref, faces_ref, ends_ref):
    _, n_z, vectors, n_y = frims_ref.shape
    thin = lax.broadcasted_iota(jnp.int32, (vectors, n_y), 1)
    for side in range(2):
        total = jnp.zeros((vectors, n_y), jnp.float32)
        for z in range(n_z):
            over = xhalo_ref[side, z].astype(jnp.float32) * rootx_ref[z, side : side + 1]
            at = slice(z * n_y, z * n_y + n_y)
            faces_ref[side, :vectors, at] = frims_ref[side, z]
            faces_ref[side, vectors:, at] = over.astype(jnp.bfloat16)
            ok = (thin >= SPOTS * z) & (thin < SPOTS * z + SPOTS)
            total = jnp.where(ok, pltpu.roll(over, (SPOTS * z + 2) % n_y, 1), total)
        ends_ref[side] = total.astype(jnp.bfloat16)
        gram = lax.dot_general(faces_ref[side], faces_ref[side], MINOR, preferred_element_type=jnp.float32)
        at = (1 + 3 * side) * vectors
        tiles_ref[:, at : at + vectors] = gram[vectors:, :vectors]
        tiles_ref[:, at + vectors : at + 2 * vectors] = gram[:vectors, vectors:]
        tiles_ref[:, at + 2 * vectors : at + 3 * vectors] = gram[vectors:, vectors:]


def fold(square, vectors):
    order = square.shape[0]
    line = lax.broadcasted_iota(jnp.int32, (order, order), 0)
    column = lax.broadcasted_iota(jnp.int32, (order, order), 1)
    pick = (lax.broadcasted_iota(jnp.int32, (order, vectors), 0) // ROWS
            == lax.broadcasted_iota(jnp.int32, (order, vectors), 1)).astype(jnp.float32)
    thick = jnp.where(line % ROWS == column % ROWS, square, 0.0).reshape(vectors, ROWS, order).sum(1)
    return exact_dot(thick, pick)


def y_tiles(tiles_ref, side_ref, rooty_ref, yhalo_ref, ends_ref, left_ref, right_ref, cut_ref):
    vectors, n_x, n_y = side_ref.shape
    order = vectors * ROWS
    blocks = n_x // ROWS
    f32, bf16 = jnp.float32, jnp.bfloat16
    rows = lax.broadcasted_iota(jnp.int32, (n_x, n_y), 0)
    lanes = lax.broadcasted_iota(jnp.int32, (n_x, n_y), 1)
    spot = lanes % SPOTS
    root = jnp.where((spot == 1) | (spot == 2), rooty_ref[...], 0.0)

    def spread(packed, column):
        return jnp.concatenate(
            [pltpu.roll(packed, (column - k) % n_y, 1) if k != column else packed for k in range(SPOTS)], axis=0)

    def pair_of(m, carry):
        kept = []
        for i in range(2):
            v = 2 * m + i
            own = side_ref[v]
            near = jnp.where(lanes < SPOTS, 0.0, pltpu.roll(own, SPOTS, 1))
            near = near + jnp.where(lanes >= n_y - SPOTS, 0.0, pltpu.roll(own, n_y - SPOTS, 1))
            near = near + jnp.where(rows == 0, 0.0, pltpu.roll(own, 1, 0))
            near = near + jnp.where(rows == n_x - 1, 0.0, pltpu.roll(own, n_x - 1, 0))
            near = near + jnp.where(spot == 2, pltpu.roll(own, n_y - 1, 1), pltpu.roll(own, 1, 1))
            flux = (near - 6.0 * own) * root
            low = spread(yhalo_ref[0, v].astype(f32), 2)
            upp = spread(yhalo_ref[1, v].astype(f32), 1)
            over = jnp.where(spot == 2, low, upp) * root
            cut_ref[0, pl.ds(v, 1)] = over[:1]
            cut_ref[1, pl.ds(v, 1)] = over[n_x - 1 :]
            kept.append((flux, over, jnp.where(spot == 2, over, 0.0), jnp.where(spot == 1, over, 0.0)))
        for b in range(blocks):
            part = slice(b * ROWS, b * ROWS + ROWS)
            both = [jnp.concatenate([x[part], y[part]], axis=0).astype(bf16) for x, y in zip(*kept)]
            at = slice(b * n_y, b * n_y + n_y)
            first = pl.ds(pl.multiple_of(m * 2 * ROWS, 2 * ROWS), 2 * ROWS)
            second = pl.ds(pl.multiple_of(order + m * 2 * ROWS, 2 * ROWS), 2 * ROWS)
            left_ref[first, at] = both[0]
            left_ref[second, at] = both[1]
            right_ref[first, at] = both[2]
            right_ref[second, at] = both[3]
        return carry

    lax.fori_loop(0, vectors // 2, pair_of, 0)
    crossed = lax.dot_general(left_ref[...], right_ref[...], MINOR, preferred_element_type=f32)

    def put(slot, value):
        tiles_ref[:, slot * vectors : (slot + 1) * vectors] = value

    for side in range(2):
        here = slice(side * order, side * order + order)
        cross = fold(crossed[:order, here], vectors)
        put(7 + 3 * side, cross.T)
        put(8 + 3 * side, cross)
        put(9 + 3 * side, fold(crossed[order:, here], vectors))
    thin = lax.broadcasted_iota(jnp.int32, (vectors, n_y), 1)
    slot = 13
    for x in range(2):
        for y in range(2):
            along = jnp.where(thin % SPOTS == 2 - y, cut_ref[x], 0.0).astype(bf16)
            put(slot, lax.dot_general(along, ends_ref[x], MINOR, preferred_element_type=f32))
            put(slot + 1, lax.dot_general(ends_ref[x], along, MINOR, preferred_element_type=f32))
            slot += 2


def main_kernel(n_row, n_col, mob_ref, own_ref, lab_ref, out_ref, all_ref,
                plain_ref, part_ref, rows_ref, root_ref, lines_ref, acc_ref, rims_ref, frims_ref, side_ref,
                rootx_ref, rooty_ref, xhalo_ref, pack_ref, yhalo_ref, faces_ref, ends_ref, left_ref, right_ref, cut_ref,
                tiles_ref, message_ref, here_ref, mine_ref, panel_ref,
                xsend_sem, xrecv_sem, ysend_sem, yrecv_sem, send_sem, recv_sem, send_sem2, recv_sem2):
    g = pl.program_id(0)
    n_z = pl.num_programs(0) - 1
    vectors = part_ref.shape[0]
    n_sub = n_row * n_col
    r = lax.axis_index("row")
    c = lax.axis_index("col")
    me = r * n_col + c
    barrier = pltpu.get_barrier_semaphore()

    def peer(k):
        other = lax.rem(me + k, n_sub)
        return other, (other // n_col, lax.rem(other, n_col))

    def rim_copy(side, some):
        return pltpu.make_async_remote_copy(
            src_ref=rims_ref.at[side, some], dst_ref=xhalo_ref.at[1 - side, some],
            send_sem=xsend_sem.at[side], recv_sem=xrecv_sem.at[1 - side],
            device_id=(lax.rem(r + 2 * side - 1 + n_row, n_row), c), device_id_type=MESH)

    def column_copy(way):
        return pltpu.make_async_remote_copy(
            src_ref=pack_ref.at[way], dst_ref=yhalo_ref.at[way],
            send_sem=ysend_sem.at[way], recv_sem=yrecv_sem.at[way],
            device_id=(r, lax.rem(c + 1 - 2 * way + n_col, n_col)), device_id_type=MESH)

    x_there = (r > 0, r < n_row - 1)
    y_there = (c > 0, c < n_col - 1)

    @pl.when(g == 0)
    def _():
        def greet(k, carry):
            pl.semaphore_signal(barrier, inc=1, device_id=peer(k)[1], device_id_type=MESH)
            return carry

        lax.fori_loop(1, n_sub, greet, 0)
        for ref in (plain_ref, part_ref, rows_ref, root_ref, acc_ref, side_ref, rooty_ref):
            ref[...] = jnp.zeros_like(ref)
        tiles_ref[:, SLOTS * vectors :] = jnp.zeros((vectors, tiles_ref.shape[1] - SLOTS * vectors), jnp.float32)
        for side in range(2):
            @pl.when(jnp.logical_not(x_there[side]))
            def _():
                xhalo_ref[side] = jnp.zeros(xhalo_ref.shape[1:], jnp.bfloat16)

            @pl.when(jnp.logical_not(y_there[side]))
            def _():
                yhalo_ref[side] = jnp.zeros(yhalo_ref.shape[1:], jnp.bfloat16)

    @pl.when(g == CHUNK)
    def _():
        pl.semaphore_wait(barrier, n_sub - 1)

    @pl.when((lax.rem(g, CHUNK) == 0) & (g > 0))
    def _():
        for side in range(2):
            @pl.when(x_there[side])
            def _():
                rim_copy(side, pl.ds(g - CHUNK, CHUNK)).start()

    refs = (mob_ref, own_ref, lab_ref, acc_ref, rims_ref, frims_ref, side_ref, rootx_ref, rooty_ref,
            plain_ref, part_ref, rows_ref, root_ref, lines_ref)

    @pl.when(g < n_z)
    def _():
        slice_step(g, n_z, True, *refs)

    @pl.when(g == n_z)
    def _():
        pack_columns(side_ref, pack_ref)
        for way in range(2):
            @pl.when(y_there[1 - way])
            def _():
                column_copy(way).start()
        slice_step(g, n_z, False, *refs)
        tiles_ref[:, :vectors] = fold(acc_ref[...], vectors)
        everything = pl.ds(0, n_z)
        for side in range(2):
            @pl.when(x_there[side])
            def _():
                rim_copy(1 - side, everything).wait_recv()
        x_tiles(tiles_ref, frims_ref, xhalo_ref, rootx_ref, faces_ref, ends_ref)
        for way in range(2):
            @pl.when(y_there[way])
            def _():
                column_copy(way).wait_recv()
        y_tiles(tiles_ref, side_ref, rooty_ref, yhalo_ref, ends_ref, left_ref, right_ref, cut_ref)
        trade(n_row, n_col, tiles_ref, out_ref, panel_ref, message_ref, mine_ref, here_ref,
              send_sem, recv_sem, send_sem2, recv_sem2)
        all_ref[...] = panel_ref[...]
        for side in range(2):
            @pl.when(x_there[side])
            def _():
                rim_copy(side, everything).wait_send()
        for way in range(2):
            @pl.when(y_there[1 - way])
            def _():
                column_copy(way).wait_send()


def main_call(own, labels, mobility, n_row, n_col):
    vectors, n_z, n_x, n_y = own.shape
    n_sub = n_row * n_col
    depth = vectors // n_col
    width = vectors // n_row * n_sub
    order = vectors * ROWS
    blocks = n_x // ROWS
    groups = vectors // GROUP
    f32, bf16 = jnp.float32, jnp.bfloat16
    last = n_z - 1
    pieces = jax.ShapeDtypeStruct((n_sub, depth, width), f32)
    return pl.pallas_call(
        functools.partial(main_kernel, n_row, n_col),
        grid=(n_z + 1,),
        in_specs=[
            pl.BlockSpec(memory_space=pltpu.SMEM),
            pl.BlockSpec((vectors, 1, n_x, n_y), lambda g: (0, jnp.minimum(g, last), 0, 0)),
            pl.BlockSpec((1, n_x, n_y), lambda g: (jnp.minimum(g, last), 0, 0)),
        ],
        out_specs=[pl.BlockSpec((n_sub, depth, width), lambda g: (0, 0, 0))] * 2,
        out_shape=[pieces, pieces],
        scratch_shapes=[
            pltpu.VMEM((2, vectors, n_x + 2 * ROWS, n_y), f32),
            pltpu.VMEM((vectors, n_x, n_y), f32),
            pltpu.VMEM((2, groups, order, blocks // groups * 2 * n_y), bf16),
            pltpu.VMEM((2, n_x, n_y), f32),
            pltpu.VMEM((4, vectors, n_y), f32),
            pltpu.VMEM((order, order), f32),
            pltpu.VMEM((2, n_z, vectors, n_y), bf16),
            pltpu.VMEM((2, n_z, vectors, n_y), bf16),
            pltpu.VMEM((vectors, n_x, n_y), f32),
            pltpu.VMEM((n_z, 2, n_y), f32),
            pltpu.VMEM((n_x, n_y), f32),
            pltpu.VMEM((2, n_z, vectors, n_y), bf16),
            pltpu.VMEM((2, vectors, n_x // SPOTS, n_y), bf16),
            pltpu.VMEM((2, vectors, n_x // SPOTS, n_y), bf16),
            pltpu.VMEM((2, 2 * vectors, n_z * n_y), bf16),
            pltpu.VMEM((2, vectors, n_y), bf16),
            pltpu.VMEM((2 * order, blocks * n_y), bf16),
            pltpu.VMEM((2 * order, blocks * n_y), bf16),
            pltpu.VMEM((2, vectors, n_y), f32),
            pltpu.VMEM((vectors, -(-SLOTS // n_col) * n_col * vectors), f32),
            pltpu.VMEM((n_sub, depth, width), f32),
            pltpu.VMEM((n_sub, depth, width), f32),
            pltpu.VMEM((depth, width), f32),
            pltpu.VMEM((n_sub, depth, width), f32),
            pltpu.SemaphoreType.DMA((2,)),
            pltpu.SemaphoreType.DMA((2,)),
            pltpu.SemaphoreType.DMA((2,)),
            pltpu.SemaphoreType.DMA((2,)),
            pltpu.SemaphoreType.DMA((n_sub,)),
            pltpu.SemaphoreType.DMA((n_sub,)),
            pltpu.SemaphoreType.DMA((n_sub,)),
            pltpu.SemaphoreType.DMA((n_sub,)),
        ],
        compiler_params=pltpu.CompilerParams(
            collective_id=0, has_side_effects=True, vmem_limit_bytes=48 * 1024 * 1024),
    )(mobility, own, labels)


def body(own, labels, mobility):
    n_row = lax.axis_size("row")
    n_col = lax.axis_size("col")
    n_sub = n_row * n_col
    vectors = own.shape[0]
    local, gathered = main_call(own, labels, mobility, n_row, n_col)
    local = panel_call(local, gathered, n_row, n_col)
    return local.reshape(
        n_sub, vectors // (NB * n_col), 1, NB, vectors // (NB * n_row), 1, NB, n_sub
    )


def solution(mesh):
    return jax.shard_map(
        body,
        mesh=mesh,
        in_specs=(P(None, None, "row", "col"), P(None, "row", "col"), P()),
        out_specs=P(None, None, "col", None, None, "row", None, None),
        check_vma=False,
    )
```

```python
import functools

import jax
import jax.numpy as jnp
from jax import lax
from jax.experimental import pallas as pl
from jax.experimental.pallas import tpu as pltpu
from jax.sharding import PartitionSpec as P

NB = 2
PSUB = 2
SLOTS = 21
MESH = pl.DeviceIdType.MESH
PLAIN = (((1,), (0,)), ((), ()))


FACES = ((-1, 0), (1, 0), (0, -1), (0, 1))


def slot_offsets():
    offsets = [((0, 0), (0, 0))]
    for face in FACES:
        offsets += [((0, 0), face), (face, (0, 0)), (face, face)]
    for face_x in FACES[:2]:
        for face_y in FACES[2:]:
            offsets += [(face_x, face_y), (face_y, face_x)]
    return offsets


def exact_dot(left, right, dims=PLAIN):
    return lax.dot_general(left, right, dims, precision=lax.Precision.HIGHEST, preferred_element_type=jnp.float32)


def swap_bits(tiles, bits):
    lanes = lax.broadcasted_iota(jnp.int32, tiles[0].shape, 1)
    width = tiles[0].shape[1]
    for index, lane in bits:
        low = lanes // lane % 2 == 0
        out = list(tiles)
        for i in range(len(tiles)):
            if i // index % 2 == 0:
                a, b = tiles[i], tiles[i + index]
                out[i] = jnp.where(low, a, pltpu.roll(b, lane, 1))
                out[i + index] = jnp.where(low, pltpu.roll(a, width - lane, 1), b)
        tiles = out
    return tiles


def powers(count):
    return [1 << i for i in range(count.bit_length() - 1)]


def trade(n_row, n_col, tile_ref, out_ref, all_ref, send_ref, mine_ref, here_ref,
          send_sem, recv_sem, send_sem2, recv_sem2):
    vectors = tile_ref.shape[0]
    n_sub = n_row * n_col
    col_blocks = vectors // (NB * n_col)
    width = n_col * vectors
    depth = col_blocks * NB
    r = lax.axis_index("row")
    c = lax.axis_index("col")
    me = r * n_col + c

    def peer(k):
        other = lax.rem(me + k, n_sub)
        return other, (other // n_col, lax.rem(other, n_col))

    at = lax.broadcasted_iota(jnp.int32, (vectors, vectors), 0)
    source = (at // NB % col_blocks * n_col + at // (NB * col_blocks)) * NB + at % NB
    turn = (source == lax.broadcasted_iota(jnp.int32, (vectors, vectors), 1)).astype(jnp.float32)
    ordered = exact_dot(turn, tile_ref[...])
    packs = tile_ref.shape[1] // width
    blank = jnp.zeros((depth, width), jnp.float32)
    for column in range(n_col):
        some = slice(column * depth, column * depth + depth)
        tiles = [ordered[some, k * width : k * width + width] if k < packs else blank for k in range(n_row)]
        tiles = swap_bits(tiles, [(bit, NB * bit) for bit in powers(n_row)])
        for row in range(n_row):
            send_ref[row * n_col + column] = tiles[row]

    def exchange(kind, source_of, target_ref, sends, recvs):
        def copy(k):
            other, where = peer(k)
            return pltpu.make_async_remote_copy(
                src_ref=source_of(other), dst_ref=target_ref.at[me], send_sem=sends.at[other], recv_sem=recvs.at[me],
                device_id=where, device_id_type=MESH)

        def begin(k, carry):
            copy(k).start()
            return carry

        lax.fori_loop(1, n_sub, begin, 0)

        def finish(k, carry):
            other, where = peer(k)
            pltpu.make_async_remote_copy(
                src_ref=source_of(other), dst_ref=target_ref.at[other], send_sem=sends.at[other],
                recv_sem=recvs.at[other], device_id=where, device_id_type=MESH).wait_recv()
            return carry

        lax.fori_loop(1, n_sub, finish, 0)

        def drain(k, carry):
            copy(k).wait_send()
            return carry

        lax.fori_loop(1, n_sub, drain, 0)

    here_ref[me] = send_ref[me]
    exchange("tiles", lambda other: send_ref.at[other], here_ref, send_sem, recv_sem)

    tiles = [here_ref[s] for s in range(n_sub)]
    quads = n_sub // n_row
    bits = [(bit, NB * bit) for bit in powers(n_row)]
    bits += [(n_row * bit, vectors * bit) for bit in powers(quads)]
    tiles = swap_bits(tiles, bits)
    offsets = slot_offsets()
    stack = jnp.concatenate([tiles[slot % quads * n_row + slot // quads] for slot in range(SLOTS)], axis=0)
    into = lax.broadcasted_iota(jnp.int32, (width, width), 1)
    sub, tru = into % n_sub, into // n_sub
    origin = sub // n_row * vectors + (tru // NB * n_row + sub % n_row) * NB + tru % NB
    order = (origin == lax.broadcasted_iota(jnp.int32, (width, width), 0)).astype(jnp.float32)
    stack = exact_dot(stack, order)
    bands = {}
    for slot, (start, stop) in enumerate(offsets):
        value = stack[slot * depth : slot * depth + depth]
        shift = start[0] * n_col + start[1]
        if shift:
            value = pltpu.roll(value, shift % width, 1)
        step = (stop[0] - start[0]) * n_col + stop[1] - start[1]
        bands[step] = bands[step] + value if step in bands else value
    lanes = lax.broadcasted_iota(jnp.int32, (depth, width), 1) % n_sub
    ends = 2 * PSUB
    reach = 2 * n_col
    packed = jnp.zeros((depth, width), jnp.float32)
    for b in range(n_sub):
        value = jnp.zeros((depth, width), jnp.float32)
        for step, band in bands.items():
            if 0 <= b - step < n_sub:
                value = jnp.where(lanes == b - step, band, value)
        out_ref[b] = value
        if b < ends:
            value = jnp.where(lanes < reach, value, 0.0)
            packed = packed + (pltpu.roll(value, reach * b, 1) if b else value)
    mine_ref[...] = packed
    all_ref[me] = packed
    exchange("panel", lambda other: mine_ref, all_ref, send_sem2, recv_sem2)


def panel_kernel(n_row, n_col, local_ref, all_ref, out_ref, low_ref):
    n_sub, depth, width = local_ref.shape
    vectors = depth * n_col
    ends, reach = 2 * PSUB, 2 * n_col
    f32 = jnp.float32
    r = lax.axis_index("row")
    c = lax.axis_index("col")
    order = ends * vectors
    at = lax.broadcasted_iota(jnp.int32, (vectors, vectors), 1)
    col_blocks = depth // NB
    source = (at // NB % col_blocks * n_col + at // (NB * col_blocks)) * NB + at % NB
    turn = (source == lax.broadcasted_iota(jnp.int32, (vectors, vectors), 0)).astype(f32)
    high = reach // ends
    by_column = []
    for column in range(n_col):
        tiles = [all_ref[row * n_col + column] for row in range(n_row)]
        bits = [(bit, ends * bit) for bit in powers(n_row)]
        by_column.append(swap_bits(tiles, bits))
    halves = []
    for h in range(high):
        parts = []
        for b in range(ends):
            parts.append(exact_dot(turn, jnp.concatenate([by_column[column][b * high + h] for column in range(n_col)], axis=0)))
        halves.append(jnp.concatenate(parts, axis=0))
    tall = 8
    count = order // tall
    work = [[halves[h][t * tall : t * tall + tall] for t in range(count)] for h in range(high)]
    for k in range(order):
        t, s = divmod(k, tall)
        b, q = divmod(k, vectors)
        tr, row, u = q // (NB * n_row), q // NB % n_row, q % NB
        lane = (tr * NB + u) * n_sub + row * ends + b
        rows = [work[h][t][s : s + 1] for h in range(high)]
        pivot = rows[0][:, lane : lane + 1]
        scale = lax.rsqrt(pivot)
        scaled = [x * scale for x in rows]
        for h in range(high):
            low_ref[k : k + 1, h * width : h * width + width] = scaled[h]
        for i in range(t, count):
            weight = work[0][i][:, lane : lane + 1] * scale
            for h in range(high):
                work[h][i] = work[h][i] - weight * scaled[h]
    shape = (order, high * width)
    lane = lax.broadcasted_iota(jnp.int32, shape, 1)
    inner = lane % width
    a = lane // width * ends + inner % ends
    p = (inner // (NB * n_sub) * n_row + inner % n_sub // ends) * NB + inner // n_sub % NB
    keep = a * vectors + p >= lax.broadcasted_iota(jnp.int32, shape, 0)
    low = jnp.where(keep, low_ref[...], 0.0)

    shape = (high * width, width)
    lane = lax.broadcasted_iota(jnp.int32, shape, 0)
    goal = lax.broadcasted_iota(jnp.int32, shape, 1)
    inner = lane % width
    a = lane // width * ends + inner % ends
    mine = (inner % n_sub // ends == r) & (inner // n_sub == goal // n_sub) & (a == goal % n_sub)
    rows_mine = exact_dot(low, mine.astype(f32))
    shape = (ends * depth, order)
    goal = lax.broadcasted_iota(jnp.int32, shape, 0)
    lane = lax.broadcasted_iota(jnp.int32, shape, 1)
    b, inner = goal // depth, goal % depth
    q = (inner // NB * n_col + c) * NB + inner % NB
    pick = (lane == b * vectors + q).astype(f32)
    panel = exact_dot(pick, rows_mine)
    for b in range(ends):
        out_ref[b] = panel[b * depth : b * depth + depth]
    lanes = lax.broadcasted_iota(jnp.int32, (depth, width), 1) % n_sub
    for h in range(1, high):
        shape = (ends * depth, width)
        goal = lax.broadcasted_iota(jnp.int32, shape, 0)
        lane = lax.broadcasted_iota(jnp.int32, shape, 1)
        b, inner = goal // depth, goal % depth
        q = (inner // NB * n_col + c) * NB + inner % NB
        place = (q // (NB * n_row) * NB + q % NB) * n_sub + q // NB % n_row * ends + b
        pick = (lane == place).astype(f32)
        chosen = exact_dot(pick, low[:, h * width : h * width + width], (((1,), (1,)), ((), ())))
        change = exact_dot(chosen, rows_mine)
        for b in range(ends):
            value = local_ref[h * ends + b] - change[b * depth : b * depth + depth]
            out_ref[h * ends + b] = jnp.where(lanes < ends, 0.0, value)
    for b in range(reach, n_sub):
        out_ref[b] = jnp.where(lanes < ends, 0.0, local_ref[b])


def panel_call(local, gathered, n_row, n_col):
    n_sub, depth, width = local.shape
    vectors = depth * n_col
    whole = pl.BlockSpec(memory_space=pltpu.VMEM)
    return pl.pallas_call(
        functools.partial(panel_kernel, n_row, n_col),
        in_specs=[whole, whole],
        out_specs=whole,
        out_shape=jax.ShapeDtypeStruct(local.shape, jnp.float32),
        scratch_shapes=[pltpu.VMEM((2 * PSUB * vectors, 2 * n_col // (2 * PSUB) * width), jnp.float32)],
        compiler_params=pltpu.CompilerParams(vmem_limit_bytes=24 * 1024 * 1024),
    )(local, gathered)


ROWS = 8
SPOTS = 4
CHUNK = 4
MINOR = (((1,), (1,)), ((), ()))


def cross_weights(n_y):
    shape = (2 * n_y, 2 * n_y)
    i = lax.broadcasted_iota(jnp.int32, shape, 0)
    j = lax.broadcasted_iota(jnp.int32, shape, 1)
    gap = i % n_y - j % n_y
    same = i // n_y == j // n_y
    near = jnp.where((gap == 1) | (gap == -1), 1.0, jnp.where(gap == 0, -6.0, 0.0))
    return jnp.where(same, near, jnp.where(gap == 0, 1.0, 0.0)).astype(jnp.bfloat16)


def stencil(p, fresh, own_ref, cross_ref, mixed_ref, first_ref, now_ref, old_ref, part_ref, rows_ref, root_ref, side_ref,
            lines_ref):
    vectors, n_x, n_y = side_ref.shape
    blocks = n_x // ROWS
    inner = slice(ROWS, ROWS + n_x)
    up, down = slice(ROWS + 1, ROWS + 1 + n_x), slice(ROWS - 1, ROWS - 1 + n_x)
    if fresh:
        both = jnp.concatenate([own_ref[:, s].reshape(vectors * n_x, n_y) for s in range(2)], axis=1)
        mixed_ref[...] = lax.dot_general(both, cross_ref[...], PLAIN, preferred_element_type=jnp.float32)
        lanes = lax.broadcasted_iota(jnp.int32, (n_x, n_y), 1)
        z = 2 * p
        kept = [(lanes < SPOTS * (z + s + 1)) & (lanes >= SPOTS * (z + s)) for s in range(2)]
    for m in range(vectors // 2):
        mids, fluxes = [[], []], [[], []]
        for v in (2 * m, 2 * m + 1):
            last = old_ref[v, inner]
            total = part_ref[v]
            mids[0].append(last)
            if fresh:
                own = own_ref[v, 0].astype(jnp.float32)
                first_ref[v, inner] = own
                next_own = own_ref[v, 1].astype(jnp.float32)
                now_ref[v, inner] = next_own
                total = total + own
                mixed = mixed_ref[v * n_x : v * n_x + n_x]
                near = mixed[:, :n_y] + (first_ref[v, up] + first_ref[v, down]) + last
                part_ref[v] = mixed[:, n_y:] + (now_ref[v, up] + now_ref[v, down])
                flux = near * root_ref[1]
                for s, value in enumerate((own, next_own)):
                    lines_ref[s, 0, v : v + 1] = value[:1]
                    lines_ref[s, 1, v : v + 1] = value[n_x - 1 :]
                    turned = pltpu.roll(own_ref[v, s], lax.rem(SPOTS * (z + s) + 2, n_y), 1)
                    side_ref[v] = jnp.where(kept[s], turned, side_ref[v])
                lines_ref[3, 0, v : v + 1] = flux[:1]
                lines_ref[3, 1, v : v + 1] = flux[n_x - 1 :]
                mids[1].append(own)
                fluxes[1].append(flux)
            flux = total * root_ref[0]
            lines_ref[2, 0, v : v + 1] = flux[:1]
            lines_ref[2, 1, v : v + 1] = flux[n_x - 1 :]
            fluxes[0].append(flux)
        where = slice(2 * m * ROWS, 2 * m * ROWS + 2 * ROWS)
        for b in range(blocks):
            part = slice(b * ROWS, b * ROWS + ROWS)
            for s in range(2 if fresh else 1):
                for which, values in enumerate((mids[s], fluxes[s])):
                    rows_ref[s, b, where, which * n_y : which * n_y + n_y] = jnp.concatenate(
                        [value[part] for value in values], axis=0).astype(jnp.bfloat16)


def gram(acc_ref, rows_ref, slices):
    both = jnp.concatenate([rows_ref[s, b] for s in slices for b in range(rows_ref.shape[1])], axis=1)
    acc_ref[...] += lax.dot_general(both, both, MINOR, preferred_element_type=jnp.float32)


def roots(p, mob_ref, lab_ref, root_ref, rootx_ref, rooty_ref):
    _, n_x, n_y = root_ref.shape
    lanes = lax.broadcasted_iota(jnp.int32, (n_x, n_y), 1)
    for s in range(2):
        z = 2 * p + s
        value = jnp.zeros((n_x, n_y), jnp.float32)
        for phase in range(mob_ref.shape[0]):
            value = value + jnp.where(lab_ref[s] == phase, mob_ref[phase], jnp.float32(0.0))
        root = jnp.sqrt(value)
        root_ref[1 + s] = jnp.where((lanes == 0) | (lanes == n_y - 1), 0.0, root)
        rootx_ref[z, 0:1] = root[:1]
        rootx_ref[z, 1:2] = root[n_x - 1 :]
        ok = (lanes < SPOTS * z + SPOTS) & (lanes >= SPOTS * z)
        rooty_ref[...] = jnp.where(ok, pltpu.roll(root, lax.rem(SPOTS * z + 2, n_y), 1), rooty_ref[...])


def pack_columns(side_ref, pack_ref):
    vectors, n_x, n_y = side_ref.shape
    quarter = n_x // SPOTS
    spot = lax.broadcasted_iota(jnp.int32, (quarter, n_y), 1) % SPOTS

    def one(v, carry):
        for to, column in enumerate((1, 2)):
            total = jnp.zeros((quarter, n_y), jnp.float32)
            for k in range(SPOTS):
                part = side_ref[v, k * quarter : k * quarter + quarter].astype(jnp.float32)
                part = pltpu.roll(part, (k - column) % n_y, 1) if k != column else part
                total = jnp.where(spot == k, part, total)
            pack_ref[to, v] = total.astype(jnp.bfloat16)
        return carry

    lax.fori_loop(0, vectors, one, 0)


def x_tiles(tiles_ref, frims_ref, xhalo_ref, rootx_ref, faces_ref, ends_ref):
    _, n_z, vectors, n_y = frims_ref.shape
    thin = lax.broadcasted_iota(jnp.int32, (vectors, n_y), 1)
    for side in range(2):
        total = jnp.zeros((vectors, n_y), jnp.float32)
        for z in range(n_z):
            over = xhalo_ref[side, z].astype(jnp.float32) * rootx_ref[z, side : side + 1]
            at = slice(z * n_y, z * n_y + n_y)
            faces_ref[side, :vectors, at] = frims_ref[side, z]
            faces_ref[side, vectors:, at] = over.astype(jnp.bfloat16)
            ok = (thin >= SPOTS * z) & (thin < SPOTS * z + SPOTS)
            total = jnp.where(ok, pltpu.roll(over, (SPOTS * z + 2) % n_y, 1), total)
        ends_ref[side] = total.astype(jnp.bfloat16)
        gram = lax.dot_general(faces_ref[side], faces_ref[side], MINOR, preferred_element_type=jnp.float32)
        at = (1 + 3 * side) * vectors
        tiles_ref[:, at : at + vectors] = gram[vectors:, :vectors]
        tiles_ref[:, at + vectors : at + 2 * vectors] = gram[:vectors, vectors:]
        tiles_ref[:, at + 2 * vectors : at + 3 * vectors] = gram[vectors:, vectors:]


def fold(square, vectors):
    order = square.shape[0]
    line = lax.broadcasted_iota(jnp.int32, (order, order), 0)
    column = lax.broadcasted_iota(jnp.int32, (order, order), 1)
    pick = (lax.broadcasted_iota(jnp.int32, (order, vectors), 0) // ROWS
            == lax.broadcasted_iota(jnp.int32, (order, vectors), 1)).astype(jnp.float32)
    thick = jnp.where(line % ROWS == column % ROWS, square, 0.0).reshape(vectors, ROWS, order).sum(1)
    return exact_dot(thick, pick)


def y_tiles(tiles_ref, acc_ref, side_ref, rooty_ref, yhalo_ref, ends_ref, left_ref, right_ref, cut_ref):
    vectors, n_x, n_y = side_ref.shape
    order = vectors * ROWS
    blocks = n_x // ROWS
    f32, bf16 = jnp.float32, jnp.bfloat16
    rows = lax.broadcasted_iota(jnp.int32, (n_x, n_y), 0)
    lanes = lax.broadcasted_iota(jnp.int32, (n_x, n_y), 1)
    spot = lanes % SPOTS
    root = jnp.where((spot == 1) | (spot == 2), rooty_ref[...], 0.0)

    def spread(packed, column):
        return jnp.concatenate(
            [pltpu.roll(packed, (column - k) % n_y, 1) if k != column else packed for k in range(SPOTS)], axis=0)

    def pair_of(m, carry):
        kept = []
        for i in range(2):
            v = 2 * m + i
            own = side_ref[v].astype(f32)
            near = jnp.where(lanes < SPOTS, 0.0, pltpu.roll(own, SPOTS, 1))
            near = near + jnp.where(lanes >= n_y - SPOTS, 0.0, pltpu.roll(own, n_y - SPOTS, 1))
            near = near + jnp.where(rows == 0, 0.0, pltpu.roll(own, 1, 0))
            near = near + jnp.where(rows == n_x - 1, 0.0, pltpu.roll(own, n_x - 1, 0))
            near = near + jnp.where(spot == 2, pltpu.roll(own, n_y - 1, 1), pltpu.roll(own, 1, 1))
            flux = (near - 6.0 * own) * root
            low = spread(yhalo_ref[0, v].astype(f32), 2)
            upp = spread(yhalo_ref[1, v].astype(f32), 1)
            over = jnp.where(spot == 2, low, upp) * root
            cut_ref[0, pl.ds(v, 1)] = over[:1]
            cut_ref[1, pl.ds(v, 1)] = over[n_x - 1 :]
            cut_ref[2, pl.ds(v, 1)] = flux[:1]
            cut_ref[3, pl.ds(v, 1)] = flux[n_x - 1 :]
            kept.append((flux, over, jnp.where(spot == 2, over, 0.0), jnp.where(spot == 1, over, 0.0)))
        for b in range(blocks):
            part = slice(b * ROWS, b * ROWS + ROWS)
            both = [jnp.concatenate([x[part], y[part]], axis=0).astype(bf16) for x, y in zip(*kept)]
            at = slice(b * n_y, b * n_y + n_y)
            first = pl.ds(pl.multiple_of(m * 2 * ROWS, 2 * ROWS), 2 * ROWS)
            second = pl.ds(pl.multiple_of(order + m * 2 * ROWS, 2 * ROWS), 2 * ROWS)
            left_ref[first, at] = both[0]
            left_ref[second, at] = both[1]
            right_ref[first, at] = both[2]
            right_ref[second, at] = both[3]
        return carry

    lax.fori_loop(0, vectors // 2, pair_of, 0)
    crossed = lax.dot_general(left_ref[...], right_ref[...], MINOR, preferred_element_type=f32)
    edges = left_ref[:order]
    edges = lax.dot_general(edges, edges, MINOR, preferred_element_type=f32)

    def put(slot, value):
        tiles_ref[:, slot * vectors : (slot + 1) * vectors] = value

    put(0, fold(acc_ref[...] + edges, vectors))
    for side in range(2):
        flux = cut_ref[2 + side].astype(bf16)
        for slot, left, right in ((1 + 3 * side, ends_ref[side], flux), (2 + 3 * side, flux, ends_ref[side])):
            here = slice(slot * vectors, (slot + 1) * vectors)
            tiles_ref[:, here] = tiles_ref[:, here] + lax.dot_general(left, right, MINOR, preferred_element_type=f32)
        here = slice(side * order, side * order + order)
        cross = fold(crossed[:order, here], vectors)
        put(7 + 3 * side, cross.T)
        put(8 + 3 * side, cross)
        put(9 + 3 * side, fold(crossed[order:, here], vectors))
    thin = lax.broadcasted_iota(jnp.int32, (vectors, n_y), 1)
    slot = 13
    for x in range(2):
        for y in range(2):
            along = jnp.where(thin % SPOTS == 2 - y, cut_ref[x], 0.0).astype(bf16)
            put(slot, lax.dot_general(along, ends_ref[x], MINOR, preferred_element_type=f32))
            put(slot + 1, lax.dot_general(ends_ref[x], along, MINOR, preferred_element_type=f32))
            slot += 2


def main_kernel(n_row, n_col, mob_ref, own_ref, lab_ref, out_ref, all_ref,
                cross_ref, mixed_ref, first_ref, plain0_ref, plain1_ref, part_ref, rows0_ref, rows1_ref, root_ref, lines_ref, acc_ref, rims_ref, frims_ref, side_ref,
                rootx_ref, rooty_ref, xhalo_ref, pack_ref, yhalo_ref, faces_ref, ends_ref, left_ref, right_ref, cut_ref,
                tiles_ref, message_ref, here_ref, mine_ref, panel_ref,
                xsend_sem, xrecv_sem, ysend_sem, yrecv_sem, send_sem, recv_sem, send_sem2, recv_sem2):
    p = pl.program_id(0)
    n_z = rims_ref.shape[1]
    pairs = n_z // 2
    vectors = side_ref.shape[0]
    n_sub = n_row * n_col
    r = lax.axis_index("row")
    c = lax.axis_index("col")
    me = r * n_col + c
    barrier = pltpu.get_barrier_semaphore()

    def peer(k):
        other = lax.rem(me + k, n_sub)
        return other, (other // n_col, lax.rem(other, n_col))

    def rim_copy(side, some):
        return pltpu.make_async_remote_copy(
            src_ref=rims_ref.at[side, some], dst_ref=xhalo_ref.at[1 - side, some],
            send_sem=xsend_sem.at[side], recv_sem=xrecv_sem.at[1 - side],
            device_id=(lax.rem(r + 2 * side - 1 + n_row, n_row), c), device_id_type=MESH)

    def column_copy(way):
        return pltpu.make_async_remote_copy(
            src_ref=pack_ref.at[way], dst_ref=yhalo_ref.at[way],
            send_sem=ysend_sem.at[way], recv_sem=yrecv_sem.at[way],
            device_id=(r, lax.rem(c + 1 - 2 * way + n_col, n_col)), device_id_type=MESH)

    x_there = (r > 0, r < n_row - 1)
    y_there = (c > 0, c < n_col - 1)

    @pl.when(p == 0)
    def _():
        def greet(k, carry):
            pl.semaphore_signal(barrier, inc=1, device_id=peer(k)[1], device_id_type=MESH)
            return carry

        lax.fori_loop(1, n_sub, greet, 0)
        cross_ref[...] = cross_weights(side_ref.shape[2])
        for ref in (first_ref, plain0_ref, plain1_ref, part_ref, rows0_ref, rows1_ref, root_ref, acc_ref, side_ref, rooty_ref):
            ref[...] = jnp.zeros_like(ref)
        tiles_ref[:, SLOTS * vectors :] = jnp.zeros((vectors, tiles_ref.shape[1] - SLOTS * vectors), jnp.float32)
        for side in range(2):
            @pl.when(jnp.logical_not(x_there[side]))
            def _():
                xhalo_ref[side] = jnp.zeros(xhalo_ref.shape[1:], jnp.bfloat16)

            @pl.when(jnp.logical_not(y_there[side]))
            def _():
                yhalo_ref[side] = jnp.zeros(yhalo_ref.shape[1:], jnp.bfloat16)

    @pl.when(2 * p == CHUNK)
    def _():
        pl.semaphore_wait(barrier, n_sub - 1)

    @pl.when((lax.rem(2 * p, CHUNK) == 0) & (p > 0))
    def _():
        for side in range(2):
            @pl.when(x_there[side])
            def _():
                rim_copy(side, pl.ds(2 * p - CHUNK, CHUNK)).start()

    plains, rows = (plain0_ref, plain1_ref), (rows0_ref, rows1_ref)

    def rims(fresh):
        if fresh:
            for side in range(2):
                for s in range(2):
                    rims_ref[side, 2 * p + s] = lines_ref[s, side].astype(jnp.bfloat16)
                frims_ref[side, 2 * p] = lines_ref[3, side].astype(jnp.bfloat16)
        for side in range(2):
            frims_ref[side, jnp.maximum(2 * p - 1, 1)] = lines_ref[2, side].astype(jnp.bfloat16)

    for odd in range(2):
        @pl.when((p < pairs) & (lax.rem(p, 2) == odd))
        def _():
            roots(p, mob_ref, lab_ref, root_ref, rootx_ref, rooty_ref)
            gram(acc_ref, rows[1 - odd], (0, 1))
            stencil(p, True, own_ref, cross_ref, mixed_ref, first_ref, plains[odd], plains[1 - odd], part_ref,
                    rows[odd], root_ref, side_ref, lines_ref)
            root_ref[0] = root_ref[2]
            rims(True)

    @pl.when(p == pairs)
    def _():
        pack_columns(side_ref, pack_ref)
        for way in range(2):
            @pl.when(y_there[1 - way])
            def _():
                column_copy(way).start()
        odd = pairs % 2
        stencil(p, False, own_ref, cross_ref, mixed_ref, first_ref, plains[odd], plains[1 - odd], part_ref, rows[odd],
                root_ref, side_ref, lines_ref)
        rims(False)
        gram(acc_ref, rows[1 - odd], (0, 1))
        gram(acc_ref, rows[odd], (0,))
        everything = pl.ds(0, n_z)
        for side in range(2):
            @pl.when(x_there[side])
            def _():
                rim_copy(1 - side, everything).wait_recv()
        x_tiles(tiles_ref, frims_ref, xhalo_ref, rootx_ref, faces_ref, ends_ref)
        for way in range(2):
            @pl.when(y_there[way])
            def _():
                column_copy(way).wait_recv()
        y_tiles(tiles_ref, acc_ref, side_ref, rooty_ref, yhalo_ref, ends_ref, left_ref, right_ref, cut_ref)
        trade(n_row, n_col, tiles_ref, out_ref, panel_ref, message_ref, mine_ref, here_ref,
              send_sem, recv_sem, send_sem2, recv_sem2)
        all_ref[...] = panel_ref[...]
        for side in range(2):
            @pl.when(x_there[side])
            def _():
                rim_copy(side, everything).wait_send()
        for way in range(2):
            @pl.when(y_there[1 - way])
            def _():
                column_copy(way).wait_send()


def main_call(own, labels, mobility, n_row, n_col):
    vectors, n_z, n_x, n_y = own.shape
    n_sub = n_row * n_col
    depth = vectors // n_col
    width = vectors // n_row * n_sub
    order = vectors * ROWS
    blocks = n_x // ROWS
    f32, bf16 = jnp.float32, jnp.bfloat16
    last = n_z // 2 - 1
    pieces = jax.ShapeDtypeStruct((n_sub, depth, width), f32)
    return pl.pallas_call(
        functools.partial(main_kernel, n_row, n_col),
        grid=(n_z // 2 + 1,),
        in_specs=[
            pl.BlockSpec(memory_space=pltpu.SMEM),
            pl.BlockSpec((vectors, 2, n_x, n_y), lambda p: (0, jnp.minimum(p, last), 0, 0)),
            pl.BlockSpec((2, n_x, n_y), lambda p: (jnp.minimum(p, last), 0, 0)),
        ],
        out_specs=[pl.BlockSpec((n_sub, depth, width), lambda g: (0, 0, 0))] * 2,
        out_shape=[pieces, pieces],
        scratch_shapes=[
            pltpu.VMEM((2 * n_y, 2 * n_y), bf16),
            pltpu.VMEM((vectors * n_x, 2 * n_y), f32),
            pltpu.VMEM((vectors, n_x + 2 * ROWS, n_y), f32),
            pltpu.VMEM((vectors, n_x + 2 * ROWS, n_y), f32),
            pltpu.VMEM((vectors, n_x + 2 * ROWS, n_y), f32),
            pltpu.VMEM((vectors, n_x, n_y), f32),
            pltpu.VMEM((2, blocks, order, 2 * n_y), bf16),
            pltpu.VMEM((2, blocks, order, 2 * n_y), bf16),
            pltpu.VMEM((3, n_x, n_y), f32),
            pltpu.VMEM((4, 2, vectors, n_y), f32),
            pltpu.VMEM((order, order), f32),
            pltpu.VMEM((2, n_z, vectors, n_y), bf16),
            pltpu.VMEM((2, n_z, vectors, n_y), bf16),
            pltpu.VMEM((vectors, n_x, n_y), bf16),
            pltpu.VMEM((n_z, 2, n_y), f32),
            pltpu.VMEM((n_x, n_y), f32),
            pltpu.VMEM((2, n_z, vectors, n_y), bf16),
            pltpu.VMEM((2, vectors, n_x // SPOTS, n_y), bf16),
            pltpu.VMEM((2, vectors, n_x // SPOTS, n_y), bf16),
            pltpu.VMEM((2, 2 * vectors, n_z * n_y), bf16),
            pltpu.VMEM((2, vectors, n_y), bf16),
            pltpu.VMEM((2 * order, blocks * n_y), bf16),
            pltpu.VMEM((2 * order, blocks * n_y), bf16),
            pltpu.VMEM((4, vectors, n_y), f32),
            pltpu.VMEM((vectors, -(-SLOTS // n_col) * n_col * vectors), f32),
            pltpu.VMEM((n_sub, depth, width), f32),
            pltpu.VMEM((n_sub, depth, width), f32),
            pltpu.VMEM((depth, width), f32),
            pltpu.VMEM((n_sub, depth, width), f32),
            pltpu.SemaphoreType.DMA((2,)),
            pltpu.SemaphoreType.DMA((2,)),
            pltpu.SemaphoreType.DMA((2,)),
            pltpu.SemaphoreType.DMA((2,)),
            pltpu.SemaphoreType.DMA((n_sub,)),
            pltpu.SemaphoreType.DMA((n_sub,)),
            pltpu.SemaphoreType.DMA((n_sub,)),
            pltpu.SemaphoreType.DMA((n_sub,)),
        ],
        compiler_params=pltpu.CompilerParams(
            collective_id=0, has_side_effects=True, vmem_limit_bytes=48 * 1024 * 1024),
    )(mobility, own, labels)


def body(own, labels, mobility):
    n_row = lax.axis_size("row")
    n_col = lax.axis_size("col")
    n_sub = n_row * n_col
    vectors = own.shape[0]
    local, gathered = main_call(own, labels, mobility, n_row, n_col)
    local = panel_call(local, gathered, n_row, n_col)
    return local.reshape(
        n_sub, vectors // (NB * n_col), 1, NB, vectors // (NB * n_row), 1, NB, n_sub
    )


def solution(mesh):
    return jax.shard_map(
        body,
        mesh=mesh,
        in_specs=(P(None, None, "row", "col"), P(None, "row", "col"), P()),
        out_specs=P(None, None, "col", None, None, "row", None, None),
        check_vma=False,
    )
```

```python
import functools

import jax
import jax.numpy as jnp
from jax import lax
from jax.experimental import pallas as pl
from jax.experimental.pallas import tpu as pltpu
from jax.sharding import PartitionSpec as P

NB = 2
PSUB = 2
SLOTS = 21
MESH = pl.DeviceIdType.MESH
PLAIN = (((1,), (0,)), ((), ()))


FACES = ((-1, 0), (1, 0), (0, -1), (0, 1))


def slot_offsets():
    offsets = [((0, 0), (0, 0))]
    for face in FACES:
        offsets += [((0, 0), face), (face, (0, 0)), (face, face)]
    for face_x in FACES[:2]:
        for face_y in FACES[2:]:
            offsets += [(face_x, face_y), (face_y, face_x)]
    return offsets


def exact_dot(left, right, dims=PLAIN):
    return lax.dot_general(left, right, dims, precision=lax.Precision.HIGHEST, preferred_element_type=jnp.float32)


def swap_bits(tiles, bits):
    lanes = lax.broadcasted_iota(jnp.int32, tiles[0].shape, 1)
    width = tiles[0].shape[1]
    for index, lane in bits:
        low = lanes // lane % 2 == 0
        out = list(tiles)
        for i in range(len(tiles)):
            if i // index % 2 == 0:
                a, b = tiles[i], tiles[i + index]
                out[i] = jnp.where(low, a, pltpu.roll(b, lane, 1))
                out[i + index] = jnp.where(low, pltpu.roll(a, width - lane, 1), b)
        tiles = out
    return tiles


def powers(count):
    return [1 << i for i in range(count.bit_length() - 1)]


def trade(n_row, n_col, tile_ref, out_ref, all_ref, send_ref, mine_ref, here_ref,
          send_sem, recv_sem, send_sem2, recv_sem2):
    vectors = tile_ref.shape[0]
    n_sub = n_row * n_col
    col_blocks = vectors // (NB * n_col)
    width = n_col * vectors
    depth = col_blocks * NB
    r = lax.axis_index("row")
    c = lax.axis_index("col")
    me = r * n_col + c

    def peer(k):
        other = lax.rem(me + k, n_sub)
        return other, (other // n_col, lax.rem(other, n_col))

    at = lax.broadcasted_iota(jnp.int32, (vectors, vectors), 0)
    source = (at // NB % col_blocks * n_col + at // (NB * col_blocks)) * NB + at % NB
    turn = (source == lax.broadcasted_iota(jnp.int32, (vectors, vectors), 1)).astype(jnp.float32)
    ordered = exact_dot(turn, tile_ref[...])
    packs = tile_ref.shape[1] // width
    blank = jnp.zeros((depth, width), jnp.float32)
    for column in range(n_col):
        some = slice(column * depth, column * depth + depth)
        tiles = [ordered[some, k * width : k * width + width] if k < packs else blank for k in range(n_row)]
        tiles = swap_bits(tiles, [(bit, NB * bit) for bit in powers(n_row)])
        for row in range(n_row):
            send_ref[row * n_col + column] = tiles[row]

    def exchange(source_of, target_ref, sends, recvs, meanwhile=None):
        def copy(k):
            other, where = peer(k)
            return pltpu.make_async_remote_copy(
                src_ref=source_of(other), dst_ref=target_ref.at[me], send_sem=sends.at[other], recv_sem=recvs.at[me],
                device_id=where, device_id_type=MESH)

        def begin(k, carry):
            copy(k).start()
            return carry

        lax.fori_loop(1, n_sub, begin, 0)
        if meanwhile:
            meanwhile()

        def finish(k, carry):
            other, where = peer(k)
            pltpu.make_async_remote_copy(
                src_ref=source_of(other), dst_ref=target_ref.at[other], send_sem=sends.at[other],
                recv_sem=recvs.at[other], device_id=where, device_id_type=MESH).wait_recv()
            return carry

        lax.fori_loop(1, n_sub, finish, 0)

        def drain(k, carry):
            copy(k).wait_send()
            return carry

        lax.fori_loop(1, n_sub, drain, 0)

    here_ref[me] = send_ref[me]
    exchange(lambda other: send_ref.at[other], here_ref, send_sem, recv_sem)

    tiles = [here_ref[s] for s in range(n_sub)]
    quads = n_sub // n_row
    bits = [(bit, NB * bit) for bit in powers(n_row)]
    bits += [(n_row * bit, vectors * bit) for bit in powers(quads)]
    tiles = swap_bits(tiles, bits)
    offsets = slot_offsets()
    stack = jnp.concatenate([tiles[slot % quads * n_row + slot // quads] for slot in range(SLOTS)], axis=0)
    into = lax.broadcasted_iota(jnp.int32, (width, width), 1)
    sub, tru = into % n_sub, into // n_sub
    origin = sub // n_row * vectors + (tru // NB * n_row + sub % n_row) * NB + tru % NB
    order = (origin == lax.broadcasted_iota(jnp.int32, (width, width), 0)).astype(jnp.float32)
    stack = exact_dot(stack, order)
    bands = {}
    for slot, (start, stop) in enumerate(offsets):
        value = stack[slot * depth : slot * depth + depth]
        shift = start[0] * n_col + start[1]
        if shift:
            value = pltpu.roll(value, shift % width, 1)
        step = (stop[0] - start[0]) * n_col + stop[1] - start[1]
        bands[step] = bands[step] + value if step in bands else value
    lanes = lax.broadcasted_iota(jnp.int32, (depth, width), 1) % n_sub
    ends = 2 * PSUB
    reach = 2 * n_col
    packed = jnp.zeros((depth, width), jnp.float32)

    def place(b):
        value = jnp.zeros((depth, width), jnp.float32)
        for step, band in bands.items():
            if 0 <= b - step < n_sub:
                value = jnp.where(lanes == b - step, band, value)
        out_ref[b] = value
        return value

    for b in range(ends):
        value = jnp.where(lanes < reach, place(b), 0.0)
        packed = packed + (pltpu.roll(value, reach * b, 1) if b else value)
    mine_ref[...] = packed
    all_ref[me] = packed
    exchange(lambda other: mine_ref, all_ref, send_sem2, recv_sem2, lambda: [place(b) for b in range(ends, n_sub)])


def panels(n_row, n_col, local_ref, all_ref, out_ref, low_ref):
    n_sub, depth, width = local_ref.shape
    vectors = depth * n_col
    ends, reach = 2 * PSUB, 2 * n_col
    f32 = jnp.float32
    r = lax.axis_index("row")
    c = lax.axis_index("col")
    order = ends * vectors
    at = lax.broadcasted_iota(jnp.int32, (vectors, vectors), 1)
    col_blocks = depth // NB
    source = (at // NB % col_blocks * n_col + at // (NB * col_blocks)) * NB + at % NB
    turn = (source == lax.broadcasted_iota(jnp.int32, (vectors, vectors), 0)).astype(f32)
    high = reach // ends
    by_column = []
    for column in range(n_col):
        tiles = [all_ref[row * n_col + column] for row in range(n_row)]
        bits = [(bit, ends * bit) for bit in powers(n_row)]
        by_column.append(swap_bits(tiles, bits))
    halves = []
    for h in range(high):
        parts = []
        for b in range(ends):
            parts.append(exact_dot(turn, jnp.concatenate([by_column[column][b * high + h] for column in range(n_col)], axis=0)))
        halves.append(jnp.concatenate(parts, axis=0))
    tall = 8
    count = order // tall
    work = [[halves[h][t * tall : t * tall + tall] for t in range(count)] for h in range(high)]
    def spread(value, s):
        return jnp.broadcast_to(value[s : s + 1], (tall, width))

    def spot(k):
        b, q = divmod(k, vectors)
        tr, row, u = q // (NB * n_row), q // NB % n_row, q % NB
        return (tr * NB + u) * n_sub + row * ends + b

    def column(i, k):
        at = spot(k)
        return jnp.broadcast_to(work[0][i][:, at : at + 1], (tall, width)) * ones

    ones = jnp.where(all_ref[0] == all_ref[0], 1.0, 0.0)
    ones = jnp.concatenate([ones] * (tall // depth), axis=0)

    few = 4
    for first in range(0, order, few):
        t, base = divmod(first, tall)
        columns = [column(t, first + s) for s in range(few)]
        rows = [[spread(work[h][t], base + s) for h in range(high)] for s in range(few)]
        scaled, weights = [], {}
        for s in range(few):
            pivot = spread(columns[s], base + s)
            inverse = 1.0 / pivot
            root = lax.rsqrt(pivot)
            k = first + s
            for h in range(high):
                low_ref[k : k + 1, h * width : h * width + width] = (rows[s][h] * root)[:1]
            scaled.append([x * inverse for x in rows[s]])
            for s2 in range(s + 1, few):
                weight = spread(columns[s], base + s2) * inverse
                weights[s, s2] = weight
                rows[s2] = [y - weight * x for x, y in zip(rows[s], rows[s2])]
                columns[s2] = columns[s2] - weight * columns[s]
        done = base + few == tall
        for i in range(t + done, count):
            if i > t:
                columns = [column(i, first + s) for s in range(few)]
                for s in range(few):
                    for s2 in range(s + 1, few):
                        columns[s2] = columns[s2] - weights[s, s2] * columns[s]
            for h in range(high):
                total = columns[0] * scaled[0][h]
                for s in range(1, few):
                    total = total + columns[s] * scaled[s][h]
                work[h][i] = work[h][i] - total
    shape = (order, high * width)
    lane = lax.broadcasted_iota(jnp.int32, shape, 1)
    inner = lane % width
    a = lane // width * ends + inner % ends
    p = (inner // (NB * n_sub) * n_row + inner % n_sub // ends) * NB + inner // n_sub % NB
    keep = a * vectors + p >= lax.broadcasted_iota(jnp.int32, shape, 0)
    low = jnp.where(keep, low_ref[...], 0.0)

    shape = (high * width, width)
    lane = lax.broadcasted_iota(jnp.int32, shape, 0)
    goal = lax.broadcasted_iota(jnp.int32, shape, 1)
    inner = lane % width
    a = lane // width * ends + inner % ends
    mine = (inner % n_sub // ends == r) & (inner // n_sub == goal // n_sub) & (a == goal % n_sub)
    rows_mine = exact_dot(low, mine.astype(f32))
    shape = (ends * depth, order)
    goal = lax.broadcasted_iota(jnp.int32, shape, 0)
    lane = lax.broadcasted_iota(jnp.int32, shape, 1)
    b, inner = goal // depth, goal % depth
    q = (inner // NB * n_col + c) * NB + inner % NB
    pick = (lane == b * vectors + q).astype(f32)
    panel = exact_dot(pick, rows_mine)
    for b in range(ends):
        out_ref[b] = panel[b * depth : b * depth + depth]
    lanes = lax.broadcasted_iota(jnp.int32, (depth, width), 1) % n_sub
    for h in range(1, high):
        shape = (ends * depth, width)
        goal = lax.broadcasted_iota(jnp.int32, shape, 0)
        lane = lax.broadcasted_iota(jnp.int32, shape, 1)
        b, inner = goal // depth, goal % depth
        q = (inner // NB * n_col + c) * NB + inner % NB
        place = (q // (NB * n_row) * NB + q % NB) * n_sub + q // NB % n_row * ends + b
        pick = (lane == place).astype(f32)
        chosen = exact_dot(pick, low[:, h * width : h * width + width], (((1,), (1,)), ((), ())))
        change = exact_dot(chosen, rows_mine)
        for b in range(ends):
            value = local_ref[h * ends + b] - change[b * depth : b * depth + depth]
            out_ref[h * ends + b] = jnp.where(lanes < ends, 0.0, value)
    for b in range(reach, n_sub):
        out_ref[b] = jnp.where(lanes < ends, 0.0, local_ref[b])


ROWS = 8
SPOTS = 4
CHUNK = 4
MINOR = (((1,), (1,)), ((), ()))


def cross_weights(n_y):
    shape = (2 * n_y, 2 * n_y)
    i = lax.broadcasted_iota(jnp.int32, shape, 0)
    j = lax.broadcasted_iota(jnp.int32, shape, 1)
    gap = i % n_y - j % n_y
    same = i // n_y == j // n_y
    near = jnp.where((gap == 1) | (gap == -1), 1.0, jnp.where(gap == 0, -6.0, 0.0))
    return jnp.where(same, near, jnp.where(gap == 0, 1.0, 0.0)).astype(jnp.bfloat16)


def stencil(p, fresh, own_ref, cross_ref, mixed_ref, first_ref, now_ref, old_ref, part_ref, rows_ref, root_ref, side_ref,
            lines_ref):
    vectors, n_x, n_y = side_ref.shape
    blocks = n_x // ROWS
    inner = slice(ROWS, ROWS + n_x)
    up, down = slice(ROWS + 1, ROWS + 1 + n_x), slice(ROWS - 1, ROWS - 1 + n_x)
    if fresh:
        both = jnp.concatenate([own_ref[:, s].reshape(vectors * n_x, n_y) for s in range(2)], axis=1)
        mixed_ref[...] = lax.dot_general(both, cross_ref[...], PLAIN, preferred_element_type=jnp.float32)
        lanes = lax.broadcasted_iota(jnp.int32, (n_x, n_y), 1)
        z = 2 * p
        kept = [(lanes < SPOTS * (z + s + 1)) & (lanes >= SPOTS * (z + s)) for s in range(2)]
    for m in range(vectors // 2):
        mids, fluxes = [[], []], [[], []]
        for v in (2 * m, 2 * m + 1):
            last = old_ref[v, inner]
            total = part_ref[v]
            mids[0].append(last)
            if fresh:
                own = own_ref[v, 0].astype(jnp.float32)
                first_ref[v, inner] = own
                next_own = own_ref[v, 1].astype(jnp.float32)
                now_ref[v, inner] = next_own
                total = total + own
                mixed = mixed_ref[v * n_x : v * n_x + n_x]
                near = mixed[:, :n_y] + (first_ref[v, up] + first_ref[v, down]) + last
                part_ref[v] = mixed[:, n_y:] + (now_ref[v, up] + now_ref[v, down])
                flux = near * root_ref[1]
                for s, value in enumerate((own, next_own)):
                    lines_ref[s, 0, v : v + 1] = value[:1]
                    lines_ref[s, 1, v : v + 1] = value[n_x - 1 :]
                    turned = pltpu.roll(own_ref[v, s], lax.rem(SPOTS * (z + s) + 2, n_y), 1)
                    side_ref[v] = jnp.where(kept[s], turned, side_ref[v])
                lines_ref[3, 0, v : v + 1] = flux[:1]
                lines_ref[3, 1, v : v + 1] = flux[n_x - 1 :]
                mids[1].append(own)
                fluxes[1].append(flux)
            flux = total * root_ref[0]
            lines_ref[2, 0, v : v + 1] = flux[:1]
            lines_ref[2, 1, v : v + 1] = flux[n_x - 1 :]
            fluxes[0].append(flux)
        where = slice(2 * m * ROWS, 2 * m * ROWS + 2 * ROWS)
        for b in range(blocks):
            part = slice(b * ROWS, b * ROWS + ROWS)
            for s in range(2 if fresh else 1):
                for which, values in enumerate((mids[s], fluxes[s])):
                    rows_ref[s, b, where, which * n_y : which * n_y + n_y] = jnp.concatenate(
                        [value[part] for value in values], axis=0).astype(jnp.bfloat16)


def gram(acc_ref, rows_ref, slices):
    both = jnp.concatenate([rows_ref[s, b] for s in slices for b in range(rows_ref.shape[1])], axis=1)
    acc_ref[...] += lax.dot_general(both, both, MINOR, preferred_element_type=jnp.float32)


def roots(p, mob_ref, lab_ref, root_ref, rootx_ref, rooty_ref):
    _, n_x, n_y = root_ref.shape
    lanes = lax.broadcasted_iota(jnp.int32, (n_x, n_y), 1)
    for s in range(2):
        z = 2 * p + s
        value = jnp.zeros((n_x, n_y), jnp.float32)
        for phase in range(mob_ref.shape[0]):
            value = value + jnp.where(lab_ref[s] == phase, mob_ref[phase], jnp.float32(0.0))
        root = jnp.sqrt(value)
        root_ref[1 + s] = jnp.where((lanes == 0) | (lanes == n_y - 1), 0.0, root)
        rootx_ref[z, 0:1] = root[:1]
        rootx_ref[z, 1:2] = root[n_x - 1 :]
        ok = (lanes < SPOTS * z + SPOTS) & (lanes >= SPOTS * z)
        rooty_ref[...] = jnp.where(ok, pltpu.roll(root, lax.rem(SPOTS * z + 2, n_y), 1), rooty_ref[...])


def pack_columns(side_ref, pack_ref):
    vectors, n_x, n_y = side_ref.shape
    quarter = n_x // SPOTS
    spot = lax.broadcasted_iota(jnp.int32, (quarter, n_y), 1) % SPOTS

    def one(v, carry):
        for to, column in enumerate((1, 2)):
            total = jnp.zeros((quarter, n_y), jnp.float32)
            for k in range(SPOTS):
                part = side_ref[v, k * quarter : k * quarter + quarter].astype(jnp.float32)
                part = pltpu.roll(part, (k - column) % n_y, 1) if k != column else part
                total = jnp.where(spot == k, part, total)
            pack_ref[to, v] = total.astype(jnp.bfloat16)
        return carry

    lax.fori_loop(0, vectors, one, 0)


def x_tiles(tiles_ref, frims_ref, xhalo_ref, rootx_ref, faces_ref, ends_ref):
    _, n_z, vectors, n_y = frims_ref.shape
    thin = lax.broadcasted_iota(jnp.int32, (vectors, n_y), 1)
    for side in range(2):
        total = jnp.zeros((vectors, n_y), jnp.float32)
        for z in range(n_z):
            over = xhalo_ref[side, z].astype(jnp.float32) * rootx_ref[z, side : side + 1]
            at = slice(z * n_y, z * n_y + n_y)
            faces_ref[side, :vectors, at] = frims_ref[side, z]
            faces_ref[side, vectors:, at] = over.astype(jnp.bfloat16)
            ok = (thin >= SPOTS * z) & (thin < SPOTS * z + SPOTS)
            total = jnp.where(ok, pltpu.roll(over, (SPOTS * z + 2) % n_y, 1), total)
        ends_ref[side] = total.astype(jnp.bfloat16)
        gram = lax.dot_general(faces_ref[side], faces_ref[side], MINOR, preferred_element_type=jnp.float32)
        at = (1 + 3 * side) * vectors
        tiles_ref[:, at : at + vectors] = gram[vectors:, :vectors]
        tiles_ref[:, at + vectors : at + 2 * vectors] = gram[:vectors, vectors:]
        tiles_ref[:, at + 2 * vectors : at + 3 * vectors] = gram[vectors:, vectors:]


def fold(square, vectors):
    order = square.shape[0]
    line = lax.broadcasted_iota(jnp.int32, (order, order), 0)
    column = lax.broadcasted_iota(jnp.int32, (order, order), 1)
    pick = (lax.broadcasted_iota(jnp.int32, (order, vectors), 0) // ROWS
            == lax.broadcasted_iota(jnp.int32, (order, vectors), 1)).astype(jnp.float32)
    thick = jnp.where(line % ROWS == column % ROWS, square, 0.0).reshape(vectors, ROWS, order).sum(1)
    return exact_dot(thick, pick)


def y_tiles(tiles_ref, acc_ref, side_ref, rooty_ref, yhalo_ref, ends_ref, left_ref, right_ref, cut_ref):
    vectors, n_x, n_y = side_ref.shape
    order = vectors * ROWS
    blocks = n_x // ROWS
    f32, bf16 = jnp.float32, jnp.bfloat16
    rows = lax.broadcasted_iota(jnp.int32, (n_x, n_y), 0)
    lanes = lax.broadcasted_iota(jnp.int32, (n_x, n_y), 1)
    spot = lanes % SPOTS
    root = jnp.where((spot == 1) | (spot == 2), rooty_ref[...], 0.0)

    def spread(packed, column):
        return jnp.concatenate(
            [pltpu.roll(packed, (column - k) % n_y, 1) if k != column else packed for k in range(SPOTS)], axis=0)

    def pair_of(m, carry):
        kept = []
        for i in range(2):
            v = 2 * m + i
            own = side_ref[v].astype(f32)
            near = jnp.where(lanes < SPOTS, 0.0, pltpu.roll(own, SPOTS, 1))
            near = near + jnp.where(lanes >= n_y - SPOTS, 0.0, pltpu.roll(own, n_y - SPOTS, 1))
            near = near + jnp.where(rows == 0, 0.0, pltpu.roll(own, 1, 0))
            near = near + jnp.where(rows == n_x - 1, 0.0, pltpu.roll(own, n_x - 1, 0))
            near = near + jnp.where(spot == 2, pltpu.roll(own, n_y - 1, 1), pltpu.roll(own, 1, 1))
            flux = (near - 6.0 * own) * root
            low = spread(yhalo_ref[0, v].astype(f32), 2)
            upp = spread(yhalo_ref[1, v].astype(f32), 1)
            over = jnp.where(spot == 2, low, upp) * root
            cut_ref[0, pl.ds(v, 1)] = over[:1]
            cut_ref[1, pl.ds(v, 1)] = over[n_x - 1 :]
            cut_ref[2, pl.ds(v, 1)] = flux[:1]
            cut_ref[3, pl.ds(v, 1)] = flux[n_x - 1 :]
            kept.append((flux, over, jnp.where(spot == 2, over, 0.0), jnp.where(spot == 1, over, 0.0)))
        for b in range(blocks):
            part = slice(b * ROWS, b * ROWS + ROWS)
            both = [jnp.concatenate([x[part], y[part]], axis=0).astype(bf16) for x, y in zip(*kept)]
            at = slice(b * n_y, b * n_y + n_y)
            first = pl.ds(pl.multiple_of(m * 2 * ROWS, 2 * ROWS), 2 * ROWS)
            second = pl.ds(pl.multiple_of(order + m * 2 * ROWS, 2 * ROWS), 2 * ROWS)
            left_ref[first, at] = both[0]
            left_ref[second, at] = both[1]
            right_ref[first, at] = both[2]
            right_ref[second, at] = both[3]
        return carry

    lax.fori_loop(0, vectors // 2, pair_of, 0)
    crossed = lax.dot_general(left_ref[...], right_ref[...], MINOR, preferred_element_type=f32)
    edges = left_ref[:order]
    edges = lax.dot_general(edges, edges, MINOR, preferred_element_type=f32)

    def put(slot, value):
        tiles_ref[:, slot * vectors : (slot + 1) * vectors] = value

    put(0, fold(acc_ref[...] + edges, vectors))
    for side in range(2):
        flux = cut_ref[2 + side].astype(bf16)
        for slot, left, right in ((1 + 3 * side, ends_ref[side], flux), (2 + 3 * side, flux, ends_ref[side])):
            here = slice(slot * vectors, (slot + 1) * vectors)
            tiles_ref[:, here] = tiles_ref[:, here] + lax.dot_general(left, right, MINOR, preferred_element_type=f32)
        here = slice(side * order, side * order + order)
        cross = fold(crossed[:order, here], vectors)
        put(7 + 3 * side, cross.T)
        put(8 + 3 * side, cross)
        put(9 + 3 * side, fold(crossed[order:, here], vectors))
    thin = lax.broadcasted_iota(jnp.int32, (vectors, n_y), 1)
    slot = 13
    for x in range(2):
        for y in range(2):
            along = jnp.where(thin % SPOTS == 2 - y, cut_ref[x], 0.0).astype(bf16)
            put(slot, lax.dot_general(along, ends_ref[x], MINOR, preferred_element_type=f32))
            put(slot + 1, lax.dot_general(ends_ref[x], along, MINOR, preferred_element_type=f32))
            slot += 2


def main_kernel(n_row, n_col, mob_ref, own_ref, lab_ref, out_ref,
                cross_ref, mixed_ref, first_ref, plain0_ref, plain1_ref, part_ref, rows0_ref, rows1_ref, root_ref, lines_ref, acc_ref, rims_ref, frims_ref, side_ref,
                rootx_ref, rooty_ref, xhalo_ref, pack_ref, yhalo_ref, faces_ref, ends_ref, left_ref, right_ref, cut_ref,
                tiles_ref, message_ref, here_ref, mine_ref, panel_ref, local_ref, low_ref,
                xsend_sem, xrecv_sem, ysend_sem, yrecv_sem, send_sem, recv_sem, send_sem2, recv_sem2):
    p = pl.program_id(0)
    n_z = rims_ref.shape[1]
    pairs = n_z // 2
    vectors = side_ref.shape[0]
    n_sub = n_row * n_col
    r = lax.axis_index("row")
    c = lax.axis_index("col")
    me = r * n_col + c
    barrier = pltpu.get_barrier_semaphore()

    def peer(k):
        other = lax.rem(me + k, n_sub)
        return other, (other // n_col, lax.rem(other, n_col))

    def rim_copy(side, some):
        return pltpu.make_async_remote_copy(
            src_ref=rims_ref.at[side, some], dst_ref=xhalo_ref.at[1 - side, some],
            send_sem=xsend_sem.at[side], recv_sem=xrecv_sem.at[1 - side],
            device_id=(lax.rem(r + 2 * side - 1 + n_row, n_row), c), device_id_type=MESH)

    def column_copy(way):
        return pltpu.make_async_remote_copy(
            src_ref=pack_ref.at[way], dst_ref=yhalo_ref.at[way],
            send_sem=ysend_sem.at[way], recv_sem=yrecv_sem.at[way],
            device_id=(r, lax.rem(c + 1 - 2 * way + n_col, n_col)), device_id_type=MESH)

    x_there = (r > 0, r < n_row - 1)
    y_there = (c > 0, c < n_col - 1)

    @pl.when(p == 0)
    def _():
        def greet(k, carry):
            pl.semaphore_signal(barrier, inc=1, device_id=peer(k)[1], device_id_type=MESH)
            return carry

        lax.fori_loop(1, n_sub, greet, 0)
        cross_ref[...] = cross_weights(side_ref.shape[2])
        for ref in (first_ref, plain0_ref, plain1_ref, part_ref, rows0_ref, rows1_ref, root_ref, acc_ref, side_ref, rooty_ref):
            ref[...] = jnp.zeros_like(ref)
        tiles_ref[:, SLOTS * vectors :] = jnp.zeros((vectors, tiles_ref.shape[1] - SLOTS * vectors), jnp.float32)
        for side in range(2):
            @pl.when(jnp.logical_not(x_there[side]))
            def _():
                xhalo_ref[side] = jnp.zeros(xhalo_ref.shape[1:], jnp.bfloat16)

            @pl.when(jnp.logical_not(y_there[side]))
            def _():
                yhalo_ref[side] = jnp.zeros(yhalo_ref.shape[1:], jnp.bfloat16)

    @pl.when(2 * p == CHUNK)
    def _():
        pl.semaphore_wait(barrier, n_sub - 1)

    @pl.when((lax.rem(2 * p, CHUNK) == 0) & (p > 0))
    def _():
        for side in range(2):
            @pl.when(x_there[side])
            def _():
                rim_copy(side, pl.ds(2 * p - CHUNK, CHUNK)).start()

    plains, rows = (plain0_ref, plain1_ref), (rows0_ref, rows1_ref)

    def rims(fresh):
        if fresh:
            for side in range(2):
                for s in range(2):
                    rims_ref[side, 2 * p + s] = lines_ref[s, side].astype(jnp.bfloat16)
                frims_ref[side, 2 * p] = lines_ref[3, side].astype(jnp.bfloat16)
        for side in range(2):
            frims_ref[side, jnp.maximum(2 * p - 1, 1)] = lines_ref[2, side].astype(jnp.bfloat16)

    for odd in range(2):
        @pl.when((p < pairs) & (lax.rem(p, 2) == odd))
        def _():
            roots(p, mob_ref, lab_ref, root_ref, rootx_ref, rooty_ref)
            gram(acc_ref, rows[1 - odd], (0, 1))
            stencil(p, True, own_ref, cross_ref, mixed_ref, first_ref, plains[odd], plains[1 - odd], part_ref,
                    rows[odd], root_ref, side_ref, lines_ref)
            root_ref[0] = root_ref[2]
            rims(True)

    @pl.when(p == pairs)
    def _():
        pack_columns(side_ref, pack_ref)
        for way in range(2):
            @pl.when(y_there[1 - way])
            def _():
                column_copy(way).start()
        odd = pairs % 2
        stencil(p, False, own_ref, cross_ref, mixed_ref, first_ref, plains[odd], plains[1 - odd], part_ref, rows[odd],
                root_ref, side_ref, lines_ref)
        rims(False)
        gram(acc_ref, rows[1 - odd], (0, 1))
        gram(acc_ref, rows[odd], (0,))
        everything = pl.ds(0, n_z)
        for side in range(2):
            @pl.when(x_there[side])
            def _():
                rim_copy(1 - side, everything).wait_recv()
        x_tiles(tiles_ref, frims_ref, xhalo_ref, rootx_ref, faces_ref, ends_ref)
        for way in range(2):
            @pl.when(y_there[way])
            def _():
                column_copy(way).wait_recv()
        y_tiles(tiles_ref, acc_ref, side_ref, rooty_ref, yhalo_ref, ends_ref, left_ref, right_ref, cut_ref)
        trade(n_row, n_col, tiles_ref, local_ref, panel_ref, message_ref, mine_ref, here_ref,
              send_sem, recv_sem, send_sem2, recv_sem2)
        panels(n_row, n_col, local_ref, panel_ref, out_ref, low_ref)
        for side in range(2):
            @pl.when(x_there[side])
            def _():
                rim_copy(side, everything).wait_send()
        for way in range(2):
            @pl.when(y_there[1 - way])
            def _():
                column_copy(way).wait_send()


def main_call(own, labels, mobility, n_row, n_col):
    vectors, n_z, n_x, n_y = own.shape
    n_sub = n_row * n_col
    depth = vectors // n_col
    width = vectors // n_row * n_sub
    order = vectors * ROWS
    blocks = n_x // ROWS
    f32, bf16 = jnp.float32, jnp.bfloat16
    last = n_z // 2 - 1
    return pl.pallas_call(
        functools.partial(main_kernel, n_row, n_col),
        grid=(n_z // 2 + 1,),
        in_specs=[
            pl.BlockSpec(memory_space=pltpu.SMEM),
            pl.BlockSpec((vectors, 2, n_x, n_y), lambda p: (0, jnp.minimum(p, last), 0, 0)),
            pl.BlockSpec((2, n_x, n_y), lambda p: (jnp.minimum(p, last), 0, 0)),
        ],
        out_specs=pl.BlockSpec((n_sub, depth, width), lambda p: (0, 0, 0)),
        out_shape=jax.ShapeDtypeStruct((n_sub, depth, width), f32),
        scratch_shapes=[
            pltpu.VMEM((2 * n_y, 2 * n_y), bf16),
            pltpu.VMEM((vectors * n_x, 2 * n_y), f32),
            pltpu.VMEM((vectors, n_x + 2 * ROWS, n_y), f32),
            pltpu.VMEM((vectors, n_x + 2 * ROWS, n_y), f32),
            pltpu.VMEM((vectors, n_x + 2 * ROWS, n_y), f32),
            pltpu.VMEM((vectors, n_x, n_y), f32),
            pltpu.VMEM((2, blocks, order, 2 * n_y), bf16),
            pltpu.VMEM((2, blocks, order, 2 * n_y), bf16),
            pltpu.VMEM((3, n_x, n_y), f32),
            pltpu.VMEM((4, 2, vectors, n_y), f32),
            pltpu.VMEM((order, order), f32),
            pltpu.VMEM((2, n_z, vectors, n_y), bf16),
            pltpu.VMEM((2, n_z, vectors, n_y), bf16),
            pltpu.VMEM((vectors, n_x, n_y), bf16),
            pltpu.VMEM((n_z, 2, n_y), f32),
            pltpu.VMEM((n_x, n_y), f32),
            pltpu.VMEM((2, n_z, vectors, n_y), bf16),
            pltpu.VMEM((2, vectors, n_x // SPOTS, n_y), bf16),
            pltpu.VMEM((2, vectors, n_x // SPOTS, n_y), bf16),
            pltpu.VMEM((2, 2 * vectors, n_z * n_y), bf16),
            pltpu.VMEM((2, vectors, n_y), bf16),
            pltpu.VMEM((2 * order, blocks * n_y), bf16),
            pltpu.VMEM((2 * order, blocks * n_y), bf16),
            pltpu.VMEM((4, vectors, n_y), f32),
            pltpu.VMEM((vectors, -(-SLOTS // n_col) * n_col * vectors), f32),
            pltpu.VMEM((n_sub, depth, width), f32),
            pltpu.VMEM((n_sub, depth, width), f32),
            pltpu.VMEM((depth, width), f32),
            pltpu.VMEM((n_sub, depth, width), f32),
            pltpu.VMEM((n_sub, depth, width), f32),
            pltpu.VMEM((2 * PSUB * vectors, 2 * n_col // (2 * PSUB) * width), f32),
            pltpu.SemaphoreType.DMA((2,)),
            pltpu.SemaphoreType.DMA((2,)),
            pltpu.SemaphoreType.DMA((2,)),
            pltpu.SemaphoreType.DMA((2,)),
            pltpu.SemaphoreType.DMA((n_sub,)),
            pltpu.SemaphoreType.DMA((n_sub,)),
            pltpu.SemaphoreType.DMA((n_sub,)),
            pltpu.SemaphoreType.DMA((n_sub,)),
        ],
        compiler_params=pltpu.CompilerParams(
            collective_id=0, has_side_effects=True, vmem_limit_bytes=62200 * 1024),
    )(mobility, own, labels)


def body(own, labels, mobility):
    n_row = lax.axis_size("row")
    n_col = lax.axis_size("col")
    n_sub = n_row * n_col
    vectors = own.shape[0]
    local = main_call(own, labels, mobility, n_row, n_col)
    return local.reshape(
        n_sub, vectors // (NB * n_col), 1, NB, vectors // (NB * n_row), 1, NB, n_sub
    )


def solution(mesh):
    return jax.shard_map(
        body,
        mesh=mesh,
        in_specs=(P(None, None, "row", "col"), P(None, "row", "col"), P()),
        out_specs=P(None, None, "col", None, None, "row", None, None),
        check_vma=False,
    )
```

```python
import functools

import jax
import jax.numpy as jnp
from jax import lax
from jax.experimental import pallas as pl
from jax.experimental.pallas import tpu as pltpu
from jax.sharding import PartitionSpec as P

NB = 2
PSUB = 2
SLOTS = 21
MESH = pl.DeviceIdType.MESH
PLAIN = (((1,), (0,)), ((), ()))


FACES = ((-1, 0), (1, 0), (0, -1), (0, 1))


def slot_offsets():
    offsets = [((0, 0), (0, 0))]
    for face in FACES:
        offsets += [((0, 0), face), (face, (0, 0)), (face, face)]
    for face_x in FACES[:2]:
        for face_y in FACES[2:]:
            offsets += [(face_x, face_y), (face_y, face_x)]
    return offsets


def exact_dot(left, right, dims=PLAIN):
    return lax.dot_general(left, right, dims, precision=lax.Precision.HIGHEST, preferred_element_type=jnp.float32)


def swap_bits(tiles, bits):
    lanes = lax.broadcasted_iota(jnp.int32, tiles[0].shape, 1)
    width = tiles[0].shape[1]
    for index, lane in bits:
        low = lanes // lane % 2 == 0
        out = list(tiles)
        for i in range(len(tiles)):
            if i // index % 2 == 0:
                a, b = tiles[i], tiles[i + index]
                out[i] = jnp.where(low, a, pltpu.roll(b, lane, 1))
                out[i + index] = jnp.where(low, pltpu.roll(a, width - lane, 1), b)
        tiles = out
    return tiles


def powers(count):
    return [1 << i for i in range(count.bit_length() - 1)]


def trade(n_row, n_col, tile_ref, out_ref, all_ref, send_ref, mine_ref, here_ref,
          send_sem, recv_sem, send_sem2, recv_sem2):
    vectors = tile_ref.shape[0]
    n_sub = n_row * n_col
    col_blocks = vectors // (NB * n_col)
    width = n_col * vectors
    depth = col_blocks * NB
    r = lax.axis_index("row")
    c = lax.axis_index("col")
    me = r * n_col + c

    upper = 2 * me // n_sub

    def peer(k):
        return lax.rem(me + upper * k + (1 - upper) * (n_sub - k), n_sub)

    at = lax.broadcasted_iota(jnp.int32, (vectors, vectors), 0)
    source = (at // NB % col_blocks * n_col + at // (NB * col_blocks)) * NB + at % NB
    turn = (source == lax.broadcasted_iota(jnp.int32, (vectors, vectors), 1)).astype(jnp.float32)
    ordered = exact_dot(turn, tile_ref[...])
    packs = tile_ref.shape[1] // width
    blank = jnp.zeros((depth, width), jnp.float32)
    for column in range(n_col):
        some = slice(column * depth, column * depth + depth)
        tiles = [ordered[some, k * width : k * width + width] if k < packs else blank for k in range(n_row)]
        tiles = swap_bits(tiles, [(bit, NB * bit) for bit in powers(n_row)])
        for row in range(n_row):
            send_ref[row * n_col + column] = tiles[row]

    def exchange(source_of, target_ref, sends, recvs):
        def copy(other):
            return pltpu.make_async_remote_copy(
                src_ref=source_of(other), dst_ref=target_ref.at[me], send_sem=sends.at[other], recv_sem=recvs.at[me],
                device_id=(other // n_col, lax.rem(other, n_col)), device_id_type=MESH)

        def begin():
            def one(k, carry):
                copy(peer(k)).start()
                return carry

            lax.fori_loop(1, n_sub, one, 0)

        def finish(first, last):
            def one(other, carry):
                @pl.when(other != me)
                def _():
                    pltpu.make_async_remote_copy(
                        src_ref=source_of(other), dst_ref=target_ref.at[other], send_sem=sends.at[other],
                        recv_sem=recvs.at[other], device_id=(other // n_col, lax.rem(other, n_col)),
                        device_id_type=MESH).wait_recv()

                return carry

            lax.fori_loop(first, last, one, 0)

        def drain():
            def one(k, carry):
                copy(peer(k)).wait_send()
                return carry

            lax.fori_loop(1, n_sub, one, 0)

        return begin, finish, drain

    offsets = slot_offsets()
    quads = n_sub // n_row
    lanes = lax.broadcasted_iota(jnp.int32, (depth, width), 1) % n_sub
    ends, reach = 2 * PSUB, 2 * n_col

    def banded(values):
        bands = {}
        for (start, stop), value in zip(offsets, values):
            shift = start[0] * n_col + start[1]
            if shift:
                value = pltpu.roll(value, shift % width, 1)
            step = (stop[0] - start[0]) * n_col + stop[1] - start[1]
            bands[step] = bands[step] + value if step in bands else value
        return bands

    def place(bands, b):
        value = jnp.zeros((depth, width), jnp.float32)
        for step, band in bands.items():
            if 0 <= b - step < n_sub:
                value = jnp.where(lanes == b - step, band, value)
        return value

    begin, finish, drain = exchange(lambda other: send_ref.at[other], here_ref, send_sem, recv_sem)
    begin2, finish2, drain2 = exchange(lambda other: mine_ref, all_ref, send_sem2, recv_sem2)
    low_bits = [(bit, NB * bit) for bit in powers(n_row)]
    here_ref[me] = send_ref[me]
    begin()

    finish(0, n_row)
    tiles = swap_bits([here_ref[s] for s in range(n_row)], low_bits)
    packs = -(-SLOTS // quads)
    stack = jnp.concatenate(tiles[:packs], axis=0)
    shape = (width, quads * width)
    lane = lax.broadcasted_iota(jnp.int32, shape, 0)
    goal = lax.broadcasted_iota(jnp.int32, shape, 1)
    sub, tru = goal % n_sub, goal % width // n_sub
    origin = goal // width * vectors + (tru // NB * n_row + sub) * NB + tru % NB
    stack = exact_dot(stack, ((origin == lane) & (sub < n_row)).astype(jnp.float32))
    values = []
    for slot in range(SLOTS):
        k, quad = divmod(slot, quads)
        values.append(stack[k * depth : k * depth + depth, quad * width : quad * width + width])
    bands = banded(values)
    packed = jnp.zeros((depth, width), jnp.float32)
    for b in range(ends):
        value = jnp.where(lanes < reach, place(bands, b), 0.0)
        packed = packed + (pltpu.roll(value, reach * b, 1) if b else value)
    mine_ref[...] = packed
    all_ref[me] = packed
    begin2()

    finish(n_row, n_sub)
    bits = low_bits + [(n_row * bit, vectors * bit) for bit in powers(quads)]
    tiles = swap_bits([here_ref[s] for s in range(n_sub)], bits)
    stack = jnp.concatenate([tiles[slot % quads * n_row + slot // quads] for slot in range(SLOTS)], axis=0)
    into = lax.broadcasted_iota(jnp.int32, (width, width), 1)
    sub, tru = into % n_sub, into // n_sub
    origin = sub // n_row * vectors + (tru // NB * n_row + sub % n_row) * NB + tru % NB
    order = (origin == lax.broadcasted_iota(jnp.int32, (width, width), 0)).astype(jnp.float32)
    stack = exact_dot(stack, order)
    bands = banded([stack[slot * depth : slot * depth + depth] for slot in range(SLOTS)])
    for b in range(ends, n_sub):
        out_ref[b] = place(bands, b)
    finish2(0, n_sub)

    def settle():
        drain()
        drain2()

    return settle


def panels(n_row, n_col, local_ref, all_ref, out_ref, low_ref):
    n_sub, depth, width = local_ref.shape
    vectors = depth * n_col
    ends, reach = 2 * PSUB, 2 * n_col
    f32 = jnp.float32
    r = lax.axis_index("row")
    c = lax.axis_index("col")
    order = ends * vectors
    at = lax.broadcasted_iota(jnp.int32, (vectors, vectors), 1)
    col_blocks = depth // NB
    source = (at // NB % col_blocks * n_col + at // (NB * col_blocks)) * NB + at % NB
    turn = (source == lax.broadcasted_iota(jnp.int32, (vectors, vectors), 0)).astype(f32)
    high = reach // ends
    by_column = []
    for column in range(n_col):
        tiles = [all_ref[row * n_col + column] for row in range(n_row)]
        bits = [(bit, ends * bit) for bit in powers(n_row)]
        by_column.append(swap_bits(tiles, bits))
    halves = []
    for h in range(high):
        parts = []
        for b in range(ends):
            parts.append(exact_dot(turn, jnp.concatenate([by_column[column][b * high + h] for column in range(n_col)], axis=0)))
        halves.append(jnp.concatenate(parts, axis=0))
    tall = 8
    count = order // tall
    work = [[halves[h][t * tall : t * tall + tall] for t in range(count)] for h in range(high)]
    def spread(value, s):
        return jnp.broadcast_to(value[s : s + 1], (tall, width))

    def spot(k):
        b, q = divmod(k, vectors)
        tr, row, u = q // (NB * n_row), q // NB % n_row, q % NB
        return (tr * NB + u) * n_sub + row * ends + b

    def column(i, k):
        at = spot(k)
        return jnp.broadcast_to(work[0][i][:, at : at + 1], (tall, width)) * ones

    ones = jnp.where(all_ref[0] == all_ref[0], 1.0, 0.0)
    ones = jnp.concatenate([ones] * (tall // depth), axis=0)

    few = 4
    for first in range(0, order, few):
        t, base = divmod(first, tall)
        columns = [column(t, first + s) for s in range(few)]
        rows = [[spread(work[h][t], base + s) for h in range(high)] for s in range(few)]
        scaled, weights = [], {}
        for s in range(few):
            pivot = spread(columns[s], base + s)
            inverse = 1.0 / pivot
            root = lax.rsqrt(pivot)
            k = first + s
            for h in range(high):
                low_ref[k : k + 1, h * width : h * width + width] = (rows[s][h] * root)[:1]
            scaled.append([x * inverse for x in rows[s]])
            for s2 in range(s + 1, few):
                weight = spread(columns[s], base + s2) * inverse
                weights[s, s2] = weight
                rows[s2] = [y - weight * x for x, y in zip(rows[s], rows[s2])]
                columns[s2] = columns[s2] - weight * columns[s]
        done = base + few == tall
        for i in range(t + done, count):
            if i > t:
                columns = [column(i, first + s) for s in range(few)]
                for s in range(few):
                    for s2 in range(s + 1, few):
                        columns[s2] = columns[s2] - weights[s, s2] * columns[s]
            for h in range(high):
                total = columns[0] * scaled[0][h]
                for s in range(1, few):
                    total = total + columns[s] * scaled[s][h]
                work[h][i] = work[h][i] - total
    shape = (order, high * width)
    lane = lax.broadcasted_iota(jnp.int32, shape, 1)
    inner = lane % width
    a = lane // width * ends + inner % ends
    p = (inner // (NB * n_sub) * n_row + inner % n_sub // ends) * NB + inner // n_sub % NB
    keep = a * vectors + p >= lax.broadcasted_iota(jnp.int32, shape, 0)
    low = jnp.where(keep, low_ref[...], 0.0)

    shape = (high * width, width)
    lane = lax.broadcasted_iota(jnp.int32, shape, 0)
    goal = lax.broadcasted_iota(jnp.int32, shape, 1)
    inner = lane % width
    a = lane // width * ends + inner % ends
    mine = (inner % n_sub // ends == r) & (inner // n_sub == goal // n_sub) & (a == goal % n_sub)
    rows_mine = exact_dot(low, mine.astype(f32))
    shape = (ends * depth, order)
    goal = lax.broadcasted_iota(jnp.int32, shape, 0)
    lane = lax.broadcasted_iota(jnp.int32, shape, 1)
    b, inner = goal // depth, goal % depth
    q = (inner // NB * n_col + c) * NB + inner % NB
    pick = (lane == b * vectors + q).astype(f32)
    panel = exact_dot(pick, rows_mine)
    for b in range(ends):
        out_ref[b] = panel[b * depth : b * depth + depth]
    lanes = lax.broadcasted_iota(jnp.int32, (depth, width), 1) % n_sub
    for h in range(1, high):
        shape = (ends * depth, width)
        goal = lax.broadcasted_iota(jnp.int32, shape, 0)
        lane = lax.broadcasted_iota(jnp.int32, shape, 1)
        b, inner = goal // depth, goal % depth
        q = (inner // NB * n_col + c) * NB + inner % NB
        place = (q // (NB * n_row) * NB + q % NB) * n_sub + q // NB % n_row * ends + b
        pick = (lane == place).astype(f32)
        chosen = exact_dot(pick, low[:, h * width : h * width + width], (((1,), (1,)), ((), ())))
        change = exact_dot(chosen, rows_mine)
        for b in range(ends):
            value = local_ref[h * ends + b] - change[b * depth : b * depth + depth]
            out_ref[h * ends + b] = jnp.where(lanes < ends, 0.0, value)
    for b in range(reach, n_sub):
        out_ref[b] = jnp.where(lanes < ends, 0.0, local_ref[b])


ROWS = 8
SPOTS = 4
CHUNK = 4
MINOR = (((1,), (1,)), ((), ()))


def cross_weights(n_y):
    shape = (2 * n_y, 2 * n_y)
    i = lax.broadcasted_iota(jnp.int32, shape, 0)
    j = lax.broadcasted_iota(jnp.int32, shape, 1)
    gap = i % n_y - j % n_y
    same = i // n_y == j // n_y
    near = jnp.where((gap == 1) | (gap == -1), 1.0, jnp.where(gap == 0, -6.0, 0.0))
    return jnp.where(same, near, jnp.where(gap == 0, 1.0, 0.0)).astype(jnp.bfloat16)


def stencil(p, fresh, own_ref, cross_ref, mixed_ref, first_ref, now_ref, old_ref, part_ref, rows_ref, root_ref, side_ref,
            lines_ref):
    vectors, n_x, n_y = side_ref.shape
    blocks = n_x // ROWS
    inner = slice(ROWS, ROWS + n_x)
    up, down = slice(ROWS + 1, ROWS + 1 + n_x), slice(ROWS - 1, ROWS - 1 + n_x)
    if fresh:
        both = jnp.concatenate([own_ref[:, s].reshape(vectors * n_x, n_y) for s in range(2)], axis=1)
        mixed_ref[...] = lax.dot_general(both, cross_ref[...], PLAIN, preferred_element_type=jnp.float32)
        lanes = lax.broadcasted_iota(jnp.int32, (n_x, n_y), 1)
        z = 2 * p
        kept = [(lanes < SPOTS * (z + s + 1)) & (lanes >= SPOTS * (z + s)) for s in range(2)]
    for m in range(vectors // 2):
        mids, fluxes = [[], []], [[], []]
        for v in (2 * m, 2 * m + 1):
            last = old_ref[v, inner]
            total = part_ref[v]
            mids[0].append(last)
            if fresh:
                own = own_ref[v, 0].astype(jnp.float32)
                first_ref[v, inner] = own
                next_own = own_ref[v, 1].astype(jnp.float32)
                now_ref[v, inner] = next_own
                total = total + own
                mixed = mixed_ref[v * n_x : v * n_x + n_x]
                near = mixed[:, :n_y] + (first_ref[v, up] + first_ref[v, down]) + last
                part_ref[v] = mixed[:, n_y:] + (now_ref[v, up] + now_ref[v, down])
                flux = near * root_ref[1]
                for s, value in enumerate((own, next_own)):
                    lines_ref[s, 0, v : v + 1] = value[:1]
                    lines_ref[s, 1, v : v + 1] = value[n_x - 1 :]
                    turned = pltpu.roll(own_ref[v, s], lax.rem(SPOTS * (z + s) + 2, n_y), 1)
                    side_ref[v] = jnp.where(kept[s], turned, side_ref[v])
                lines_ref[3, 0, v : v + 1] = flux[:1]
                lines_ref[3, 1, v : v + 1] = flux[n_x - 1 :]
                mids[1].append(own)
                fluxes[1].append(flux)
            flux = total * root_ref[0]
            lines_ref[2, 0, v : v + 1] = flux[:1]
            lines_ref[2, 1, v : v + 1] = flux[n_x - 1 :]
            fluxes[0].append(flux)
        where = slice(2 * m * ROWS, 2 * m * ROWS + 2 * ROWS)
        for b in range(blocks):
            part = slice(b * ROWS, b * ROWS + ROWS)
            for s in range(2 if fresh else 1):
                for which, values in enumerate((mids[s], fluxes[s])):
                    rows_ref[s, b, where, which * n_y : which * n_y + n_y] = jnp.concatenate(
                        [value[part] for value in values], axis=0).astype(jnp.bfloat16)


def gram(acc_ref, rows_ref, slices):
    both = jnp.concatenate([rows_ref[s, b] for s in slices for b in range(rows_ref.shape[1])], axis=1)
    acc_ref[...] += lax.dot_general(both, both, MINOR, preferred_element_type=jnp.float32)


def roots(p, mob_ref, lab_ref, root_ref, rootx_ref, rooty_ref):
    _, n_x, n_y = root_ref.shape
    lanes = lax.broadcasted_iota(jnp.int32, (n_x, n_y), 1)
    for s in range(2):
        z = 2 * p + s
        value = jnp.zeros((n_x, n_y), jnp.float32)
        for phase in range(mob_ref.shape[0]):
            value = value + jnp.where(lab_ref[s] == phase, mob_ref[phase], jnp.float32(0.0))
        root = jnp.sqrt(value)
        root_ref[1 + s] = jnp.where((lanes == 0) | (lanes == n_y - 1), 0.0, root)
        rootx_ref[z, 0:1] = root[:1]
        rootx_ref[z, 1:2] = root[n_x - 1 :]
        ok = (lanes < SPOTS * z + SPOTS) & (lanes >= SPOTS * z)
        rooty_ref[...] = jnp.where(ok, pltpu.roll(root, lax.rem(SPOTS * z + 2, n_y), 1), rooty_ref[...])


def pack_columns(side_ref, pack_ref):
    vectors, n_x, n_y = side_ref.shape
    quarter = n_x // SPOTS
    spot = lax.broadcasted_iota(jnp.int32, (quarter, n_y), 1) % SPOTS

    def some(m, carry):
        for v in range(4):
            v = 4 * m + v
            for to, column in enumerate((1, 2)):
                total = jnp.zeros((quarter, n_y), jnp.float32)
                for k in range(SPOTS):
                    part = side_ref[v, k * quarter : k * quarter + quarter].astype(jnp.float32)
                    part = pltpu.roll(part, (k - column) % n_y, 1) if k != column else part
                    total = jnp.where(spot == k, part, total)
                pack_ref[to, v] = total.astype(jnp.bfloat16)
        return carry

    lax.fori_loop(0, vectors // 4, some, 0)


def x_tiles(tiles_ref, frims_ref, xhalo_ref, rootx_ref, faces_ref, ends_ref):
    _, n_z, vectors, n_y = frims_ref.shape
    thin = lax.broadcasted_iota(jnp.int32, (vectors, n_y), 1)
    for side in range(2):
        total = jnp.zeros((vectors, n_y), jnp.float32)
        for z in range(n_z):
            over = xhalo_ref[side, z].astype(jnp.float32) * rootx_ref[z, side : side + 1]
            at = slice(z * n_y, z * n_y + n_y)
            faces_ref[side, :vectors, at] = frims_ref[side, z]
            faces_ref[side, vectors:, at] = over.astype(jnp.bfloat16)
            ok = (thin >= SPOTS * z) & (thin < SPOTS * z + SPOTS)
            total = jnp.where(ok, pltpu.roll(over, (SPOTS * z + 2) % n_y, 1), total)
        ends_ref[side] = total.astype(jnp.bfloat16)
        gram = lax.dot_general(faces_ref[side], faces_ref[side], MINOR, preferred_element_type=jnp.float32)
        at = (1 + 3 * side) * vectors
        tiles_ref[:, at : at + vectors] = gram[vectors:, :vectors]
        tiles_ref[:, at + vectors : at + 2 * vectors] = gram[:vectors, vectors:]
        tiles_ref[:, at + 2 * vectors : at + 3 * vectors] = gram[vectors:, vectors:]


def fold(square, vectors):
    order = square.shape[0]
    line = lax.broadcasted_iota(jnp.int32, (order, order), 0)
    column = lax.broadcasted_iota(jnp.int32, (order, order), 1)
    pick = (lax.broadcasted_iota(jnp.int32, (order, vectors), 0) // ROWS
            == lax.broadcasted_iota(jnp.int32, (order, vectors), 1)).astype(jnp.float32)
    thick = jnp.where(line % ROWS == column % ROWS, square, 0.0).reshape(vectors, ROWS, order).sum(1)
    return exact_dot(thick, pick)


def y_tiles(tiles_ref, acc_ref, side_ref, rooty_ref, yhalo_ref, ends_ref, left_ref, right_ref, cut_ref):
    vectors, n_x, n_y = side_ref.shape
    order = vectors * ROWS
    blocks = n_x // ROWS
    f32, bf16 = jnp.float32, jnp.bfloat16
    rows = lax.broadcasted_iota(jnp.int32, (n_x, n_y), 0)
    lanes = lax.broadcasted_iota(jnp.int32, (n_x, n_y), 1)
    spot = lanes % SPOTS
    root = jnp.where((spot == 1) | (spot == 2), rooty_ref[...], 0.0)

    def spread(packed, column):
        return jnp.concatenate(
            [pltpu.roll(packed, (column - k) % n_y, 1) if k != column else packed for k in range(SPOTS)], axis=0)

    def pair_of(m, carry):
        kept = []
        for i in range(2):
            v = 2 * m + i
            own = side_ref[v].astype(f32)
            near = jnp.where(lanes < SPOTS, 0.0, pltpu.roll(own, SPOTS, 1))
            near = near + jnp.where(lanes >= n_y - SPOTS, 0.0, pltpu.roll(own, n_y - SPOTS, 1))
            near = near + jnp.where(rows == 0, 0.0, pltpu.roll(own, 1, 0))
            near = near + jnp.where(rows == n_x - 1, 0.0, pltpu.roll(own, n_x - 1, 0))
            near = near + jnp.where(spot == 2, pltpu.roll(own, n_y - 1, 1), pltpu.roll(own, 1, 1))
            flux = (near - 6.0 * own) * root
            low = spread(yhalo_ref[0, v].astype(f32), 2)
            upp = spread(yhalo_ref[1, v].astype(f32), 1)
            over = jnp.where(spot == 2, low, upp) * root
            cut_ref[0, pl.ds(v, 1)] = over[:1]
            cut_ref[1, pl.ds(v, 1)] = over[n_x - 1 :]
            cut_ref[2, pl.ds(v, 1)] = flux[:1]
            cut_ref[3, pl.ds(v, 1)] = flux[n_x - 1 :]
            kept.append((flux, over, jnp.where(spot == 2, over, 0.0), jnp.where(spot == 1, over, 0.0)))
        for b in range(blocks):
            part = slice(b * ROWS, b * ROWS + ROWS)
            both = [jnp.concatenate([x[part], y[part]], axis=0).astype(bf16) for x, y in zip(*kept)]
            at = slice(b * n_y, b * n_y + n_y)
            first = pl.ds(pl.multiple_of(m * 2 * ROWS, 2 * ROWS), 2 * ROWS)
            second = pl.ds(pl.multiple_of(order + m * 2 * ROWS, 2 * ROWS), 2 * ROWS)
            left_ref[first, at] = both[0]
            left_ref[second, at] = both[1]
            right_ref[first, at] = both[2]
            right_ref[second, at] = both[3]
        return carry

    lax.fori_loop(0, vectors // 2, pair_of, 0)
    crossed = lax.dot_general(left_ref[...], right_ref[...], MINOR, preferred_element_type=f32)
    edges = left_ref[:order]
    edges = lax.dot_general(edges, edges, MINOR, preferred_element_type=f32)

    def put(slot, value):
        tiles_ref[:, slot * vectors : (slot + 1) * vectors] = value

    put(0, fold(acc_ref[...] + edges, vectors))
    for side in range(2):
        flux = cut_ref[2 + side].astype(bf16)
        for slot, left, right in ((1 + 3 * side, ends_ref[side], flux), (2 + 3 * side, flux, ends_ref[side])):
            here = slice(slot * vectors, (slot + 1) * vectors)
            tiles_ref[:, here] = tiles_ref[:, here] + lax.dot_general(left, right, MINOR, preferred_element_type=f32)
        here = slice(side * order, side * order + order)
        cross = fold(crossed[:order, here], vectors)
        put(7 + 3 * side, cross.T)
        put(8 + 3 * side, cross)
        put(9 + 3 * side, fold(crossed[order:, here], vectors))
    thin = lax.broadcasted_iota(jnp.int32, (vectors, n_y), 1)
    slot = 13
    for x in range(2):
        for y in range(2):
            along = jnp.where(thin % SPOTS == 2 - y, cut_ref[x], 0.0).astype(bf16)
            put(slot, lax.dot_general(along, ends_ref[x], MINOR, preferred_element_type=f32))
            put(slot + 1, lax.dot_general(ends_ref[x], along, MINOR, preferred_element_type=f32))
            slot += 2


def main_kernel(n_row, n_col, mob_ref, own_ref, lab_ref, out_ref,
                cross_ref, mixed_ref, first_ref, plain0_ref, plain1_ref, part_ref, rows0_ref, rows1_ref, root_ref, lines_ref, acc_ref, rims_ref, frims_ref, side_ref,
                rootx_ref, rooty_ref, xhalo_ref, pack_ref, yhalo_ref, faces_ref, ends_ref, left_ref, right_ref, cut_ref,
                tiles_ref, message_ref, here_ref, mine_ref, panel_ref, local_ref, low_ref,
                xsend_sem, xrecv_sem, ysend_sem, yrecv_sem, send_sem, recv_sem, send_sem2, recv_sem2):
    p = pl.program_id(0)
    n_z = rims_ref.shape[1]
    pairs = n_z // 2
    vectors = side_ref.shape[0]
    n_sub = n_row * n_col
    r = lax.axis_index("row")
    c = lax.axis_index("col")
    me = r * n_col + c
    barrier = pltpu.get_barrier_semaphore()

    def peer(k):
        other = lax.rem(me + k, n_sub)
        return other, (other // n_col, lax.rem(other, n_col))

    def rim_copy(side, some):
        return pltpu.make_async_remote_copy(
            src_ref=rims_ref.at[side, some], dst_ref=xhalo_ref.at[1 - side, some],
            send_sem=xsend_sem.at[side], recv_sem=xrecv_sem.at[1 - side],
            device_id=(lax.rem(r + 2 * side - 1 + n_row, n_row), c), device_id_type=MESH)

    def column_copy(way):
        return pltpu.make_async_remote_copy(
            src_ref=pack_ref.at[way], dst_ref=yhalo_ref.at[way],
            send_sem=ysend_sem.at[way], recv_sem=yrecv_sem.at[way],
            device_id=(r, lax.rem(c + 1 - 2 * way + n_col, n_col)), device_id_type=MESH)

    x_there = (r > 0, r < n_row - 1)
    y_there = (c > 0, c < n_col - 1)

    @pl.when(p == 0)
    def _():
        def greet(k, carry):
            pl.semaphore_signal(barrier, inc=1, device_id=peer(k)[1], device_id_type=MESH)
            return carry

        lax.fori_loop(1, n_sub, greet, 0)
        cross_ref[...] = cross_weights(side_ref.shape[2])
        for ref in (plain1_ref, part_ref, rows1_ref, root_ref, acc_ref, side_ref, rooty_ref):
            ref[...] = jnp.zeros_like(ref)
        rim = jnp.zeros((vectors, ROWS, side_ref.shape[2]), jnp.float32)
        for ref in (first_ref, plain0_ref):
            ref[:, :ROWS] = rim
            ref[:, ROWS + side_ref.shape[1] :] = rim
        tiles_ref[:, SLOTS * vectors :] = jnp.zeros((vectors, tiles_ref.shape[1] - SLOTS * vectors), jnp.float32)
        for side in range(2):
            @pl.when(jnp.logical_not(x_there[side]))
            def _():
                xhalo_ref[side] = jnp.zeros(xhalo_ref.shape[1:], jnp.bfloat16)

            @pl.when(jnp.logical_not(y_there[side]))
            def _():
                yhalo_ref[side] = jnp.zeros(yhalo_ref.shape[1:], jnp.bfloat16)

    @pl.when(2 * p == CHUNK)
    def _():
        pl.semaphore_wait(barrier, n_sub - 1)

    @pl.when((lax.rem(2 * p, CHUNK) == 0) & (p > 0))
    def _():
        for side in range(2):
            @pl.when(x_there[side])
            def _():
                rim_copy(side, pl.ds(2 * p - CHUNK, CHUNK)).start()

    plains, rows = (plain0_ref, plain1_ref), (rows0_ref, rows1_ref)

    def rims(fresh):
        if fresh:
            for side in range(2):
                for s in range(2):
                    rims_ref[side, 2 * p + s] = lines_ref[s, side].astype(jnp.bfloat16)
                frims_ref[side, 2 * p] = lines_ref[3, side].astype(jnp.bfloat16)
        for side in range(2):
            frims_ref[side, jnp.maximum(2 * p - 1, 1)] = lines_ref[2, side].astype(jnp.bfloat16)

    for odd in range(2):
        @pl.when((p < pairs) & (lax.rem(p, 2) == odd))
        def _():
            roots(p, mob_ref, lab_ref, root_ref, rootx_ref, rooty_ref)
            gram(acc_ref, rows[1 - odd], (0, 1))
            stencil(p, True, own_ref, cross_ref, mixed_ref, first_ref, plains[odd], plains[1 - odd], part_ref,
                    rows[odd], root_ref, side_ref, lines_ref)
            root_ref[0] = root_ref[2]
            rims(True)

    @pl.when(p == pairs)
    def _():
        pack_columns(side_ref, pack_ref)
        for way in range(2):
            @pl.when(y_there[1 - way])
            def _():
                column_copy(way).start()
        odd = pairs % 2
        stencil(p, False, own_ref, cross_ref, mixed_ref, first_ref, plains[odd], plains[1 - odd], part_ref, rows[odd],
                root_ref, side_ref, lines_ref)
        rims(False)
        gram(acc_ref, rows[1 - odd], (0, 1))
        gram(acc_ref, rows[odd], (0,))
        everything = pl.ds(0, n_z)
        for side in range(2):
            @pl.when(x_there[side])
            def _():
                rim_copy(1 - side, everything).wait_recv()
        x_tiles(tiles_ref, frims_ref, xhalo_ref, rootx_ref, faces_ref, ends_ref)
        for way in range(2):
            @pl.when(y_there[way])
            def _():
                column_copy(way).wait_recv()
        y_tiles(tiles_ref, acc_ref, side_ref, rooty_ref, yhalo_ref, ends_ref, left_ref, right_ref, cut_ref)
        settle = trade(n_row, n_col, tiles_ref, local_ref, panel_ref, message_ref, mine_ref, here_ref,
              send_sem, recv_sem, send_sem2, recv_sem2)
        panels(n_row, n_col, local_ref, panel_ref, out_ref, low_ref)
        settle()
        for side in range(2):
            @pl.when(x_there[side])
            def _():
                rim_copy(side, everything).wait_send()
        for way in range(2):
            @pl.when(y_there[1 - way])
            def _():
                column_copy(way).wait_send()


def main_call(own, labels, mobility, n_row, n_col):
    vectors, n_z, n_x, n_y = own.shape
    n_sub = n_row * n_col
    depth = vectors // n_col
    width = vectors // n_row * n_sub
    order = vectors * ROWS
    blocks = n_x // ROWS
    f32, bf16 = jnp.float32, jnp.bfloat16
    last = n_z // 2 - 1
    return pl.pallas_call(
        functools.partial(main_kernel, n_row, n_col),
        grid=(n_z // 2 + 1,),
        in_specs=[
            pl.BlockSpec(memory_space=pltpu.SMEM),
            pl.BlockSpec((vectors, 2, n_x, n_y), lambda p: (0, jnp.minimum(p, last), 0, 0)),
            pl.BlockSpec((2, n_x, n_y), lambda p: (jnp.minimum(p, last), 0, 0)),
        ],
        out_specs=pl.BlockSpec((n_sub, depth, width), lambda p: (0, 0, 0)),
        out_shape=jax.ShapeDtypeStruct((n_sub, depth, width), f32),
        scratch_shapes=[
            pltpu.VMEM((2 * n_y, 2 * n_y), bf16),
            pltpu.VMEM((vectors * n_x, 2 * n_y), f32),
            pltpu.VMEM((vectors, n_x + 2 * ROWS, n_y), f32),
            pltpu.VMEM((vectors, n_x + 2 * ROWS, n_y), f32),
            pltpu.VMEM((vectors, n_x + 2 * ROWS, n_y), f32),
            pltpu.VMEM((vectors, n_x, n_y), f32),
            pltpu.VMEM((2, blocks, order, 2 * n_y), bf16),
            pltpu.VMEM((2, blocks, order, 2 * n_y), bf16),
            pltpu.VMEM((3, n_x, n_y), f32),
            pltpu.VMEM((4, 2, vectors, n_y), f32),
            pltpu.VMEM((order, order), f32),
            pltpu.VMEM((2, n_z, vectors, n_y), bf16),
            pltpu.VMEM((2, n_z, vectors, n_y), bf16),
            pltpu.VMEM((vectors, n_x, n_y), bf16),
            pltpu.VMEM((n_z, 2, n_y), f32),
            pltpu.VMEM((n_x, n_y), f32),
            pltpu.VMEM((2, n_z, vectors, n_y), bf16),
            pltpu.VMEM((2, vectors, n_x // SPOTS, n_y), bf16),
            pltpu.VMEM((2, vectors, n_x // SPOTS, n_y), bf16),
            pltpu.VMEM((2, 2 * vectors, n_z * n_y), bf16),
            pltpu.VMEM((2, vectors, n_y), bf16),
            pltpu.VMEM((2 * order, blocks * n_y), bf16),
            pltpu.VMEM((2 * order, blocks * n_y), bf16),
            pltpu.VMEM((4, vectors, n_y), f32),
            pltpu.VMEM((vectors, -(-SLOTS // n_col) * n_col * vectors), f32),
            pltpu.VMEM((n_sub, depth, width), f32),
            pltpu.VMEM((n_sub, depth, width), f32),
            pltpu.VMEM((depth, width), f32),
            pltpu.VMEM((n_sub, depth, width), f32),
            pltpu.VMEM((n_sub, depth, width), f32),
            pltpu.VMEM((2 * PSUB * vectors, 2 * n_col // (2 * PSUB) * width), f32),
            pltpu.SemaphoreType.DMA((2,)),
            pltpu.SemaphoreType.DMA((2,)),
            pltpu.SemaphoreType.DMA((2,)),
            pltpu.SemaphoreType.DMA((2,)),
            pltpu.SemaphoreType.DMA((n_sub,)),
            pltpu.SemaphoreType.DMA((n_sub,)),
            pltpu.SemaphoreType.DMA((n_sub,)),
            pltpu.SemaphoreType.DMA((n_sub,)),
        ],
        compiler_params=pltpu.CompilerParams(
            collective_id=0, has_side_effects=True, vmem_limit_bytes=62200 * 1024),
    )(mobility, own, labels)


def body(own, labels, mobility):
    n_row = lax.axis_size("row")
    n_col = lax.axis_size("col")
    n_sub = n_row * n_col
    vectors = own.shape[0]
    local = main_call(own, labels, mobility, n_row, n_col)
    return local.reshape(
        n_sub, vectors // (NB * n_col), 1, NB, vectors // (NB * n_row), 1, NB, n_sub
    )


def solution(mesh):
    return jax.shard_map(
        body,
        mesh=mesh,
        in_specs=(P(None, None, "row", "col"), P(None, "row", "col"), P()),
        out_specs=P(None, None, "col", None, None, "row", None, None),
        check_vma=False,
    )
```

```python
import functools

import jax
import jax.numpy as jnp
from jax import lax
from jax.experimental import pallas as pl
from jax.experimental.pallas import tpu as pltpu
from jax.sharding import PartitionSpec as P

NB = 2
PSUB = 2
SLOTS = 21
MESH = pl.DeviceIdType.MESH
PLAIN = (((1,), (0,)), ((), ()))


FACES = ((-1, 0), (1, 0), (0, -1), (0, 1))


def slot_offsets():
    offsets = [((0, 0), (0, 0))]
    for face in FACES:
        offsets += [((0, 0), face), (face, (0, 0)), (face, face)]
    for face_x in FACES[:2]:
        for face_y in FACES[2:]:
            offsets += [(face_x, face_y), (face_y, face_x)]
    return offsets


def exact_dot(left, right, dims=PLAIN):
    return lax.dot_general(left, right, dims, precision=lax.Precision.HIGHEST, preferred_element_type=jnp.float32)


def swap_bits(tiles, bits):
    lanes = lax.broadcasted_iota(jnp.int32, tiles[0].shape, 1)
    width = tiles[0].shape[1]
    for index, lane in bits:
        low = lanes // lane % 2 == 0
        out = list(tiles)
        for i in range(len(tiles)):
            if i // index % 2 == 0:
                a, b = tiles[i], tiles[i + index]
                out[i] = jnp.where(low, a, pltpu.roll(b, lane, 1))
                out[i + index] = jnp.where(low, pltpu.roll(a, width - lane, 1), b)
        tiles = out
    return tiles


def powers(count):
    return [1 << i for i in range(count.bit_length() - 1)]


def trade(n_row, n_col, tile_ref, out_ref, all_ref, send_ref, mine_ref, here_ref,
          send_sem, recv_sem, send_sem2, recv_sem2):
    vectors = tile_ref.shape[0]
    n_sub = n_row * n_col
    col_blocks = vectors // (NB * n_col)
    width = n_col * vectors
    depth = col_blocks * NB
    r = lax.axis_index("row")
    c = lax.axis_index("col")
    me = r * n_col + c

    upper = 2 * me // n_sub

    def peer(k):
        return lax.rem(me + upper * k + (1 - upper) * (n_sub - k), n_sub)

    at = lax.broadcasted_iota(jnp.int32, (vectors, vectors), 0)
    source = (at // NB % col_blocks * n_col + at // (NB * col_blocks)) * NB + at % NB
    turn = (source == lax.broadcasted_iota(jnp.int32, (vectors, vectors), 1)).astype(jnp.float32)
    ordered = exact_dot(turn, tile_ref[...])
    packs = tile_ref.shape[1] // width
    blank = jnp.zeros((depth, width), jnp.float32)
    for column in range(n_col):
        some = slice(column * depth, column * depth + depth)
        tiles = [ordered[some, k * width : k * width + width] if k < packs else blank for k in range(n_row)]
        tiles = swap_bits(tiles, [(bit, NB * bit) for bit in powers(n_row)])
        for row in range(n_row):
            send_ref[row * n_col + column] = tiles[row]

    def exchange(source_of, target_ref, sends, recvs):
        def copy(other):
            return pltpu.make_async_remote_copy(
                src_ref=source_of(other), dst_ref=target_ref.at[me], send_sem=sends.at[other], recv_sem=recvs.at[me],
                device_id=(other // n_col, lax.rem(other, n_col)), device_id_type=MESH)

        def begin():
            def one(k, carry):
                copy(peer(k)).start()
                return carry

            lax.fori_loop(1, n_sub, one, 0)

        def finish(first, last):
            def one(other, carry):
                @pl.when(other != me)
                def _():
                    pltpu.make_async_remote_copy(
                        src_ref=source_of(other), dst_ref=target_ref.at[other], send_sem=sends.at[other],
                        recv_sem=recvs.at[other], device_id=(other // n_col, lax.rem(other, n_col)),
                        device_id_type=MESH).wait_recv()

                return carry

            lax.fori_loop(first, last, one, 0)

        def drain():
            def one(k, carry):
                copy(peer(k)).wait_send()
                return carry

            lax.fori_loop(1, n_sub, one, 0)

        return begin, finish, drain

    offsets = slot_offsets()
    quads = n_sub // n_row
    lanes = lax.broadcasted_iota(jnp.int32, (depth, width), 1) % n_sub
    ends, reach = 2 * PSUB, 2 * n_col

    def banded(values):
        bands = {}
        for (start, stop), value in zip(offsets, values):
            shift = start[0] * n_col + start[1]
            if shift:
                value = pltpu.roll(value, shift % width, 1)
            step = (stop[0] - start[0]) * n_col + stop[1] - start[1]
            bands[step] = bands[step] + value if step in bands else value
        return bands

    def place(bands, b):
        value = jnp.zeros((depth, width), jnp.float32)
        for step, band in bands.items():
            if 0 <= b - step < n_sub:
                value = jnp.where(lanes == b - step, band, value)
        return value

    begin, finish, drain = exchange(lambda other: send_ref.at[other], here_ref, send_sem, recv_sem)
    begin2, finish2, drain2 = exchange(lambda other: mine_ref, all_ref, send_sem2, recv_sem2)
    low_bits = [(bit, NB * bit) for bit in powers(n_row)]
    here_ref[me] = send_ref[me]
    begin()

    finish(0, n_row)
    tiles = swap_bits([here_ref[s] for s in range(n_row)], low_bits)
    packs = -(-SLOTS // quads)
    stack = jnp.concatenate(tiles[:packs], axis=0)
    shape = (width, quads * width)
    lane = lax.broadcasted_iota(jnp.int32, shape, 0)
    goal = lax.broadcasted_iota(jnp.int32, shape, 1)
    sub, tru = goal % n_sub, goal % width // n_sub
    origin = goal // width * vectors + (tru // NB * n_row + sub) * NB + tru % NB
    stack = exact_dot(stack, ((origin == lane) & (sub < n_row)).astype(jnp.float32))
    values = []
    for slot in range(SLOTS):
        k, quad = divmod(slot, quads)
        values.append(stack[k * depth : k * depth + depth, quad * width : quad * width + width])
    bands = banded(values)
    packed = jnp.zeros((depth, width), jnp.float32)
    for b in range(ends):
        value = jnp.where(lanes < reach, place(bands, b), 0.0)
        packed = packed + (pltpu.roll(value, reach * b, 1) if b else value)
    mine_ref[...] = packed
    all_ref[me] = packed
    begin2()

    finish(n_row, n_sub)
    bits = low_bits + [(n_row * bit, vectors * bit) for bit in powers(quads)]
    tiles = swap_bits([here_ref[s] for s in range(n_sub)], bits)
    stack = jnp.concatenate([tiles[slot % quads * n_row + slot // quads] for slot in range(SLOTS)], axis=0)
    into = lax.broadcasted_iota(jnp.int32, (width, width), 1)
    sub, tru = into % n_sub, into // n_sub
    origin = sub // n_row * vectors + (tru // NB * n_row + sub % n_row) * NB + tru % NB
    order = (origin == lax.broadcasted_iota(jnp.int32, (width, width), 0)).astype(jnp.float32)
    stack = exact_dot(stack, order)
    bands = banded([stack[slot * depth : slot * depth + depth] for slot in range(SLOTS)])
    for b in range(ends, n_sub):
        out_ref[b] = place(bands, b)
    finish2(0, n_sub)

    def settle():
        drain()
        drain2()

    return settle


def panels(n_row, n_col, local_ref, all_ref, out_ref, low_ref):
    n_sub, depth, width = local_ref.shape
    vectors = depth * n_col
    ends, reach = 2 * PSUB, 2 * n_col
    f32 = jnp.float32
    r = lax.axis_index("row")
    c = lax.axis_index("col")
    order = ends * vectors
    at = lax.broadcasted_iota(jnp.int32, (vectors, vectors), 1)
    col_blocks = depth // NB
    source = (at // NB % col_blocks * n_col + at // (NB * col_blocks)) * NB + at % NB
    turn = (source == lax.broadcasted_iota(jnp.int32, (vectors, vectors), 0)).astype(f32)
    high = reach // ends
    by_column = []
    for column in range(n_col):
        tiles = [all_ref[row * n_col + column] for row in range(n_row)]
        bits = [(bit, ends * bit) for bit in powers(n_row)]
        by_column.append(swap_bits(tiles, bits))
    halves = []
    for h in range(high):
        parts = []
        for b in range(ends):
            parts.append(exact_dot(turn, jnp.concatenate([by_column[column][b * high + h] for column in range(n_col)], axis=0)))
        halves.append(jnp.concatenate(parts, axis=0))
    tall = 8
    count = order // tall
    work = [[halves[h][t * tall : t * tall + tall] for t in range(count)] for h in range(high)]
    def spread(value, s):
        return jnp.broadcast_to(value[s : s + 1], (tall, width))

    def spot(k):
        b, q = divmod(k, vectors)
        tr, row, u = q // (NB * n_row), q // NB % n_row, q % NB
        return (tr * NB + u) * n_sub + row * ends + b

    def column(i, k):
        at = spot(k)
        return jnp.broadcast_to(work[0][i][:, at : at + 1], (tall, width)) * ones

    ones = jnp.where(all_ref[0] == all_ref[0], 1.0, 0.0)
    ones = jnp.concatenate([ones] * (tall // depth), axis=0)

    few = 4
    for first in range(0, order, few):
        t, base = divmod(first, tall)
        columns = [column(t, first + s) for s in range(few)]
        rows = [[spread(work[h][t], base + s) for h in range(high)] for s in range(few)]
        scaled, weights = [], {}
        for s in range(few):
            pivot = spread(columns[s], base + s)
            inverse = 1.0 / pivot
            root = lax.rsqrt(pivot)
            k = first + s
            for h in range(high):
                low_ref[k : k + 1, h * width : h * width + width] = (rows[s][h] * root)[:1]
            scaled.append([x * inverse for x in rows[s]])
            for s2 in range(s + 1, few):
                weight = spread(columns[s], base + s2) * inverse
                weights[s, s2] = weight
                rows[s2] = [y - weight * x for x, y in zip(rows[s], rows[s2])]
                columns[s2] = columns[s2] - weight * columns[s]
        done = base + few == tall
        for i in range(t + done, count):
            if i > t:
                columns = [column(i, first + s) for s in range(few)]
                for s in range(few):
                    for s2 in range(s + 1, few):
                        columns[s2] = columns[s2] - weights[s, s2] * columns[s]
            for h in range(high):
                total = columns[0] * scaled[0][h]
                for s in range(1, few):
                    total = total + columns[s] * scaled[s][h]
                work[h][i] = work[h][i] - total
    shape = (order, high * width)
    lane = lax.broadcasted_iota(jnp.int32, shape, 1)
    inner = lane % width
    a = lane // width * ends + inner % ends
    p = (inner // (NB * n_sub) * n_row + inner % n_sub // ends) * NB + inner // n_sub % NB
    keep = a * vectors + p >= lax.broadcasted_iota(jnp.int32, shape, 0)
    low = jnp.where(keep, low_ref[...], 0.0)

    shape = (high * width, width)
    lane = lax.broadcasted_iota(jnp.int32, shape, 0)
    goal = lax.broadcasted_iota(jnp.int32, shape, 1)
    inner = lane % width
    a = lane // width * ends + inner % ends
    mine = (inner % n_sub // ends == r) & (inner // n_sub == goal // n_sub) & (a == goal % n_sub)
    rows_mine = exact_dot(low, mine.astype(f32))
    shape = (ends * depth, order)
    goal = lax.broadcasted_iota(jnp.int32, shape, 0)
    lane = lax.broadcasted_iota(jnp.int32, shape, 1)
    b, inner = goal // depth, goal % depth
    q = (inner // NB * n_col + c) * NB + inner % NB
    pick = (lane == b * vectors + q).astype(f32)
    panel = exact_dot(pick, rows_mine)
    for b in range(ends):
        out_ref[b] = panel[b * depth : b * depth + depth]
    lanes = lax.broadcasted_iota(jnp.int32, (depth, width), 1) % n_sub
    for h in range(1, high):
        shape = (ends * depth, width)
        goal = lax.broadcasted_iota(jnp.int32, shape, 0)
        lane = lax.broadcasted_iota(jnp.int32, shape, 1)
        b, inner = goal // depth, goal % depth
        q = (inner // NB * n_col + c) * NB + inner % NB
        place = (q // (NB * n_row) * NB + q % NB) * n_sub + q // NB % n_row * ends + b
        pick = (lane == place).astype(f32)
        chosen = exact_dot(pick, low[:, h * width : h * width + width], (((1,), (1,)), ((), ())))
        change = exact_dot(chosen, rows_mine)
        for b in range(ends):
            value = local_ref[h * ends + b] - change[b * depth : b * depth + depth]
            out_ref[h * ends + b] = jnp.where(lanes < ends, 0.0, value)
    for b in range(reach, n_sub):
        out_ref[b] = jnp.where(lanes < ends, 0.0, local_ref[b])


ROWS = 8
SPOTS = 4
CHUNK = 4
MINOR = (((1,), (1,)), ((), ()))


def cross_weights(n_y):
    shape = (2 * n_y, 2 * n_y)
    i = lax.broadcasted_iota(jnp.int32, shape, 0)
    j = lax.broadcasted_iota(jnp.int32, shape, 1)
    gap = i % n_y - j % n_y
    same = i // n_y == j // n_y
    near = jnp.where((gap == 1) | (gap == -1), 1.0, jnp.where(gap == 0, -6.0, 0.0))
    return jnp.where(same, near, jnp.where(gap == 0, 1.0, 0.0)).astype(jnp.bfloat16)


def stencil(p, fresh, own_ref, cross_ref, mixed_ref, first_ref, now_ref, old_ref, part_ref, rows_ref, root_ref, side_ref,
            lines_ref):
    vectors, n_x, n_y = side_ref.shape
    blocks = n_x // ROWS
    inner = slice(ROWS, ROWS + n_x)
    up, down = slice(ROWS + 1, ROWS + 1 + n_x), slice(ROWS - 1, ROWS - 1 + n_x)
    if fresh:
        both = jnp.concatenate([own_ref[:, s].reshape(vectors * n_x, n_y) for s in range(2)], axis=1)
        mixed_ref[...] = lax.dot_general(both, cross_ref[...], PLAIN, preferred_element_type=jnp.float32)
        lanes = lax.broadcasted_iota(jnp.int32, (n_x, n_y), 1)
        z = 2 * p
        kept = [(lanes < SPOTS * (z + s + 1)) & (lanes >= SPOTS * (z + s)) for s in range(2)]
    for m in range(vectors // 2):
        mids, fluxes = [[], []], [[], []]
        for v in (2 * m, 2 * m + 1):
            last = old_ref[v, inner]
            total = part_ref[v]
            mids[0].append(last)
            if fresh:
                own = own_ref[v, 0].astype(jnp.float32)
                first_ref[v, inner] = own
                next_own = own_ref[v, 1].astype(jnp.float32)
                now_ref[v, inner] = next_own
                total = total + own
                mixed = mixed_ref[v * n_x : v * n_x + n_x]
                near = mixed[:, :n_y] + (first_ref[v, up] + first_ref[v, down]) + last
                part_ref[v] = mixed[:, n_y:] + (now_ref[v, up] + now_ref[v, down])
                flux = near * root_ref[1]
                for s, value in enumerate((own, next_own)):
                    lines_ref[s, 0, v : v + 1] = value[:1]
                    lines_ref[s, 1, v : v + 1] = value[n_x - 1 :]
                for s in range(2):
                    turned = pltpu.roll(own_ref[v, s], lax.rem(SPOTS * (z + s) + 2, n_y), 1)
                    side_ref[v] = jnp.where(kept[s], turned, side_ref[v])
                lines_ref[3, 0, v : v + 1] = flux[:1]
                lines_ref[3, 1, v : v + 1] = flux[n_x - 1 :]
                mids[1].append(own)
                fluxes[1].append(flux)
            flux = total * root_ref[0]
            lines_ref[2, 0, v : v + 1] = flux[:1]
            lines_ref[2, 1, v : v + 1] = flux[n_x - 1 :]
            fluxes[0].append(flux)
        where = slice(2 * m * ROWS, 2 * m * ROWS + 2 * ROWS)
        for b in range(blocks):
            part = slice(b * ROWS, b * ROWS + ROWS)
            for s in range(2 if fresh else 1):
                for which, values in enumerate((mids[s], fluxes[s])):
                    rows_ref[s, b, where, which * n_y : which * n_y + n_y] = jnp.concatenate(
                        [value[part] for value in values], axis=0).astype(jnp.bfloat16)


def gram(acc_ref, rows_ref, slices):
    both = jnp.concatenate([rows_ref[s, b] for s in slices for b in range(rows_ref.shape[1])], axis=1)
    acc_ref[...] += lax.dot_general(both, both, MINOR, preferred_element_type=jnp.float32)


def roots(p, mob_ref, lab_ref, root_ref, rootx_ref, rooty_ref):
    _, n_x, n_y = root_ref.shape
    lanes = lax.broadcasted_iota(jnp.int32, (n_x, n_y), 1)
    for s in range(2):
        z = 2 * p + s
        value = jnp.zeros((n_x, n_y), jnp.float32)
        for phase in range(mob_ref.shape[0]):
            value = value + jnp.where(lab_ref[s] == phase, mob_ref[phase], jnp.float32(0.0))
        root = jnp.sqrt(value)
        root_ref[1 + s] = jnp.where((lanes == 0) | (lanes == n_y - 1), 0.0, root)
        rootx_ref[z, 0:1] = root[:1]
        rootx_ref[z, 1:2] = root[n_x - 1 :]
        ok = (lanes < SPOTS * z + SPOTS) & (lanes >= SPOTS * z)
        rooty_ref[...] = jnp.where(ok, pltpu.roll(root, lax.rem(SPOTS * z + 2, n_y), 1), rooty_ref[...])


def pack_columns(side_ref, pack_ref):
    vectors, n_x, n_y = side_ref.shape
    quarter = n_x // SPOTS
    spot = lax.broadcasted_iota(jnp.int32, (quarter, n_y), 1) % SPOTS

    def some(m, carry):
        for v in range(4):
            v = 4 * m + v
            for to, column in enumerate((1, 2)):
                total = jnp.zeros((quarter, n_y), jnp.float32)
                for k in range(SPOTS):
                    part = side_ref[v, k * quarter : k * quarter + quarter].astype(jnp.float32)
                    part = pltpu.roll(part, (k - column) % n_y, 1) if k != column else part
                    total = jnp.where(spot == k, part, total)
                pack_ref[to, v] = total.astype(jnp.bfloat16)
        return carry

    lax.fori_loop(0, vectors // 4, some, 0)


def x_tiles(tiles_ref, frims_ref, xhalo_ref, rootx_ref, faces_ref, ends_ref):
    _, n_z, vectors, n_y = frims_ref.shape
    thin = lax.broadcasted_iota(jnp.int32, (vectors, n_y), 1)
    for side in range(2):
        total = jnp.zeros((vectors, n_y), jnp.float32)
        for z in range(n_z):
            over = xhalo_ref[side, z].astype(jnp.float32) * rootx_ref[z, side : side + 1]
            at = slice(z * n_y, z * n_y + n_y)
            faces_ref[side, :vectors, at] = frims_ref[side, z]
            faces_ref[side, vectors:, at] = over.astype(jnp.bfloat16)
            ok = (thin >= SPOTS * z) & (thin < SPOTS * z + SPOTS)
            total = jnp.where(ok, pltpu.roll(over, (SPOTS * z + 2) % n_y, 1), total)
        ends_ref[side] = total.astype(jnp.bfloat16)
        gram = lax.dot_general(faces_ref[side], faces_ref[side], MINOR, preferred_element_type=jnp.float32)
        at = (1 + 3 * side) * vectors
        tiles_ref[:, at : at + vectors] = gram[vectors:, :vectors]
        tiles_ref[:, at + vectors : at + 2 * vectors] = gram[:vectors, vectors:]
        tiles_ref[:, at + 2 * vectors : at + 3 * vectors] = gram[vectors:, vectors:]


def fold(squares, vectors):
    order = squares[0].shape[0]
    line = lax.broadcasted_iota(jnp.int32, (order, order), 0)
    column = lax.broadcasted_iota(jnp.int32, (order, order), 1)
    same = line % ROWS == column % ROWS
    pick = (lax.broadcasted_iota(jnp.int32, (order, vectors), 0) // ROWS
            == lax.broadcasted_iota(jnp.int32, (order, vectors), 1)).astype(jnp.float32)
    thick = [jnp.where(same, square, 0.0).reshape(vectors, ROWS, order).sum(1) for square in squares]
    thin = exact_dot(jnp.concatenate(thick, axis=0), pick)
    return [thin[i * vectors : (i + 1) * vectors] for i in range(len(squares))]


def y_tiles(tiles_ref, acc_ref, side_ref, rooty_ref, yhalo_ref, ends_ref, left_ref, right_ref, cut_ref):
    vectors, n_x, n_y = side_ref.shape
    order = vectors * ROWS
    blocks = n_x // ROWS
    f32, bf16 = jnp.float32, jnp.bfloat16
    rows = lax.broadcasted_iota(jnp.int32, (n_x, n_y), 0)
    lanes = lax.broadcasted_iota(jnp.int32, (n_x, n_y), 1)
    spot = lanes % SPOTS
    root = jnp.where((spot == 1) | (spot == 2), rooty_ref[...], 0.0)

    def spread(packed, column):
        return jnp.concatenate(
            [pltpu.roll(packed, (column - k) % n_y, 1) if k != column else packed for k in range(SPOTS)], axis=0)

    def pair_of(m, carry):
        kept = []
        for i in range(2):
            v = 2 * m + i
            own = side_ref[v].astype(f32)
            near = jnp.where(lanes < SPOTS, 0.0, pltpu.roll(own, SPOTS, 1))
            near = near + jnp.where(lanes >= n_y - SPOTS, 0.0, pltpu.roll(own, n_y - SPOTS, 1))
            near = near + jnp.where(rows == 0, 0.0, pltpu.roll(own, 1, 0))
            near = near + jnp.where(rows == n_x - 1, 0.0, pltpu.roll(own, n_x - 1, 0))
            near = near + jnp.where(spot == 2, pltpu.roll(own, n_y - 1, 1), pltpu.roll(own, 1, 1))
            flux = (near - 6.0 * own) * root
            low = spread(yhalo_ref[0, v].astype(f32), 2)
            upp = spread(yhalo_ref[1, v].astype(f32), 1)
            over = jnp.where(spot == 2, low, upp) * root
            cut_ref[0, pl.ds(v, 1)] = over[:1]
            cut_ref[1, pl.ds(v, 1)] = over[n_x - 1 :]
            cut_ref[2, pl.ds(v, 1)] = flux[:1]
            cut_ref[3, pl.ds(v, 1)] = flux[n_x - 1 :]
            kept.append((flux, over, jnp.where(spot == 2, over, 0.0), jnp.where(spot == 1, over, 0.0)))
        for b in range(blocks):
            part = slice(b * ROWS, b * ROWS + ROWS)
            both = [jnp.concatenate([x[part], y[part]], axis=0).astype(bf16) for x, y in zip(*kept)]
            at = slice(b * n_y, b * n_y + n_y)
            first = pl.ds(pl.multiple_of(m * 2 * ROWS, 2 * ROWS), 2 * ROWS)
            second = pl.ds(pl.multiple_of(order + m * 2 * ROWS, 2 * ROWS), 2 * ROWS)
            left_ref[first, at] = both[0]
            left_ref[second, at] = both[1]
            right_ref[first, at] = both[2]
            right_ref[second, at] = both[3]
        return carry

    lax.fori_loop(0, vectors // 2, pair_of, 0)
    crossed = lax.dot_general(left_ref[...], right_ref[...], MINOR, preferred_element_type=f32)
    edges = left_ref[:order]
    edges = lax.dot_general(edges, edges, MINOR, preferred_element_type=f32)

    def put(slot, value):
        tiles_ref[:, slot * vectors : (slot + 1) * vectors] = value

    squares = [acc_ref[...] + edges]
    for side in range(2):
        here = slice(side * order, side * order + order)
        squares += [crossed[:order, here], crossed[order:, here]]
    folded = fold(squares, vectors)
    put(0, folded[0])
    for side in range(2):
        flux = cut_ref[2 + side].astype(bf16)
        for slot, left, right in ((1 + 3 * side, ends_ref[side], flux), (2 + 3 * side, flux, ends_ref[side])):
            here = slice(slot * vectors, (slot + 1) * vectors)
            tiles_ref[:, here] = tiles_ref[:, here] + lax.dot_general(left, right, MINOR, preferred_element_type=f32)
        cross = folded[1 + 2 * side]
        put(7 + 3 * side, cross.T)
        put(8 + 3 * side, cross)
        put(9 + 3 * side, folded[2 + 2 * side])
    thin = lax.broadcasted_iota(jnp.int32, (vectors, n_y), 1)
    slot = 13
    for x in range(2):
        for y in range(2):
            along = jnp.where(thin % SPOTS == 2 - y, cut_ref[x], 0.0).astype(bf16)
            put(slot, lax.dot_general(along, ends_ref[x], MINOR, preferred_element_type=f32))
            put(slot + 1, lax.dot_general(ends_ref[x], along, MINOR, preferred_element_type=f32))
            slot += 2


def main_kernel(n_row, n_col, mob_ref, own_ref, lab_ref, out_ref,
                cross_ref, mixed_ref, first_ref, plain0_ref, plain1_ref, part_ref, rows0_ref, rows1_ref, root_ref, lines_ref, acc_ref, rims_ref, frims_ref, side_ref,
                rootx_ref, rooty_ref, xhalo_ref, pack_ref, yhalo_ref, faces_ref, ends_ref, left_ref, right_ref, cut_ref,
                tiles_ref, message_ref, here_ref, mine_ref, panel_ref, local_ref, low_ref,
                xsend_sem, xrecv_sem, ysend_sem, yrecv_sem, send_sem, recv_sem, send_sem2, recv_sem2):
    p = pl.program_id(0)
    n_z = rims_ref.shape[1]
    pairs = n_z // 2
    vectors = side_ref.shape[0]
    n_sub = n_row * n_col
    r = lax.axis_index("row")
    c = lax.axis_index("col")
    me = r * n_col + c
    barrier = pltpu.get_barrier_semaphore()

    def peer(k):
        other = lax.rem(me + k, n_sub)
        return other, (other // n_col, lax.rem(other, n_col))

    def rim_copy(side, some):
        return pltpu.make_async_remote_copy(
            src_ref=rims_ref.at[side, some], dst_ref=xhalo_ref.at[1 - side, some],
            send_sem=xsend_sem.at[side], recv_sem=xrecv_sem.at[1 - side],
            device_id=(lax.rem(r + 2 * side - 1 + n_row, n_row), c), device_id_type=MESH)

    def column_copy(way):
        return pltpu.make_async_remote_copy(
            src_ref=pack_ref.at[way], dst_ref=yhalo_ref.at[way],
            send_sem=ysend_sem.at[way], recv_sem=yrecv_sem.at[way],
            device_id=(r, lax.rem(c + 1 - 2 * way + n_col, n_col)), device_id_type=MESH)

    x_there = (r > 0, r < n_row - 1)
    y_there = (c > 0, c < n_col - 1)

    @pl.when(p == 0)
    def _():
        def greet(k, carry):
            pl.semaphore_signal(barrier, inc=1, device_id=peer(k)[1], device_id_type=MESH)
            return carry

        lax.fori_loop(1, n_sub, greet, 0)
        cross_ref[...] = cross_weights(side_ref.shape[2])
        for ref in (plain1_ref, part_ref, rows1_ref, root_ref, acc_ref, side_ref, rooty_ref):
            ref[...] = jnp.zeros_like(ref)
        rim = jnp.zeros((vectors, ROWS, side_ref.shape[2]), jnp.float32)
        for ref in (first_ref, plain0_ref):
            ref[:, :ROWS] = rim
            ref[:, ROWS + side_ref.shape[1] :] = rim
        tiles_ref[:, SLOTS * vectors :] = jnp.zeros((vectors, tiles_ref.shape[1] - SLOTS * vectors), jnp.float32)
        for side in range(2):
            @pl.when(jnp.logical_not(x_there[side]))
            def _():
                xhalo_ref[side] = jnp.zeros(xhalo_ref.shape[1:], jnp.bfloat16)

            @pl.when(jnp.logical_not(y_there[side]))
            def _():
                yhalo_ref[side] = jnp.zeros(yhalo_ref.shape[1:], jnp.bfloat16)

    @pl.when(2 * p == CHUNK)
    def _():
        pl.semaphore_wait(barrier, n_sub - 1)

    @pl.when((lax.rem(2 * p, CHUNK) == 0) & (p > 0))
    def _():
        for side in range(2):
            @pl.when(x_there[side])
            def _():
                rim_copy(side, pl.ds(2 * p - CHUNK, CHUNK)).start()

    plains, rows = (plain0_ref, plain1_ref), (rows0_ref, rows1_ref)

    def rims(fresh):
        if fresh:
            for side in range(2):
                for s in range(2):
                    rims_ref[side, 2 * p + s] = lines_ref[s, side].astype(jnp.bfloat16)
                frims_ref[side, 2 * p] = lines_ref[3, side].astype(jnp.bfloat16)
        for side in range(2):
            frims_ref[side, jnp.maximum(2 * p - 1, 1)] = lines_ref[2, side].astype(jnp.bfloat16)

    for odd in range(2):
        @pl.when((p < pairs) & (lax.rem(p, 2) == odd))
        def _():
            roots(p, mob_ref, lab_ref, root_ref, rootx_ref, rooty_ref)
            gram(acc_ref, rows[1 - odd], (0, 1))
            stencil(p, True, own_ref, cross_ref, mixed_ref, first_ref, plains[odd], plains[1 - odd], part_ref,
                    rows[odd], root_ref, side_ref, lines_ref)
            root_ref[0] = root_ref[2]
            rims(True)

    @pl.when(p == pairs)
    def _():
        pack_columns(side_ref, pack_ref)
        for way in range(2):
            @pl.when(y_there[1 - way])
            def _():
                column_copy(way).start()
        odd = pairs % 2
        stencil(p, False, own_ref, cross_ref, mixed_ref, first_ref, plains[odd], plains[1 - odd], part_ref, rows[odd],
                root_ref, side_ref, lines_ref)
        rims(False)
        gram(acc_ref, rows[1 - odd], (0, 1))
        gram(acc_ref, rows[odd], (0,))
        everything = pl.ds(0, n_z)
        for side in range(2):
            @pl.when(x_there[side])
            def _():
                rim_copy(1 - side, everything).wait_recv()
        x_tiles(tiles_ref, frims_ref, xhalo_ref, rootx_ref, faces_ref, ends_ref)
        for way in range(2):
            @pl.when(y_there[way])
            def _():
                column_copy(way).wait_recv()
        y_tiles(tiles_ref, acc_ref, side_ref, rooty_ref, yhalo_ref, ends_ref, left_ref, right_ref, cut_ref)
        settle = trade(n_row, n_col, tiles_ref, local_ref, panel_ref, message_ref, mine_ref, here_ref,
              send_sem, recv_sem, send_sem2, recv_sem2)
        panels(n_row, n_col, local_ref, panel_ref, out_ref, low_ref)
        settle()
        for side in range(2):
            @pl.when(x_there[side])
            def _():
                rim_copy(side, everything).wait_send()
        for way in range(2):
            @pl.when(y_there[1 - way])
            def _():
                column_copy(way).wait_send()


def main_call(own, labels, mobility, n_row, n_col):
    vectors, n_z, n_x, n_y = own.shape
    n_sub = n_row * n_col
    depth = vectors // n_col
    width = vectors // n_row * n_sub
    order = vectors * ROWS
    blocks = n_x // ROWS
    f32, bf16 = jnp.float32, jnp.bfloat16
    last = n_z // 2 - 1
    return pl.pallas_call(
        functools.partial(main_kernel, n_row, n_col),
        grid=(n_z // 2 + 1,),
        in_specs=[
            pl.BlockSpec(memory_space=pltpu.SMEM),
            pl.BlockSpec((vectors, 2, n_x, n_y), lambda p: (0, jnp.minimum(p, last), 0, 0)),
            pl.BlockSpec((2, n_x, n_y), lambda p: (jnp.minimum(p, last), 0, 0)),
        ],
        out_specs=pl.BlockSpec((n_sub, depth, width), lambda p: (0, 0, 0)),
        out_shape=jax.ShapeDtypeStruct((n_sub, depth, width), f32),
        scratch_shapes=[
            pltpu.VMEM((2 * n_y, 2 * n_y), bf16),
            pltpu.VMEM((vectors * n_x, 2 * n_y), f32),
            pltpu.VMEM((vectors, n_x + 2 * ROWS, n_y), f32),
            pltpu.VMEM((vectors, n_x + 2 * ROWS, n_y), f32),
            pltpu.VMEM((vectors, n_x + 2 * ROWS, n_y), f32),
            pltpu.VMEM((vectors, n_x, n_y), f32),
            pltpu.VMEM((2, blocks, order, 2 * n_y), bf16),
            pltpu.VMEM((2, blocks, order, 2 * n_y), bf16),
            pltpu.VMEM((3, n_x, n_y), f32),
            pltpu.VMEM((4, 2, vectors, n_y), f32),
            pltpu.VMEM((order, order), f32),
            pltpu.VMEM((2, n_z, vectors, n_y), bf16),
            pltpu.VMEM((2, n_z, vectors, n_y), bf16),
            pltpu.VMEM((vectors, n_x, n_y), bf16),
            pltpu.VMEM((n_z, 2, n_y), f32),
            pltpu.VMEM((n_x, n_y), f32),
            pltpu.VMEM((2, n_z, vectors, n_y), bf16),
            pltpu.VMEM((2, vectors, n_x // SPOTS, n_y), bf16),
            pltpu.VMEM((2, vectors, n_x // SPOTS, n_y), bf16),
            pltpu.VMEM((2, 2 * vectors, n_z * n_y), bf16),
            pltpu.VMEM((2, vectors, n_y), bf16),
            pltpu.VMEM((2 * order, blocks * n_y), bf16),
            pltpu.VMEM((2 * order, blocks * n_y), bf16),
            pltpu.VMEM((4, vectors, n_y), f32),
            pltpu.VMEM((vectors, -(-SLOTS // n_col) * n_col * vectors), f32),
            pltpu.VMEM((n_sub, depth, width), f32),
            pltpu.VMEM((n_sub, depth, width), f32),
            pltpu.VMEM((depth, width), f32),
            pltpu.VMEM((n_sub, depth, width), f32),
            pltpu.VMEM((n_sub, depth, width), f32),
            pltpu.VMEM((2 * PSUB * vectors, 2 * n_col // (2 * PSUB) * width), f32),
            pltpu.SemaphoreType.DMA((2,)),
            pltpu.SemaphoreType.DMA((2,)),
            pltpu.SemaphoreType.DMA((2,)),
            pltpu.SemaphoreType.DMA((2,)),
            pltpu.SemaphoreType.DMA((n_sub,)),
            pltpu.SemaphoreType.DMA((n_sub,)),
            pltpu.SemaphoreType.DMA((n_sub,)),
            pltpu.SemaphoreType.DMA((n_sub,)),
        ],
        compiler_params=pltpu.CompilerParams(
            collective_id=0, has_side_effects=True, vmem_limit_bytes=48 * 1024 * 1024),
    )(pltpu.with_memory_space_constraint(mobility, pltpu.HBM), own, pltpu.with_memory_space_constraint(labels, pltpu.HBM))


def body(own, labels, mobility):
    n_row = lax.axis_size("row")
    n_col = lax.axis_size("col")
    n_sub = n_row * n_col
    vectors = own.shape[0]
    local = main_call(own, labels, mobility, n_row, n_col)
    return local.reshape(
        n_sub, vectors // (NB * n_col), 1, NB, vectors // (NB * n_row), 1, NB, n_sub
    )


def solution(mesh):
    return jax.shard_map(
        body,
        mesh=mesh,
        in_specs=(P(None, None, "row", "col"), P(None, "row", "col"), P()),
        out_specs=P(None, None, "col", None, None, "row", None, None),
        check_vma=False,
    )
```
